512 devices in a mesh: rep: 4 (over x), tm: 16 (over z), height: 8 (over y, core).
Axes of the slice: x: 4, y: 4, z: 16, core: 2. Of those that a mesh axis runs over, the one named last changes fastest.
Arguments:
- inputs: bfloat16 [4, 64, 128, 32, 128], P('rep', 'tm', 'height'), may hold values from -32 to 32
- spatial_kernel: bfloat16 [3, 3, 128, 128], replicated, may hold values from -0.1875 to 0.1875
- temporal_kernel: bfloat16 [3, 128, 128], replicated, may hold values from -0.3125 to 0.3125
- norm_gain: float32 [128], replicated, may hold values from 0.1 to 1.9
- norm_shift: float32 [128], replicated, may hold values from -3 to 3
- cotangent: bfloat16 [4, 64, 128, 32, 128], P('rep', 'tm', 'height'), may hold values from -6 to 6
Outputs:
- outputs: bfloat16 [4, 64, 128, 32, 128], P('rep', 'tm', 'height')
- grad_inputs: bfloat16 [4, 64, 128, 32, 128], P('rep', 'tm', 'height')
- grad_spatial: float32 [3, 3, 128, 128], replicated
- grad_temporal: float32 [3, 128, 128], replicated
- grad_gain: float32 [128], replicated
- grad_shift: float32 [128], replicated
The draws below stay inside these ranges and needn't reach their ends.
All inputs are finite; a program needn't handle non-finite values.
Results may differ from the reference program's by a relative error of at most 0.0041.
The reference program's roundings to bfloat16 on the way (of `feature`, `grad_mixed` and `grad_feature`) count: a program that leaves them out, or rounds other values in their place, can miss the bound.
Values may be sent and summed in bfloat16 or wider, within the bound.
No kernel may reach another device: no remote copies, remote signals or barrier semaphores. Data moves between devices by JAX's collectives and lax.ppermute only.
A program may use at most 64 MiB of HBM per device.

```python
import math
import jax
import jax.numpy as jnp
from jax import lax

C = 128
GROUPS = 32
WIDTH = 32
CLIPS = 4
FRAMES = 64
ROWS = 128
PIXELS = 1048576


def draw_inputs(key, part):
    keys = jax.random.split(jax.random.fold_in(key, 7), 3)
    shape = (CLIPS, FRAMES, ROWS, WIDTH, C)
    base = jnp.clip(jax.random.normal(keys[0], shape, jnp.float32), -3.0, 3.0)
    pixel_scale = jnp.exp(jax.random.uniform(keys[1], (CLIPS, FRAMES, ROWS, WIDTH, 1), jnp.float32, -1.15, 1.15))
    channel_scale = jnp.exp(jax.random.uniform(keys[2], (C,), jnp.float32, -0.8, 0.8))
    frame_pos = jnp.arange(FRAMES).astype(jnp.float32) / max(FRAMES - 1, 1)
    row_pos = jnp.arange(ROWS).astype(jnp.float32) / max(ROWS - 1, 1)
    frame_scale = jnp.exp(1.1 * (frame_pos - 0.5))
    row_scale = jnp.exp(1.1 * (row_pos - 0.5))
    values = 0.5 * base * pixel_scale * channel_scale
    values = values * frame_scale[:, None, None, None] * row_scale[:, None, None]
    return values.astype(jnp.bfloat16)


def levels(rng, extent, pieces, least, high):
    def one(axis_at, shards_of):
        draws = jax.random.uniform(jax.random.fold_in(jax.random.fold_in(rng, 6), axis_at), (shards_of,), jnp.float32, least / len(pieces), high / len(pieces))
        return jnp.repeat(jnp.exp(draws), extent[axis_at] // shards_of).reshape((-1,) + (1,) * (len(extent) - axis_at - 1))

    level = one(*pieces[0])
    for cut in pieces[1:]:
        level = level * one(*cut)
    return level


def centred(rng, dims, spread, reach, cuts=(), dtype=jnp.bfloat16):
    level = levels(rng, dims, cuts, -0.22, 0.18) if cuts else 1.0
    values = jax.random.normal(rng, dims, jnp.float32) * spread * level
    return jnp.minimum(jnp.maximum(values, -reach), reach).astype(dtype)


def setup_inputs(seed: int = 0) -> dict:
    key_list = jax.random.split(jax.random.key(seed), 7)
    inputs = draw_inputs(jax.random.fold_in(key_list[6], 71), 0)
    spatial_kernel = centred(key_list[1], (3, 3, C, C), (9 * C) ** -0.5, 0.1875)
    temporal_kernel = centred(key_list[2], (3, C, C), (3 * C) ** -0.5, 0.3125)
    norm_gain = jnp.clip(1.0 + 0.18 * jax.random.normal(key_list[3], (C,), jnp.float32), 0.1, 1.9)
    norm_shift = centred(key_list[4], (C,), 0.5, 3.0, (), jnp.float32)
    cotangent = centred(key_list[5], (CLIPS, FRAMES, ROWS, WIDTH, C), 1.0, 6.0, ((0, 4), (1, 16), (2, 8)))
    return dict(inputs=inputs, spatial_kernel=spatial_kernel, temporal_kernel=temporal_kernel, norm_gain=norm_gain, norm_shift=norm_shift, cotangent=cotangent)


EPS = 1e-05

def one_clip(pair, spatial_kernel, temporal_kernel, norm_gain, norm_shift):
    inputs, cotangent = pair
    frames, rows, columns, channels = inputs.shape
    group_size = channels // GROUPS
    padded = jnp.pad(inputs.astype(jnp.float32), ((0, 0), (1, 1), (1, 1), (0, 0)))
    spatial = spatial_kernel.astype(jnp.float32)
    temporal = temporal_kernel.astype(jnp.float32)
    total = jnp.zeros((frames, rows, columns, channels), jnp.float32)
    for row_tap in range(3):
        for col_tap in range(3):
            window = padded[:, row_tap:row_tap + rows, col_tap:col_tap + columns]
            total = total + jnp.einsum('frwc,cd->frwd', window, spatial[row_tap, col_tap])
    feature = total.astype(jnp.bfloat16)
    earlier = jnp.pad(feature.astype(jnp.float32), ((2, 0), (0, 0), (0, 0), (0, 0)))
    mixed = jnp.zeros((frames, rows, columns, channels), jnp.float32)
    for time_tap in range(3):
        mixed = mixed + jnp.einsum('frwc,cd->frwd', earlier[time_tap:time_tap + frames], temporal[time_tap])
    grouped = mixed.reshape(frames, rows, columns, GROUPS, group_size)
    first = grouped.sum((1, 2, 4))
    second = (grouped * grouped).sum((1, 2, 4))
    counted = (jnp.arange(frames).astype(jnp.float32) + 1.0)[:, None] * float(rows * columns * group_size)
    mean = jnp.cumsum(first, 0) / counted
    variance = jnp.cumsum(second, 0) / counted - mean * mean
    inv_std = lax.rsqrt(variance + EPS)
    normed = (grouped - mean[:, None, None, :, None]) * inv_std[:, None, None, :, None]
    gain = norm_gain.reshape(GROUPS, group_size)
    shift = norm_shift.reshape(GROUPS, group_size)
    pre = normed * gain + shift
    sigma = jax.nn.sigmoid(pre)
    outputs = (inputs.astype(jnp.float32) + (pre * sigma).reshape(frames, rows, columns, channels)).astype(jnp.bfloat16)
    grad_pre = cotangent.astype(jnp.float32).reshape(grouped.shape) * (sigma * (1.0 + pre * (1.0 - sigma)))
    gain_part = (grad_pre * normed).sum((0, 1, 2)).reshape(channels)
    shift_part = grad_pre.sum((0, 1, 2)).reshape(channels)
    grad_normed = grad_pre * gain
    sum_a = grad_normed.sum((1, 2, 4))
    sum_b = (grad_normed * normed).sum((1, 2, 4))
    q_first = (-inv_std * sum_a + inv_std * inv_std * sum_b * mean) / counted
    q_second = -inv_std * inv_std * sum_b / (2.0 * counted)
    carry_first = jnp.cumsum(q_first[::-1], 0)[::-1]
    carry_second = jnp.cumsum(q_second[::-1], 0)[::-1]
    grad_mixed = inv_std[:, None, None, :, None] * grad_normed + carry_first[:, None, None, :, None] + 2.0 * grouped * carry_second[:, None, None, :, None]
    grad_mixed = grad_mixed.reshape(frames, rows, columns, channels).astype(jnp.bfloat16)
    mixed_wide = grad_mixed.astype(jnp.float32)
    later = jnp.pad(mixed_wide, ((0, 2), (0, 0), (0, 0), (0, 0)))
    grad_feature = jnp.zeros((frames, rows, columns, channels), jnp.float32)
    temporal_terms = []
    for time_tap in range(3):
        grad_feature = grad_feature + jnp.einsum('frwd,cd->frwc', later[2 - time_tap:2 - time_tap + frames], temporal[time_tap])
        temporal_terms.append(jnp.einsum('frwc,frwd->cd', earlier[time_tap:time_tap + frames], mixed_wide))
    temporal_part = jnp.stack(temporal_terms)
    grad_feature = grad_feature.astype(jnp.bfloat16).astype(jnp.float32)
    padded_grad = jnp.pad(grad_feature, ((0, 0), (1, 1), (1, 1), (0, 0)))
    grad_in = cotangent.astype(jnp.float32)
    spatial_terms = []
    for row_tap in range(3):
        for col_tap in range(3):
            back = padded_grad[:, 2 - row_tap:2 - row_tap + rows, 2 - col_tap:2 - col_tap + columns]
            grad_in = grad_in + jnp.einsum('frwd,cd->frwc', back, spatial[row_tap, col_tap])
            window = padded[:, row_tap:row_tap + rows, col_tap:col_tap + columns]
            spatial_terms.append(jnp.einsum('frwc,frwd->cd', window, grad_feature))
    spatial_part = jnp.stack(spatial_terms).reshape(3, 3, channels, channels)
    return (outputs, grad_in.astype(jnp.bfloat16), spatial_part, temporal_part, gain_part, shift_part)

def reference(inputs, spatial_kernel, temporal_kernel, norm_gain, norm_shift, cotangent):

    def per_clip(pair):
        return one_clip(pair, spatial_kernel, temporal_kernel, norm_gain, norm_shift)
    results = lax.map(per_clip, (inputs, cotangent))
    scale = 1.0 / math.sqrt(PIXELS)
    return (results[0], results[1], results[2].sum(0) * scale, results[3].sum(0) * scale, results[4].sum(0) * scale, results[5].sum(0) * scale)
```

```python
import math

import jax
import jax.numpy as jnp
from jax import lax
from jax.sharding import PartitionSpec as P

GROUPS = 32


EPS = 1e-05


def with_halo(value, sides, width):
    for axis, dim in sides:
        count, length = (lax.axis_size(axis), value.shape[dim])
        up = [(i, (i + 1) % count) for i in range(count - 1)]
        down = [(j, i) for i, j in up]
        last = lax.slice_in_dim(value, length - width, length, axis=dim)
        first = lax.slice_in_dim(value, 0, width, axis=dim)
        before = lax.ppermute(last, axis, up)
        after = lax.ppermute(first, axis, down)
        value = jnp.concatenate([before, value, after], axis=dim)
    return value


def from_behind(value, axis, steps):
    count = lax.axis_size(axis)
    first, last = (max(0, -steps), min(count, count - steps))
    return lax.ppermute(value, axis, [(source, source + steps) for source in range(first, last)])


def share(part, axes):
    count = 1
    for axis in axes:
        count *= lax.axis_size(axis)
    copies = jnp.broadcast_to(part[None], (count,) + part.shape)
    return lax.all_to_all(copies, axes, 0, 0, tiled=True)


def every_frame(first, second):
    frames = first.shape[0]
    time_devices, height_devices = lax.axis_size("tm"), lax.axis_size("height")
    mine = jnp.concatenate([first.reshape(-1), second.reshape(-1)])
    every = share(mine, ("tm", "height")).reshape(time_devices, height_devices, 2, frames, GROUPS)
    summed = every.sum(1).transpose(1, 0, 2, 3).reshape(2, time_devices * frames, GROUPS)
    return summed[0], summed[1]


def total_over_devices(part):
    rows, channels = part.shape
    ends = ("rep", "height")
    pieces = lax.axis_size("rep") * lax.axis_size("height")
    piece = -(-rows // pieces)
    padded = jnp.pad(part.astype(jnp.bfloat16), ((0, pieces * piece - rows), (0, 0)))
    got = lax.all_to_all(padded.reshape(pieces, piece, channels), ends, 0, 0, tiled=True)
    partial = got.astype(jnp.float32).sum(0).astype(jnp.bfloat16)
    summed = share(partial, ("tm",)).astype(jnp.float32).sum(0).astype(jnp.bfloat16)
    return share(summed, ends).astype(jnp.float32).reshape(pieces * piece, channels)[:rows]


def reverse_sum(values):
    return jnp.cumsum(values[::-1], 0)[::-1]


def widen(stat):
    return stat[:, None, None, :, None]


def shards(inputs, spatial_kernel, temporal_kernel, norm_gain, norm_shift, cotangent):
    pixels_in = inputs[0]
    frames, rows, columns, channels = pixels_in.shape
    group_size = channels // GROUPS
    time_devices = lax.axis_size("tm")
    height_devices = lax.axis_size("height")
    frame_start = lax.axis_index("tm") * frames
    per_frame = float(rows * height_devices * columns * group_size)
    halo_in = with_halo(pixels_in, (("height", 1),), 1)
    padded = jnp.pad(halo_in, ((0, 0), (0, 0), (1, 1), (0, 0)))
    total = jnp.zeros((frames, rows, columns, channels), jnp.float32)
    for row_tap in range(3):
        for col_tap in range(3):
            window = padded[:, row_tap : row_tap + rows, col_tap : col_tap + columns]
            total = total + jnp.einsum(
                "frwc,cd->frwd",
                window,
                spatial_kernel[row_tap, col_tap],
                preferred_element_type=jnp.float32,
            )
    feature = total.astype(jnp.bfloat16)
    prior = from_behind(feature[frames - 2 :], "tm", 1)
    earlier = jnp.concatenate([prior, feature], 0)
    mixed = jnp.zeros((frames, rows, columns, channels), jnp.float32)
    for time_tap in range(3):
        mixed = mixed + jnp.einsum(
            "frwc,cd->frwd",
            earlier[time_tap : time_tap + frames],
            temporal_kernel[time_tap],
            preferred_element_type=jnp.float32,
        )
    grouped = mixed.reshape(frames, rows, columns, GROUPS, group_size)
    first = grouped.sum((1, 2, 4))
    second = (grouped * grouped).sum((1, 2, 4))
    first_all, second_all = every_frame(first, second)
    counted_all = (jnp.arange(time_devices * frames).astype(jnp.float32) + 1.0)[:, None] * per_frame
    mean_all = jnp.cumsum(first_all, 0) / counted_all
    variance_all = jnp.cumsum(second_all, 0) / counted_all - mean_all * mean_all
    inv_std_all = lax.rsqrt(variance_all + EPS)
    mean = lax.dynamic_slice_in_dim(mean_all, frame_start, frames, 0)
    inv_std = lax.dynamic_slice_in_dim(inv_std_all, frame_start, frames, 0)
    normed = (grouped - widen(mean)) * widen(inv_std)
    gain = norm_gain.reshape(GROUPS, group_size)
    shift = norm_shift.reshape(GROUPS, group_size)
    pre = normed * gain + shift
    sigma = jax.nn.sigmoid(pre)
    outputs = (
        pixels_in.astype(jnp.float32) + (pre * sigma).reshape(frames, rows, columns, channels)
    ).astype(jnp.bfloat16)
    grad_pre = cotangent[0].astype(jnp.float32).reshape(grouped.shape) * (
        sigma * (1.0 + pre * (1.0 - sigma))
    )
    gain_part = (grad_pre * normed).sum((0, 1, 2)).reshape(channels)
    shift_part = grad_pre.sum((0, 1, 2)).reshape(channels)
    grad_normed = grad_pre * gain
    local_a = grad_normed.sum((1, 2, 4))
    local_b = (grad_normed * normed).sum((1, 2, 4))
    sum_a, sum_b = every_frame(local_a, local_b)
    q_first = (-inv_std_all * sum_a + inv_std_all * inv_std_all * sum_b * mean_all) / counted_all
    q_second = -inv_std_all * inv_std_all * sum_b / (2.0 * counted_all)
    carry_first = lax.dynamic_slice_in_dim(reverse_sum(q_first), frame_start, frames, 0)
    carry_second = lax.dynamic_slice_in_dim(reverse_sum(q_second), frame_start, frames, 0)
    grad_mixed = (
        widen(inv_std) * grad_normed + widen(carry_first) + 2.0 * grouped * widen(carry_second)
    )
    grad_mixed = grad_mixed.reshape(frames, rows, columns, channels).astype(jnp.bfloat16)
    temporal_terms = []
    for time_tap in range(3):
        temporal_terms.append(
            jnp.einsum(
                "frwc,frwd->cd",
                earlier[time_tap : time_tap + frames],
                grad_mixed,
                preferred_element_type=jnp.float32,
            )
        )
    temporal_part = jnp.stack(temporal_terms)
    following = from_behind(grad_mixed[:2], "tm", -1)
    later = jnp.concatenate([grad_mixed, following], 0)
    grad_feature = jnp.zeros((frames, rows, columns, channels), jnp.float32)
    for time_tap in range(3):
        grad_feature = grad_feature + jnp.einsum(
            "frwd,cd->frwc",
            later[2 - time_tap : 2 - time_tap + frames],
            temporal_kernel[time_tap],
            preferred_element_type=jnp.float32,
        )
    grad_feature = grad_feature.astype(jnp.bfloat16)
    halo_grad = with_halo(grad_feature, (("height", 1),), 1)
    padded_grad = jnp.pad(halo_grad, ((0, 0), (0, 0), (1, 1), (0, 0)))
    grad_in = cotangent[0].astype(jnp.float32)
    spatial_terms = []
    for row_tap in range(3):
        for col_tap in range(3):
            back = padded_grad[
                :, 2 - row_tap : 2 - row_tap + rows, 2 - col_tap : 2 - col_tap + columns
            ]
            grad_in = grad_in + jnp.einsum(
                "frwd,cd->frwc",
                back,
                spatial_kernel[row_tap, col_tap],
                preferred_element_type=jnp.float32,
            )
            window = padded[:, row_tap : row_tap + rows, col_tap : col_tap + columns]
            spatial_terms.append(
                jnp.einsum(
                    "frwc,frwd->cd", window, grad_feature, preferred_element_type=jnp.float32
                )
            )
    spatial_part = jnp.stack(spatial_terms).reshape(3, 3, channels, channels)
    grad_inputs = grad_in.astype(jnp.bfloat16)
    parts = [
        spatial_part.reshape(9 * channels, channels),
        temporal_part.reshape(3 * channels, channels),
        gain_part[None],
        shift_part[None],
    ]
    sums = total_over_devices(jnp.concatenate(parts, 0))
    spatial_sum = sums[: 9 * channels].reshape(3, 3, channels, channels)
    temporal_sum = sums[9 * channels : 12 * channels].reshape(3, channels, channels)
    gain_sum, shift_sum = sums[12 * channels], sums[12 * channels + 1]
    pixel_total = lax.axis_size("rep") * frames * time_devices * rows * height_devices * columns
    scale = 1.0 / math.sqrt(pixel_total)
    return (
        outputs[None],
        grad_inputs[None],
        spatial_sum * scale,
        temporal_sum * scale,
        gain_sum * scale,
        shift_sum * scale,
    )


def solution(mesh):
    in_specs = (
        P("rep", "tm", "height", None, None),
        P(),
        P(),
        P(),
        P(),
        P("rep", "tm", "height", None, None),
    )
    out_specs = (
        P("rep", "tm", "height", None, None),
        P("rep", "tm", "height", None, None),
        P(),
        P(),
        P(),
        P(),
    )
    return jax.shard_map(shards, mesh=mesh, in_specs=in_specs, out_specs=out_specs, check_vma=False)
```

```python
import functools
import math

import jax
import jax.numpy as jnp
from jax import lax
from jax.experimental import pallas as pl
from jax.experimental.pallas import tpu as pltpu
from jax.sharding import PartitionSpec as P

GROUPS = 32


EPS = 1e-05
TILE = 128


def iota(shape, dim):
    return lax.broadcasted_iota(jnp.int32, shape, dim)


def exact_dot(a, b):
    return lax.dot_general(
        a,
        b,
        (((1,), (0,)), ((), ())),
        precision=lax.Precision.HIGHEST,
        preferred_element_type=jnp.float32,
    )


def dot(a, b, turned=False):
    return lax.dot_general(
        a,
        b,
        (((1,), (1 if turned else 0,)), ((), ())),
        preferred_element_type=jnp.float32,
    )


def group_matrix(size):
    return (iota((TILE, TILE), 0) // size == iota((TILE, TILE), 1) // size).astype(jnp.float32)


def per_device_sums(got, time_devices, height_devices, earlier):
    shape = (2 * time_devices, got.shape[0])
    row, col = iota(shape, 0), iota(shape, 1)
    at, source = row % time_devices, col // (2 * height_devices)
    keep = (source < at) if earlier else (source == at)
    keep = keep & (row // time_devices == col % 2)
    return exact_dot(keep.astype(jnp.float32), got)


def moved(value, step, columns):
    pixels = value.shape[0]
    rolled = pltpu.roll(value, step % pixels, 0)
    place = iota(value.shape, 0) % columns
    edge = 0 if step > 0 else columns - 1
    return jnp.where(place == edge, 0.0, rolled)


def three_rows(block, rows, columns):
    size = rows * columns
    return jnp.concatenate(
        [block[i * columns : i * columns + size] for i in range(3)], axis=1
    )


def convolve(block, weight, rows, columns, turned):
    taps = dot(three_rows(block, rows, columns), weight, turned)
    c = taps.shape[1] // 3
    sign = -1 if turned else 1
    return (
        taps[:, c : 2 * c]
        + moved(taps[:, :c], sign, columns)
        + moved(taps[:, 2 * c :], -sign, columns)
    )


def flat(value):
    return value.reshape(-1, value.shape[-1])


def put_weight(weight_ref, spatial_ref):
    for i in range(3):
        for j in range(3):
            weight_ref[i * TILE : (i + 1) * TILE, j * TILE : (j + 1) * TILE] = spatial_ref[i, j]


def put_payload(out_ref, firsts, seconds):
    frames = len(firsts)
    sums = exact_dot(jnp.concatenate(firsts + seconds, 0), group_matrix(frames))
    lane = iota((1, TILE), 1) % frames
    rows = []
    for start in (0, frames):
        line = jnp.zeros((1, TILE), jnp.float32)
        for f in range(frames):
            line = jnp.where(lane == f, sums[start + f : start + f + 1], line)
        rows.append(line)
    line = jnp.where(iota((8, TILE), 0) % 2 == 0, rows[0], rows[1])
    for i in range(out_ref.shape[0] // 8):
        out_ref[i * 8 : (i + 1) * 8] = line


def own_features(x_ref, before_ref, after_ref, spatial_ref, feature_ref, weight_ref):
    put_weight(weight_ref, spatial_ref)
    frames, rows, columns, _ = x_ref.shape

    def one(f, _):
        block = jnp.concatenate([flat(before_ref[f]), flat(x_ref[f]), flat(after_ref[f])], 0)
        out = convolve(block, weight_ref[...], rows + 2, columns, False)
        feature_ref[f] = out.astype(jnp.bfloat16).reshape(feature_ref.shape[1:])
        return 0

    lax.fori_loop(0, frames, one, 0)


def mix(blocks, temporal_ref):
    return dot(jnp.concatenate(blocks, axis=1), flat(temporal_ref[...]))


def mixed_and_sums(
    feature_ref, prev_ref, spatial_ref, temporal_ref, prior_ref, mixed_ref, out_ref, weight_ref
):
    put_weight(weight_ref, spatial_ref)
    frames, rows, columns, _ = mixed_ref.shape

    def one(f, _):
        out = convolve(flat(prev_ref[f]), weight_ref[...], rows, columns, False)
        prior_ref[f] = out.astype(jnp.bfloat16).reshape(prior_ref.shape[1:])
        return 0

    lax.fori_loop(0, 2, one, 0)
    firsts, seconds = [], []
    for f in range(frames):
        blocks = [
            flat(prior_ref[f + k]) if f + k < 2 else flat(feature_ref[f + k - 2]) for k in range(3)
        ]
        out = mix(blocks, temporal_ref)
        mixed_ref[f] = out.reshape(mixed_ref.shape[1:])
        inner = out[columns : (rows - 1) * columns]
        firsts.append(inner.sum(0, keepdims=True))
        seconds.append((inner * inner).sum(0, keepdims=True))
    put_payload(out_ref, firsts, seconds)


def next_and_turned(
    next_ref,
    feature_ref,
    prior_ref,
    x_ref,
    before_ref,
    after_ref,
    spatial_ref,
    temporal_ref,
    mixed_ref,
    xt_ref,
    ft_ref,
    weight_ref,
    held_ref,
):
    put_weight(weight_ref, spatial_ref)
    frames, rows, columns, _ = x_ref.shape
    ext = rows + 2

    def one(f, _):
        out = convolve(flat(next_ref[f]), weight_ref[...], ext, columns, False)
        held_ref[f] = out.astype(jnp.bfloat16).reshape(held_ref.shape[1:])
        return 0

    lax.fori_loop(0, 2, one, 0)
    for f in range(2):
        blocks = [
            flat(feature_ref[f + 2 + k]) if f + k < 2 else flat(held_ref[f + k - 2])
            for k in range(3)
        ]
        mixed_ref[f] = mix(blocks, temporal_ref).reshape(mixed_ref.shape[1:])

    for f in range(frames):
        block = jnp.concatenate(
            [flat(before_ref[f, 1:]), flat(x_ref[f]), flat(after_ref[f, :1])], 0
        )
        xt_ref[f] = three_rows(block, rows, columns).astype(jnp.float32).T.astype(jnp.bfloat16)
        seen = [
            flat(prior_ref[f + k, 1 : rows + 1])
            if f + k < 2
            else flat(feature_ref[f + k - 2, 1 : rows + 1])
            for k in range(3)
        ]
        ft_ref[f] = jnp.concatenate(seen, axis=1).astype(jnp.float32).T.astype(jnp.bfloat16)


def counts(f, frames, time_devices, per_frame):
    at = iota((time_devices, TILE), 0) * frames + (f + 1)
    return at.astype(jnp.float32) * per_frame


def statistics_and_sums(
    time_devices,
    height_devices,
    per_frame,
    got_ref,
    mixed_ref,
    cot_ref,
    gain_ref,
    shift_ref,
    stats_ref,
    out_ref,
    parts_ref,
):
    frames, rows, columns, _ = cot_ref.shape
    me = lax.axis_index("tm")
    got = got_ref[...]
    here = per_device_sums(got, time_devices, height_devices, False)
    earlier = per_device_sums(got, time_devices, height_devices, True)
    group = group_matrix(frames)
    lane = iota(here.shape, 1) % frames
    for f in range(frames):
        sums = exact_dot(earlier + jnp.where(lane <= f, here, 0.0), group)
        count = counts(f, frames, time_devices, per_frame)
        mean = sums[:time_devices] / count
        variance = sums[time_devices:] / count - mean * mean
        at = 2 * f * time_devices
        stats_ref[at : at + time_devices] = mean
        stats_ref[at + time_devices : at + 2 * time_devices] = lax.rsqrt(variance + EPS)
    gain, shift = gain_ref[...], shift_ref[...]
    step = 4
    firsts, seconds = [], []
    for f in range(frames):
        mean = stats_ref[pl.ds(2 * f * time_devices + me, 1)]
        inv_std = stats_ref[pl.ds((2 * f + 1) * time_devices + me, 1)]

        def some(i, sums, f=f, mean=mean, inv_std=inv_std):
            normed = (flat(mixed_ref[f, pl.ds(1 + i * step, step)]) - mean) * inv_std
            pre = normed * gain + shift
            sigma = 1.0 / (1.0 + jnp.exp(-pre))
            cot = flat(cot_ref[f, pl.ds(i * step, step)]).astype(jnp.float32)
            grad = cot * (sigma * (1.0 + pre * (1.0 - sigma)))
            split = (-1, 8, TILE)
            return (
                sums[0] + grad.reshape(split).sum(0),
                sums[1] + (grad * normed).reshape(split).sum(0),
            )

        zero = jnp.zeros((8, TILE), jnp.float32)
        a, b = lax.fori_loop(0, rows // step, some, (zero, zero), unroll=2)
        firsts.append(a.sum(0, keepdims=True))
        seconds.append(b.sum(0, keepdims=True))
    put_payload(out_ref, [a * gain for a in firsts], [b * gain for b in seconds])
    total_a, total_b = sum(firsts[1:], firsts[0]), sum(seconds[1:], seconds[0])
    parts_ref[...] = jnp.where(iota((16, TILE), 0) < 8, total_b, total_a)


def outputs_and_grads(
    time_devices,
    stats_ref,
    mixed_ref,
    mixed_next_ref,
    x_ref,
    cot_ref,
    before_ref,
    after_ref,
    next_ref,
    gain_ref,
    shift_ref,
    scaled_ref,
    outputs_ref,
):
    frames, rows, columns, _ = cot_ref.shape
    me = lax.axis_index("tm")
    following = jnp.minimum(me + 1, time_devices - 1)
    gain, shift = gain_ref[...], shift_ref[...]
    step = 4

    def grads(mixed, cot, mean, inv_std):
        pre = (mixed - mean) * inv_std * gain + shift
        sigma = 1.0 / (1.0 + jnp.exp(-pre))
        grad = cot.astype(jnp.float32) * (sigma * (1.0 + pre * (1.0 - sigma)))
        return pre * sigma, inv_std * (grad * gain)

    for f in range(frames + 2):
        own = f < frames
        at, g = (me, f) if own else (following, f - frames)
        mean = stats_ref[pl.ds(2 * g * time_devices + at, 1)]
        inv_std = stats_ref[pl.ds((2 * g + 1) * time_devices + at, 1)]
        source = mixed_ref if own else mixed_next_ref

        def edge(row, cot, f=f, g=g, mean=mean, inv_std=inv_std, source=source):
            _, scaled = grads(source[g, row], cot, mean, inv_std)
            scaled_ref[f, row] = scaled

        edge(0, before_ref[frames + g, 1] if own else next_ref[2 + g, 1])
        edge(rows + 1, after_ref[frames + g, 0] if own else next_ref[2 + g, rows + 2])

        def some(i, _, f=f, g=g, own=own, mean=mean, inv_std=inv_std, source=source):
            here = pl.ds(1 + i * step, step)
            cot = cot_ref[g, pl.ds(i * step, step)] if own else next_ref[2 + g, pl.ds(2 + i * step, step)]
            silu, scaled = grads(flat(source[g, here]), flat(cot), mean, inv_std)
            scaled_ref[f, here] = scaled.reshape(step, columns, TILE)
            if own:
                kept = flat(x_ref[g, pl.ds(i * step, step)]).astype(jnp.float32) + silu
                outputs_ref[g, pl.ds(i * step, step)] = kept.astype(jnp.bfloat16).reshape(
                    step, columns, TILE
                )
            return 0

        lax.fori_loop(0, rows // step, some, 0, unroll=2)


def parameter_grads(
    time_devices,
    height_devices,
    per_frame,
    got_ref,
    stats_ref,
    scaled_ref,
    mixed_ref,
    mixed_next_ref,
    xt_ref,
    ft_ref,
    temporal_ref,
    parts_ref,
    feature_grad_ref,
    out_ref,
    carry_ref,
    mixed_grad_ref,
):
    frames, ext, columns, _ = mixed_ref.shape
    rows = ext - 2
    me, level = lax.axis_index("tm"), lax.axis_index("height")
    following = jnp.minimum(me + 1, time_devices - 1)
    here = per_device_sums(got_ref[...], time_devices, height_devices, False)
    group = group_matrix(frames)
    lane = iota(here.shape, 1) % frames
    firsts, seconds = [], []
    for f in range(frames):
        sums = exact_dot(jnp.where(lane == f, here, 0.0), group)
        sum_a, sum_b = sums[:time_devices], sums[time_devices:]
        at = 2 * f * time_devices
        mean = stats_ref[at : at + time_devices]
        inv_std = stats_ref[at + time_devices : at + 2 * time_devices]
        count = counts(f, frames, time_devices, per_frame)
        firsts.append((-inv_std * sum_a + inv_std * inv_std * sum_b * mean) / count)
        seconds.append(-inv_std * inv_std * sum_b / (2.0 * count))
    square = (time_devices, time_devices)
    later = (iota(square, 1) > iota(square, 0)).astype(jnp.float32)
    for kind, values in enumerate((firsts, seconds)):
        run = exact_dot(later, sum(values[1:], values[0]))
        for f in range(frames - 1, -1, -1):
            run = run + values[f]
            at = (2 * f + kind) * time_devices
            carry_ref[at : at + time_devices] = run
    exists = (me < time_devices - 1).astype(jnp.float32)
    for f in range(frames + 2):
        own = f < frames
        at, g = (me, f) if own else (following, f - frames)
        first = carry_ref[pl.ds(2 * g * time_devices + at, 1)]
        second = 2.0 * carry_ref[pl.ds((2 * g + 1) * time_devices + at, 1)]
        source = mixed_ref if own else mixed_next_ref

        def some(i, _, f=f, g=g, own=own, first=first, second=second, source=source):
            at = pl.ds(i * 3, 3)
            grad = flat(scaled_ref[f, at]) + first + flat(source[g, at]) * second
            if not own:
                grad = grad * exists
            mixed_grad_ref[f, at] = grad.astype(jnp.bfloat16).reshape(3, columns, TILE)
            return 0

        lax.fori_loop(0, ext // 3, some, 0, unroll=3)
    turned = jnp.concatenate([temporal_ref[k] for k in range(3)], axis=1)
    place = iota((ext * columns, TILE), 0) // columns
    outside = ((place == 0) & (level == 0)) | ((place == ext - 1) & (level == height_devices - 1))
    spatial = jnp.zeros((3 * TILE, 3 * TILE), jnp.float32)
    temporal = jnp.zeros((3 * TILE, TILE), jnp.float32)
    for f in range(frames):
        blocks = [flat(mixed_grad_ref[f + 2 - k]) for k in range(3)]
        grad = dot(jnp.concatenate(blocks, axis=1), turned, True)
        grad = jnp.where(outside, 0.0, grad).astype(jnp.bfloat16)
        feature_grad_ref[f] = grad.reshape(ext, columns, TILE)
        inner = grad[columns : (rows + 1) * columns]
        wide = inner.astype(jnp.float32)
        shifted = jnp.concatenate(
            [
                moved(wide, -1, columns).astype(jnp.bfloat16),
                inner,
                moved(wide, 1, columns).astype(jnp.bfloat16),
            ],
            axis=1,
        )
        spatial = spatial + dot(xt_ref[f], shifted)
        temporal = temporal + dot(ft_ref[f], flat(mixed_grad_ref[f, 1 : rows + 1]))
    pieces = out_ref.shape[0]
    piece = 12 * TILE // pieces
    blocks = [spatial[:, j * TILE : (j + 1) * TILE] for j in range(3)] + [temporal]
    whole = jnp.concatenate(blocks, axis=0).astype(jnp.bfloat16)
    for p in range(pieces):
        out_ref[p, :piece] = whole[p * piece : (p + 1) * piece]
        tail = parts_ref[8 * min(p, 1) : 8 * min(p, 1) + 8]
        tail = jnp.where((iota((8, TILE), 0) == 0) & (p < 2), tail, 0.0)
        out_ref[p, piece : piece + 8] = tail.astype(jnp.bfloat16)


def input_grads(grad_ref, cot_ref, spatial_ref, out_ref, weight_ref):
    frames, rows, columns, _ = cot_ref.shape
    for s in range(3):
        for j in range(3):
            weight_ref[j * TILE : (j + 1) * TILE, s * TILE : (s + 1) * TILE] = spatial_ref[2 - s, j]

    def one(f, _):
        out = convolve(flat(grad_ref[f]), weight_ref[...], rows, columns, True)
        out = out + flat(cot_ref[f]).astype(jnp.float32)
        out_ref[f] = out.astype(jnp.bfloat16).reshape(out_ref.shape[1:])
        return 0

    lax.fori_loop(0, frames, one, 0)


def sum_and_copy(got_ref, out_ref):
    total = got_ref[0].astype(jnp.float32)
    for i in range(1, got_ref.shape[0]):
        total = total + got_ref[i].astype(jnp.float32)
    total = total.astype(jnp.bfloat16)
    for i in range(out_ref.shape[0]):
        out_ref[i] = total


def call(body, name, outs, args, scratch=(), flops=0):
    moved_bytes = sum(a.size * a.dtype.itemsize for a in (*args, *outs))
    whole = pl.BlockSpec(memory_space=pltpu.VMEM)
    return pl.pallas_call(
        body,
        name=name,
        out_shape=outs,
        in_specs=[whole] * len(args),
        out_specs=[whole] * len(outs),
        scratch_shapes=list(scratch),
        compiler_params=pltpu.CompilerParams(vmem_limit_bytes=48 * 1024 * 1024),
        cost_estimate=pl.CostEstimate(
            flops=flops, bytes_accessed=moved_bytes, transcendentals=0
        ),
    )(*args)


def shards(inputs, spatial_kernel, temporal_kernel, norm_gain, norm_shift, cotangent):
    x, cot = inputs[0], cotangent[0]
    frames, rows, columns, channels = x.shape
    ext = rows + 2
    reps, time_devices, height_devices = (lax.axis_size(a) for a in ("rep", "tm", "height"))
    per_frame = float(rows * height_devices * columns * (channels // GROUPS))
    bf16, f32 = jnp.bfloat16, jnp.float32
    out = jax.ShapeDtypeStruct
    frame = (columns, channels)
    gain, shift = norm_gain[None], norm_shift[None]
    weight = pltpu.VMEM((3 * channels, 3 * channels), bf16)
    conv = 2 * 9 * channels * channels * columns

    up = [(i, i + 1) for i in range(height_devices - 1)]
    down = [(j, i) for i, j in up]
    before = lax.ppermute(jnp.concatenate([x[:, rows - 2 :], cot[:, rows - 2 :]], 0), "height", up)
    after = lax.ppermute(jnp.concatenate([x[:, :2], cot[:, :2]], 0), "height", down)
    onward = [(i, i + 1) for i in range(time_devices - 1)]
    back = [(j, i) for i, j in onward]
    last = jnp.concatenate([before[2:4], x[2:4], after[2:4]], 1)
    prev = lax.ppermute(last, "tm", onward)
    first = jnp.concatenate(
        [
            jnp.concatenate([before[:2], before[4:6]], 0),
            jnp.concatenate([x[:2], cot[:2]], 0),
            jnp.concatenate([after[:2], after[4:6]], 0),
        ],
        1,
    )
    following = lax.ppermute(first, "tm", back)

    (feature,) = call(
        own_features,
        "own_features",
        [out((frames, ext) + frame, bf16)],
        (x, before, after, spatial_kernel),
        [weight],
        conv * frames * ext,
    )
    peers = time_devices * height_devices
    prior, mixed, payload = call(
        mixed_and_sums,
        "mixed_and_sums",
        [
            out((2, ext) + frame, bf16),
            out((frames, ext) + frame, f32),
            out((2 * peers, channels), f32),
        ],
        (feature, prev, spatial_kernel, temporal_kernel),
        [weight],
        conv * frames * ext,
    )
    share = ("tm", "height")
    got = lax.all_to_all(payload, share, 0, 0, tiled=True)
    mixed_next, xt, ft = call(
        next_and_turned,
        "next_and_turned",
        [
            out((2, ext) + frame, f32),
            out((frames, 3 * channels, rows * columns), bf16),
            out((frames, 3 * channels, rows * columns), bf16),
        ],
        (following, feature, prior, x, before, after, spatial_kernel, temporal_kernel),
        [weight, pltpu.VMEM((2, ext) + frame, bf16)],
        conv * 2 * ext,
    )
    stats, payload, parts = call(
        functools.partial(statistics_and_sums, time_devices, height_devices, per_frame),
        "statistics_and_sums",
        [
            out((2 * frames * time_devices, channels), f32),
            out((2 * peers, channels), f32),
            out((16, channels), f32),
        ],
        (got, mixed, cot, gain, shift),
    )
    got = lax.all_to_all(payload, share, 0, 0, tiled=True)
    scaled, outputs = call(
        functools.partial(outputs_and_grads, time_devices),
        "outputs_and_grads",
        [out((frames + 2, ext) + frame, f32), out((frames, rows) + frame, bf16)],
        (stats, mixed, mixed_next, x, cot, before, after, following, gain, shift),
    )
    ends = ("rep", "height")
    pieces = reps * height_devices
    feature_grad, partial = call(
        functools.partial(parameter_grads, time_devices, height_devices, per_frame),
        "parameter_grads",
        [
            out((frames, ext) + frame, bf16),
            out((pieces, 12 * TILE // pieces + 8, channels), bf16),
        ],
        (got, stats, scaled, mixed, mixed_next, xt, ft, temporal_kernel, parts),
        [
            pltpu.VMEM((2 * frames * time_devices, channels), f32),
            pltpu.VMEM((frames + 2, ext) + frame, bf16),
        ],
        conv * frames * rows * 2,
    )
    partial = lax.all_to_all(partial, ends, 0, 0, tiled=True)
    (grad_inputs,) = call(
        input_grads,
        "input_grads",
        [out((frames, rows) + frame, bf16)],
        (feature_grad, cot, spatial_kernel),
        [weight],
        conv * frames * rows,
    )
    piece = partial.shape[1:]
    (partial,) = call(sum_and_copy, "sum_first", [out((time_devices,) + piece, bf16)], (partial,))
    partial = lax.all_to_all(partial, "tm", 0, 0, tiled=True)
    (partial,) = call(sum_and_copy, "sum_second", [out((pieces,) + piece, bf16)], (partial,))
    sums = lax.all_to_all(partial, ends, 0, 0, tiled=True).astype(f32)
    pixel_total = reps * frames * time_devices * rows * height_devices * columns
    scale = 1.0 / math.sqrt(pixel_total)
    body = piece[0] - 8
    grads = (sums[:, :body] * scale).reshape(12, channels, channels)
    spatial_sum = grads[:9].reshape(3, 3, channels, channels).swapaxes(0, 1)
    return (
        outputs[None],
        grad_inputs[None],
        spatial_sum,
        grads[9:],
        sums[0, body] * scale,
        sums[1, body] * scale,
    )


def solution(mesh):
    in_specs = (
        P("rep", "tm", "height", None, None),
        P(),
        P(),
        P(),
        P(),
        P("rep", "tm", "height", None, None),
    )
    out_specs = (
        P("rep", "tm", "height", None, None),
        P("rep", "tm", "height", None, None),
        P(),
        P(),
        P(),
        P(),
    )
    return jax.shard_map(shards, mesh=mesh, in_specs=in_specs, out_specs=out_specs, check_vma=False)
```

```python
import functools
import math

import jax
import jax.numpy as jnp
from jax import lax
from jax.experimental import pallas as pl
from jax.experimental.pallas import tpu as pltpu
from jax.sharding import PartitionSpec as P

GROUPS = 32


EPS = 1e-05
TILE = 128
WIDE, NARROW = 58, 16


def iota(shape, dim):
    return lax.broadcasted_iota(jnp.int32, shape, dim)


def exact_dot(a, b):
    return lax.dot_general(
        a,
        b,
        (((1,), (0,)), ((), ())),
        precision=lax.Precision.HIGHEST,
        preferred_element_type=jnp.float32,
    )


def dot(a, b, turned=False):
    return lax.dot_general(
        a,
        b,
        (((1,), (1 if turned else 0,)), ((), ())),
        preferred_element_type=jnp.float32,
    )


def group_matrix(size):
    return (iota((TILE, TILE), 0) // size == iota((TILE, TILE), 1) // size).astype(jnp.float32)


def per_device_sums(got, time_devices, height_devices, earlier):
    shape = (2 * time_devices, got.shape[0])
    row, col = iota(shape, 0), iota(shape, 1)
    at, source = row % time_devices, col // (2 * height_devices)
    keep = (source < at) if earlier else (source == at)
    keep = keep & (row // time_devices == col % 2)
    return exact_dot(keep.astype(jnp.float32), got)


def moved(value, step, columns):
    pixels = value.shape[0]
    rolled = pltpu.roll(value, step % pixels, 0)
    place = iota(value.shape, 0) % columns
    edge = 0 if step > 0 else columns - 1
    return jnp.where(place == edge, 0.0, rolled)


def three_rows(block, rows, columns):
    size = rows * columns
    return jnp.concatenate(
        [block[i * columns : i * columns + size] for i in range(3)], axis=1
    )


def convolve(block, weight, rows, columns, turned):
    taps = dot(three_rows(block, rows, columns), weight, turned)
    c = taps.shape[1] // 3
    sign = -1 if turned else 1
    return (
        taps[:, c : 2 * c]
        + moved(taps[:, :c], sign, columns)
        + moved(taps[:, 2 * c :], -sign, columns)
    )


def flat(value):
    return value.reshape(-1, value.shape[-1])


def put_weight(weight_ref, spatial_ref):
    for i in range(3):
        for j in range(3):
            weight_ref[i * TILE : (i + 1) * TILE, j * TILE : (j + 1) * TILE] = spatial_ref[i, j]


def put_payload(out_ref, firsts, seconds):
    frames = len(firsts)
    sums = exact_dot(jnp.concatenate(firsts + seconds, 0), group_matrix(frames))
    lane = iota((1, TILE), 1) % frames
    rows = []
    for start in (0, frames):
        line = jnp.zeros((1, TILE), jnp.float32)
        for f in range(frames):
            line = jnp.where(lane == f, sums[start + f : start + f + 1], line)
        rows.append(line)
    line = jnp.where(iota((8, TILE), 0) % 2 == 0, rows[0], rows[1])
    for i in range(out_ref.shape[0] // 8):
        out_ref[i * 8 : (i + 1) * 8] = line


def fetch(pairs, sems):
    copies = [pltpu.make_async_copy(a, b, sems.at[i]) for i, (a, b) in enumerate(pairs)]
    for copy in copies:
        copy.start()
    return copies


def turned(value):
    return value.astype(jnp.float32).T.astype(jnp.bfloat16)


def own_features(
    x_ref,
    before_ref,
    after_ref,
    spatial_ref,
    feature_ref,
    late_ref,
    xt_ref,
    ft_ref,
    weight_ref,
    xt_held,
    ft_held,
    sems,
):
    put_weight(weight_ref, spatial_ref)
    frames, rows, columns, _ = x_ref.shape

    def one(f, _):
        block = jnp.concatenate([flat(before_ref[f]), flat(x_ref[f]), flat(after_ref[f])], 0)
        out = convolve(block, weight_ref[...], rows + 2, columns, False)
        feature_ref[f] = out.astype(jnp.bfloat16).reshape(feature_ref.shape[1:])
        return 0

    lax.fori_loop(0, frames, one, 0)
    for f in range(frames):
        block = jnp.concatenate(
            [flat(before_ref[f, 1:]), flat(x_ref[f]), flat(after_ref[f, :1])], 0
        )
        xt_held[f] = turned(three_rows(block, rows, columns))
        ft_held[f] = turned(flat(feature_ref[f, 1 : rows + 1]))
    copies = fetch(
        [
            (feature_ref.at[pl.ds(frames - 2, 2)], late_ref),
            (xt_held, xt_ref),
            (ft_held, ft_ref),
        ],
        sems,
    )
    for copy in copies:
        copy.wait()


def mix(blocks, temporal_ref):
    return dot(jnp.concatenate(blocks, axis=1), flat(temporal_ref[...]))


def mixed_and_sums(
    feature_ref,
    prev_ref,
    spatial_ref,
    temporal_ref,
    mixed_ref,
    out_ref,
    ft_ref,
    weight_ref,
    prior_ref,
    ft_held,
    sems,
):
    put_weight(weight_ref, spatial_ref)
    frames, rows, columns, _ = mixed_ref.shape

    def one(f, _):
        out = convolve(flat(prev_ref[f]), weight_ref[...], rows, columns, False)
        prior_ref[f] = out.astype(jnp.bfloat16).reshape(prior_ref.shape[1:])
        return 0

    lax.fori_loop(0, 2, one, 0)
    for f in range(2):
        ft_held[f] = turned(flat(prior_ref[f, 1 : rows - 1]))
    copies = fetch([(ft_held, ft_ref)], sems)
    firsts, seconds = [], []
    for f in range(frames):
        blocks = [
            flat(prior_ref[f + k]) if f + k < 2 else flat(feature_ref[f + k - 2]) for k in range(3)
        ]
        out = mix(blocks, temporal_ref)
        mixed_ref[f] = out.reshape(mixed_ref.shape[1:])
        inner = out[columns : (rows - 1) * columns]
        firsts.append(inner.sum(0, keepdims=True))
        seconds.append((inner * inner).sum(0, keepdims=True))
    put_payload(out_ref, firsts, seconds)
    copies[0].wait()


def next_frames(
    next_hbm,
    late_hbm,
    spatial_hbm,
    temporal_hbm,
    mixed_ref,
    weight_ref,
    held_ref,
    next_ref,
    late_ref,
    spatial_ref,
    temporal_ref,
    sems,
):
    copies = fetch(
        [
            (spatial_hbm, spatial_ref),
            (next_hbm.at[pl.ds(0, 2)], next_ref),
            (late_hbm, late_ref),
            (temporal_hbm, temporal_ref),
        ],
        sems,
    )
    _, ext, columns, _ = mixed_ref.shape
    copies[0].wait()
    put_weight(weight_ref, spatial_ref)
    copies[1].wait()

    def one(f, _):
        out = convolve(flat(next_ref[f]), weight_ref[...], ext, columns, False)
        held_ref[f] = out.astype(jnp.bfloat16).reshape(held_ref.shape[1:])
        return 0

    lax.fori_loop(0, 2, one, 0)
    copies[2].wait()
    copies[3].wait()
    for f in range(2):
        blocks = [flat(late_ref[f + k]) if f + k < 2 else flat(held_ref[f + k - 2]) for k in range(3)]
        mixed_ref[f] = mix(blocks, temporal_ref).reshape(mixed_ref.shape[1:])


def counts(f, frames, time_devices, per_frame):
    at = iota((time_devices, TILE), 0) * frames + (f + 1)
    return at.astype(jnp.float32) * per_frame


def statistics_and_sums(
    time_devices,
    height_devices,
    per_frame,
    got_ref,
    mixed_ref,
    cot_ref,
    gain_ref,
    shift_ref,
    stats_ref,
    out_ref,
    parts_ref,
):
    frames, rows, columns, _ = cot_ref.shape
    me = lax.axis_index("tm")
    got = got_ref[...]
    here = per_device_sums(got, time_devices, height_devices, False)
    earlier = per_device_sums(got, time_devices, height_devices, True)
    group = group_matrix(frames)
    lane = iota(here.shape, 1) % frames
    for f in range(frames):
        sums = exact_dot(earlier + jnp.where(lane <= f, here, 0.0), group)
        count = counts(f, frames, time_devices, per_frame)
        mean = sums[:time_devices] / count
        variance = sums[time_devices:] / count - mean * mean
        at = 2 * f * time_devices
        stats_ref[at : at + time_devices] = mean
        stats_ref[at + time_devices : at + 2 * time_devices] = lax.rsqrt(variance + EPS)
    gain, shift = gain_ref[...], shift_ref[...]
    step = 4
    firsts, seconds = [], []
    for f in range(frames):
        mean = stats_ref[pl.ds(2 * f * time_devices + me, 1)]
        inv_std = stats_ref[pl.ds((2 * f + 1) * time_devices + me, 1)]

        def some(i, sums, f=f, mean=mean, inv_std=inv_std):
            normed = (flat(mixed_ref[f, pl.ds(1 + i * step, step)]) - mean) * inv_std
            pre = normed * gain + shift
            sigma = 1.0 / (1.0 + jnp.exp(-pre))
            cot = flat(cot_ref[f, pl.ds(i * step, step)]).astype(jnp.float32)
            grad = cot * (sigma * (1.0 + pre * (1.0 - sigma)))
            split = (-1, 8, TILE)
            return (
                sums[0] + grad.reshape(split).sum(0),
                sums[1] + (grad * normed).reshape(split).sum(0),
            )

        zero = jnp.zeros((8, TILE), jnp.float32)
        a, b = lax.fori_loop(0, rows // step, some, (zero, zero), unroll=2)
        firsts.append(a.sum(0, keepdims=True))
        seconds.append(b.sum(0, keepdims=True))
    put_payload(out_ref, [a * gain for a in firsts], [b * gain for b in seconds])
    total_a, total_b = sum(firsts[1:], firsts[0]), sum(seconds[1:], seconds[0])
    parts_ref[...] = jnp.where(iota((16, TILE), 0) < 8, total_b, total_a)


def outputs_and_grads(
    time_devices,
    stats_ref,
    mixed_ref,
    mixed_next_ref,
    x_ref,
    cot_ref,
    gain_ref,
    shift_ref,
    before_hbm,
    after_hbm,
    next_hbm,
    outputs_ref,
    scaled_hbm,
    scaled_ref,
    before_ref,
    after_ref,
    next_ref,
    in_sems,
    out_sems,
):
    frames, rows, columns, _ = cot_ref.shape
    copies = fetch(
        [
            (before_hbm.at[pl.ds(frames, frames)], before_ref),
            (after_hbm.at[pl.ds(frames, frames)], after_ref),
            (next_hbm.at[pl.ds(2, 2)], next_ref),
        ],
        in_sems,
    )
    me = lax.axis_index("tm")
    following = jnp.minimum(me + 1, time_devices - 1)
    gain, shift = gain_ref[...], shift_ref[...]
    step = 4

    def grads(mixed, cot, mean, inv_std):
        pre = (mixed - mean) * inv_std * gain + shift
        sigma = 1.0 / (1.0 + jnp.exp(-pre))
        grad = cot.astype(jnp.float32) * (sigma * (1.0 + pre * (1.0 - sigma)))
        return pre * sigma, inv_std * (grad * gain)

    leaving = []

    for f in range(frames + 2):
        own = f < frames
        at, g = (me, f) if own else (following, f - frames)
        mean = stats_ref[pl.ds(2 * g * time_devices + at, 1)]
        inv_std = stats_ref[pl.ds((2 * g + 1) * time_devices + at, 1)]
        source = mixed_ref if own else mixed_next_ref

        def edge(row, cot, f=f, g=g, mean=mean, inv_std=inv_std, source=source):
            _, scaled = grads(source[g, row], cot, mean, inv_std)
            scaled_ref[f, row] = scaled


        if f == frames:
            copies[2].wait()

        def some(i, _, f=f, g=g, own=own, mean=mean, inv_std=inv_std, source=source):
            here = pl.ds(1 + i * step, step)
            cot = cot_ref[g, pl.ds(i * step, step)] if own else next_ref[g, pl.ds(2 + i * step, step)]
            silu, scaled = grads(flat(source[g, here]), flat(cot), mean, inv_std)
            scaled_ref[f, here] = scaled.reshape(step, columns, TILE)
            if own:
                kept = flat(x_ref[g, pl.ds(i * step, step)]).astype(jnp.float32) + silu
                outputs_ref[g, pl.ds(i * step, step)] = kept.astype(jnp.bfloat16).reshape(
                    step, columns, TILE
                )
            return 0

        lax.fori_loop(0, rows // step, some, 0, unroll=2)
        if f == 0:
            copies[0].wait()
            copies[1].wait()
        edge(0, before_ref[g, 1] if own else next_ref[g, 1])
        edge(rows + 1, after_ref[g, 0] if own else next_ref[g, rows + 2])
        copy = pltpu.make_async_copy(scaled_ref.at[f], scaled_hbm.at[f], out_sems.at[f])
        copy.start()
        leaving.append(copy)
    for copy in leaving:
        copy.wait()


def parameter_grads(
    time_devices,
    height_devices,
    per_frame,
    got_ref,
    stats_ref,
    parts_ref,
    mixed_hbm,
    mixed_next_hbm,
    scaled_hbm,
    xt_hbm,
    ft_hbm,
    ft_prior_hbm,
    temporal_hbm,
    out_ref,
    feature_grad_hbm,
    carry_ref,
    mixed_grad_ref,
    feature_grad_ref,
    mixed_ref,
    scaled_ref,
    xt_ref,
    ft_ref,
    temporal_ref,
    sems,
    out_sems,
):
    frames, ext, columns, _ = feature_grad_ref.shape
    rows = ext - 2
    copies = fetch(
        [
            (mixed_hbm, mixed_ref.at[pl.ds(0, frames)]),
            (mixed_next_hbm, mixed_ref.at[pl.ds(frames, 2)]),
            (scaled_hbm, scaled_ref),
            (temporal_hbm, temporal_ref),
            (xt_hbm, xt_ref),
            (ft_hbm, ft_ref.at[pl.ds(2, frames)]),
            (ft_prior_hbm, ft_ref.at[pl.ds(0, 2)]),
        ],
        sems,
    )
    me, level = lax.axis_index("tm"), lax.axis_index("height")
    following = jnp.minimum(me + 1, time_devices - 1)
    here = per_device_sums(got_ref[...], time_devices, height_devices, False)
    group = group_matrix(frames)
    lane = iota(here.shape, 1) % frames
    firsts, seconds = [], []
    for f in range(frames):
        sums = exact_dot(jnp.where(lane == f, here, 0.0), group)
        sum_a, sum_b = sums[:time_devices], sums[time_devices:]
        at = 2 * f * time_devices
        mean = stats_ref[at : at + time_devices]
        inv_std = stats_ref[at + time_devices : at + 2 * time_devices]
        count = counts(f, frames, time_devices, per_frame)
        firsts.append((-inv_std * sum_a + inv_std * inv_std * sum_b * mean) / count)
        seconds.append(-inv_std * inv_std * sum_b / (2.0 * count))
    square = (time_devices, time_devices)
    later = (iota(square, 1) > iota(square, 0)).astype(jnp.float32)
    for kind, values in enumerate((firsts, seconds)):
        run = exact_dot(later, sum(values[1:], values[0]))
        for f in range(frames - 1, -1, -1):
            run = run + values[f]
            at = (2 * f + kind) * time_devices
            carry_ref[at : at + time_devices] = run
    for copy in copies[:3]:
        copy.wait()
    exists = (me < time_devices - 1).astype(jnp.float32)
    for f in range(frames + 2):
        own = f < frames
        at, g = (me, f) if own else (following, f - frames)
        first = carry_ref[pl.ds(2 * g * time_devices + at, 1)]
        second = 2.0 * carry_ref[pl.ds((2 * g + 1) * time_devices + at, 1)]

        def some(i, _, f=f, own=own, first=first, second=second):
            at = pl.ds(i * 3, 3)
            grad = flat(scaled_ref[f, at]) + first + flat(mixed_ref[f, at]) * second
            if not own:
                grad = grad * exists
            mixed_grad_ref[f, at] = grad.astype(jnp.bfloat16).reshape(3, columns, TILE)
            return 0

        lax.fori_loop(0, ext // 3, some, 0, unroll=3)
    copies[3].wait()
    back = jnp.concatenate([temporal_ref[k] for k in range(3)], axis=1)
    for copy in copies[4:]:
        copy.wait()
    leaving = []
    place = iota((ext * columns, TILE), 0) // columns
    outside = ((place == 0) & (level == 0)) | ((place == ext - 1) & (level == height_devices - 1))
    spatial = jnp.zeros((3 * TILE, 3 * TILE), jnp.float32)
    temporal = jnp.zeros((3 * TILE, TILE), jnp.float32)
    for f in range(frames):
        blocks = [flat(mixed_grad_ref[f + 2 - k]) for k in range(3)]
        grad = dot(jnp.concatenate(blocks, axis=1), back, True)
        grad = jnp.where(outside, 0.0, grad).astype(jnp.bfloat16)
        feature_grad_ref[f] = grad.reshape(ext, columns, TILE)
        copy = pltpu.make_async_copy(
            feature_grad_ref.at[f], feature_grad_hbm.at[f], out_sems.at[f]
        )
        copy.start()
        leaving.append(copy)
        inner = grad[columns : (rows + 1) * columns]
        wide = inner.astype(jnp.float32)
        shifted = jnp.concatenate(
            [
                moved(wide, -1, columns).astype(jnp.bfloat16),
                inner,
                moved(wide, 1, columns).astype(jnp.bfloat16),
            ],
            axis=1,
        )
        spatial = spatial + dot(xt_ref[f], shifted)
        temporal = temporal + dot(flat(ft_ref[f : f + 3]), flat(mixed_grad_ref[f, 1 : rows + 1]))
    pieces = out_ref.shape[0]
    piece = 12 * TILE // pieces
    blocks = [spatial[:, j * TILE : (j + 1) * TILE] for j in range(3)] + [temporal]
    whole = jnp.concatenate(blocks, axis=0).astype(jnp.bfloat16)
    for p in range(pieces):
        out_ref[p, :piece] = whole[p * piece : (p + 1) * piece]
        tail = parts_ref[8 * min(p, 1) : 8 * min(p, 1) + 8]
        tail = jnp.where((iota((8, TILE), 0) == 0) & (p < 2), tail, 0.0)
        out_ref[p, piece : piece + 8] = tail.astype(jnp.bfloat16)
    for copy in leaving:
        copy.wait()


def input_grads(grad_ref, cot_ref, spatial_ref, out_ref, weight_ref):
    frames, rows, columns, _ = cot_ref.shape
    for s in range(3):
        for j in range(3):
            weight_ref[j * TILE : (j + 1) * TILE, s * TILE : (s + 1) * TILE] = spatial_ref[2 - s, j]

    def one(f, _):
        out = convolve(flat(grad_ref[f]), weight_ref[...], rows, columns, True)
        out = out + flat(cot_ref[f]).astype(jnp.float32)
        out_ref[f] = out.astype(jnp.bfloat16).reshape(out_ref.shape[1:])
        return 0

    lax.fori_loop(0, frames, one, 0)


def sum_and_copy(got_ref, out_ref):
    total = got_ref[0].astype(jnp.float32)
    for i in range(1, got_ref.shape[0]):
        total = total + got_ref[i].astype(jnp.float32)
    total = total.astype(jnp.bfloat16)
    for i in range(out_ref.shape[0]):
        out_ref[i] = total


def finish(scale, got_ref, spatial_ref, temporal_ref, gain_ref, shift_ref):
    pieces, piece = got_ref.shape[0], got_ref.shape[1] - 8
    for p in range(pieces):
        value = got_ref[p].astype(jnp.float32) * scale
        if p < 2:
            (gain_ref, shift_ref)[p][...] = value[piece : piece + 1]
        at = p * piece
        while at < (p + 1) * piece:
            block, row = at // TILE, at % TILE
            size = min(TILE - row, (p + 1) * piece - at)
            part = value[at - p * piece : at - p * piece + size]
            if block < 9:
                spatial_ref[block % 3, block // 3, row : row + size] = part
            else:
                temporal_ref[block - 9, row : row + size] = part
            at += size


def call(body, name, outs, args, scratch=(), flops=0, far=(), far_outs=(), limit=WIDE):
    everything = (*args, *far, *outs, *far_outs)
    moved_bytes = sum(a.size * a.dtype.itemsize for a in everything)
    near, away = pl.BlockSpec(memory_space=pltpu.VMEM), pl.BlockSpec(memory_space=pl.ANY)
    return pl.pallas_call(
        body,
        name=name,
        out_shape=[*outs, *far_outs],
        in_specs=[near] * len(args) + [away] * len(far),
        out_specs=[near] * len(outs) + [away] * len(far_outs),
        scratch_shapes=list(scratch),
        compiler_params=pltpu.CompilerParams(vmem_limit_bytes=limit * 1024 * 1024),
        cost_estimate=pl.CostEstimate(
            flops=flops, bytes_accessed=moved_bytes, transcendentals=0
        ),
    )(*args, *far)


def shards(inputs, spatial_kernel, temporal_kernel, norm_gain, norm_shift, cotangent):
    x, cot = inputs[0], cotangent[0]
    frames, rows, columns, channels = x.shape
    ext = rows + 2
    reps, time_devices, height_devices = (lax.axis_size(a) for a in ("rep", "tm", "height"))
    per_frame = float(rows * height_devices * columns * (channels // GROUPS))
    bf16, f32 = jnp.bfloat16, jnp.float32
    out = jax.ShapeDtypeStruct
    frame = (columns, channels)
    gain, shift = norm_gain[None], norm_shift[None]
    weight = pltpu.VMEM((3 * channels, 3 * channels), bf16)
    conv = 2 * 9 * channels * channels * columns

    up = [(i, i + 1) for i in range(height_devices - 1)]
    down = [(j, i) for i, j in up]
    before = lax.ppermute(jnp.concatenate([x[:, rows - 2 :], cot[:, rows - 2 :]], 0), "height", up)
    after = lax.ppermute(jnp.concatenate([x[:, :2], cot[:, :2]], 0), "height", down)
    onward = [(i, i + 1) for i in range(time_devices - 1)]
    back = [(j, i) for i, j in onward]
    last = jnp.concatenate([before[2:4], x[2:4], after[2:4]], 1)
    prev = lax.ppermute(last, "tm", onward)
    first = jnp.concatenate(
        [
            jnp.concatenate([before[:2], before[4:6]], 0),
            jnp.concatenate([x[:2], cot[:2]], 0),
            jnp.concatenate([after[:2], after[4:6]], 0),
        ],
        1,
    )
    following = lax.ppermute(first, "tm", back)

    dma = lambda count: pltpu.SemaphoreType.DMA((count,))
    turned_x = out((frames, 3 * channels, rows * columns), bf16)
    turned_own = out((frames, channels, rows * columns), bf16)
    turned_prior = out((2, channels, rows * columns), bf16)
    held = lambda a: pltpu.VMEM(a.shape, a.dtype)
    two = out((2, ext) + frame, bf16)
    feature, late, xt, ft = call(
        own_features,
        "own_features",
        [out((frames, ext) + frame, bf16)],
        (x, before, after, spatial_kernel),
        [weight, held(turned_x), held(turned_own), dma(3)],
        conv * frames * ext,
        far_outs=[two, turned_x, turned_own],
    )
    peers = time_devices * height_devices
    mixed, payload, ft_prior = call(
        mixed_and_sums,
        "mixed_and_sums",
        [out((frames, ext) + frame, f32), out((2 * peers, channels), f32)],
        (feature, prev, spatial_kernel, temporal_kernel),
        [weight, held(two), held(turned_prior), dma(1)],
        conv * frames * ext,
        far_outs=[turned_prior],
    )
    share = ("tm", "height")
    got = lax.all_to_all(payload, share, 0, 0, tiled=True)
    (mixed_next,) = call(
        next_frames,
        "next_frames",
        [out((2, ext) + frame, f32)],
        (),
        [
            weight,
            held(two),
            pltpu.VMEM((2, rows + 4) + frame, bf16),
            held(two),
            held(spatial_kernel),
            held(temporal_kernel),
            dma(4),
        ],
        conv * 2 * ext,
        far=(following, late, spatial_kernel, temporal_kernel),
    )
    stats, payload, parts = call(
        functools.partial(statistics_and_sums, time_devices, height_devices, per_frame),
        "statistics_and_sums",
        [
            out((2 * frames * time_devices, channels), f32),
            out((2 * peers, channels), f32),
            out((16, channels), f32),
        ],
        (got, mixed, cot, gain, shift),
        limit=NARROW,
    )
    got = lax.all_to_all(payload, share, 0, 0, tiled=True)
    scaled_shape = out((frames + 2, ext) + frame, f32)
    outputs, scaled = call(
        functools.partial(outputs_and_grads, time_devices),
        "outputs_and_grads",
        [out((frames, rows) + frame, bf16)],
        (stats, mixed, mixed_next, x, cot, gain, shift),
        [
            held(scaled_shape),
            pltpu.VMEM((frames, 2) + frame, bf16),
            pltpu.VMEM((frames, 2) + frame, bf16),
            pltpu.VMEM((2, rows + 4) + frame, bf16),
            dma(3),
            dma(frames + 2),
        ],
        far=(before, after, following),
        far_outs=[scaled_shape],
    )
    ends = ("rep", "height")
    pieces = reps * height_devices
    own_two = out((frames, ext) + frame, bf16)
    partial, feature_grad = call(
        functools.partial(parameter_grads, time_devices, height_devices, per_frame),
        "parameter_grads",
        [out((pieces, 12 * TILE // pieces + 8, channels), bf16)],
        (got, stats, parts),
        [
            pltpu.VMEM((2 * frames * time_devices, channels), f32),
            pltpu.VMEM((frames + 2, ext) + frame, bf16),
            held(own_two),
            held(scaled_shape),
            held(scaled_shape),
            held(turned_x),
            pltpu.VMEM((frames + 2, channels, rows * columns), bf16),
            held(temporal_kernel),
            dma(7),
            dma(frames),
        ],
        conv * frames * rows * 2,
        far=(mixed, mixed_next, scaled, xt, ft, ft_prior, temporal_kernel),
        far_outs=[own_two],
    )
    partial = lax.all_to_all(partial, ends, 0, 0, tiled=True)
    (grad_inputs,) = call(
        input_grads,
        "input_grads",
        [out((frames, rows) + frame, bf16)],
        (feature_grad, cot, spatial_kernel),
        [weight],
        conv * frames * rows,
    )
    piece = partial.shape[1:]
    (partial,) = call(sum_and_copy, "sum_first", [out((time_devices,) + piece, bf16)], (partial,), limit=NARROW)
    partial = lax.all_to_all(partial, "tm", 0, 0, tiled=True)
    (partial,) = call(sum_and_copy, "sum_second", [out((pieces,) + piece, bf16)], (partial,), limit=NARROW)
    sums = lax.all_to_all(partial, ends, 0, 0, tiled=True)
    pixel_total = reps * frames * time_devices * rows * height_devices * columns
    spatial_sum, temporal_sum, gain_sum, shift_sum = call(
        functools.partial(finish, 1.0 / math.sqrt(pixel_total)),
        "finish",
        [
            out(spatial_kernel.shape, f32),
            out(temporal_kernel.shape, f32),
            out((1, channels), f32),
            out((1, channels), f32),
        ],
        (sums,),
        limit=NARROW,
    )
    return (
        outputs[None],
        grad_inputs[None],
        spatial_sum,
        temporal_sum,
        gain_sum[0],
        shift_sum[0],
    )


def solution(mesh):
    in_specs = (
        P("rep", "tm", "height", None, None),
        P(),
        P(),
        P(),
        P(),
        P("rep", "tm", "height", None, None),
    )
    out_specs = (
        P("rep", "tm", "height", None, None),
        P("rep", "tm", "height", None, None),
        P(),
        P(),
        P(),
        P(),
    )
    return jax.shard_map(shards, mesh=mesh, in_specs=in_specs, out_specs=out_specs, check_vma=False)
```

```python
import functools
import math

import jax
import jax.numpy as jnp
from jax import lax
from jax.experimental import pallas as pl
from jax.experimental.pallas import tpu as pltpu
from jax.sharding import PartitionSpec as P

GROUPS = 32


EPS = 1e-05
TILE = 128
WIDE, NARROW = 58, 16


def iota(shape, dim):
    return lax.broadcasted_iota(jnp.int32, shape, dim)


def exact_dot(a, b):
    return lax.dot_general(
        a,
        b,
        (((1,), (0,)), ((), ())),
        precision=lax.Precision.HIGHEST,
        preferred_element_type=jnp.float32,
    )


def dot(a, b, turned=False):
    return lax.dot_general(
        a,
        b,
        (((1,), (1 if turned else 0,)), ((), ())),
        preferred_element_type=jnp.float32,
    )


def group_matrix(size):
    return (iota((TILE, TILE), 0) // size == iota((TILE, TILE), 1) // size).astype(jnp.float32)


def per_device_sums(got, time_devices, height_devices, earlier):
    shape = (2 * time_devices, got.shape[0])
    row, col = iota(shape, 0), iota(shape, 1)
    at, source = row % time_devices, col // (2 * height_devices)
    keep = (source < at) if earlier else (source == at)
    keep = keep & (row // time_devices == col % 2)
    return exact_dot(keep.astype(jnp.float32), got)


def moved(value, step, columns):
    pixels = value.shape[0]
    rolled = pltpu.roll(value, step % pixels, 0)
    place = iota(value.shape, 0) % columns
    edge = 0 if step > 0 else columns - 1
    return jnp.where(place == edge, 0.0, rolled)


def three_rows(block, rows, columns):
    size = rows * columns
    return jnp.concatenate(
        [block[i * columns : i * columns + size] for i in range(3)], axis=1
    )


def convolve(block, weight, rows, columns, turned):
    taps = dot(three_rows(block, rows, columns), weight, turned)
    c = taps.shape[1] // 3
    sign = -1 if turned else 1
    return (
        taps[:, c : 2 * c]
        + moved(taps[:, :c], sign, columns)
        + moved(taps[:, 2 * c :], -sign, columns)
    )


def flat(value):
    return value.reshape(-1, value.shape[-1])


def put_weight(weight_ref, spatial_ref):
    for i in range(3):
        for j in range(3):
            weight_ref[i * TILE : (i + 1) * TILE, j * TILE : (j + 1) * TILE] = spatial_ref[i, j]


def put_payload(out_ref, firsts, seconds):
    frames = len(firsts)
    sums = exact_dot(jnp.concatenate(firsts + seconds, 0), group_matrix(frames))
    lane = iota((1, TILE), 1) % frames
    rows = []
    for start in (0, frames):
        line = jnp.zeros((1, TILE), jnp.float32)
        for f in range(frames):
            line = jnp.where(lane == f, sums[start + f : start + f + 1], line)
        rows.append(line)
    line = jnp.where(iota((8, TILE), 0) % 2 == 0, rows[0], rows[1])
    for i in range(out_ref.shape[0] // 8):
        out_ref[i * 8 : (i + 1) * 8] = line


def fetch(pairs, sems):
    copies = [pltpu.make_async_copy(a, b, sems.at[i]) for i, (a, b) in enumerate(pairs)]
    for copy in copies:
        copy.start()
    return copies


def turned(value):
    return value.astype(jnp.float32).T.astype(jnp.bfloat16)


def own_features(
    x_ref, before_ref, after_ref, spatial_ref, feature_ref, far_ref, weight_ref, sems
):
    put_weight(weight_ref, spatial_ref)
    frames, rows, columns, _ = x_ref.shape

    def one(f, _):
        block = jnp.concatenate([flat(before_ref[f]), flat(x_ref[f]), flat(after_ref[f])], 0)
        out = convolve(block, weight_ref[...], rows + 2, columns, False)
        feature_ref[f] = out.astype(jnp.bfloat16).reshape(feature_ref.shape[1:])
        return 0

    lax.fori_loop(0, frames, one, 0)
    for copy in fetch([(feature_ref, far_ref)], sems):
        copy.wait()


def turn(
    x_ref,
    before_ref,
    after_ref,
    prev_ref,
    feature_ref,
    spatial_ref,
    xt_ref,
    ft_ref,
    weight_ref,
    prior_ref,
):
    put_weight(weight_ref, spatial_ref)
    frames, rows, columns, _ = x_ref.shape
    size = rows * columns

    def one(f, _):
        out = convolve(flat(prev_ref[f]), weight_ref[...], rows + 2, columns, False)
        prior_ref[f] = out.astype(jnp.bfloat16).reshape(prior_ref.shape[1:])
        return 0

    lax.fori_loop(0, 2, one, 0)
    for f in range(frames + 2):
        seen = prior_ref[f, 1 : rows + 1] if f < 2 else feature_ref[f - 2, 1 : rows + 1]
        ft_ref[:, f * size : (f + 1) * size] = turned(flat(seen))
    for f in range(frames):
        block = jnp.concatenate(
            [flat(before_ref[f, 1:]), flat(x_ref[f]), flat(after_ref[f, :1])], 0
        )
        xt_ref[:, f * size : (f + 1) * size] = turned(three_rows(block, rows, columns))


def mix(blocks, temporal_ref):
    return dot(jnp.concatenate(blocks, axis=1), flat(temporal_ref[...]))


def mixed_and_sums(
    feature_ref,
    prev_ref,
    spatial_ref,
    temporal_ref,
    mixed_ref,
    out_ref,
    weight_ref,
    prior_ref,
):
    put_weight(weight_ref, spatial_ref)
    frames, rows, columns, _ = mixed_ref.shape

    def one(f, _):
        out = convolve(flat(prev_ref[f]), weight_ref[...], rows, columns, False)
        prior_ref[f] = out.astype(jnp.bfloat16).reshape(prior_ref.shape[1:])
        return 0

    lax.fori_loop(0, 2, one, 0)
    firsts, seconds = [], []
    for f in range(frames):
        blocks = [
            flat(prior_ref[f + k]) if f + k < 2 else flat(feature_ref[f + k - 2]) for k in range(3)
        ]
        out = mix(blocks, temporal_ref)
        mixed_ref[f] = out.reshape(mixed_ref.shape[1:])
        inner = out[columns : (rows - 1) * columns]
        firsts.append(inner.sum(0, keepdims=True))
        seconds.append((inner * inner).sum(0, keepdims=True))
    put_payload(out_ref, firsts, seconds)


def next_frames(
    next_hbm,
    late_hbm,
    spatial_hbm,
    temporal_hbm,
    mixed_ref,
    weight_ref,
    held_ref,
    next_ref,
    late_ref,
    spatial_ref,
    temporal_ref,
    sems,
):
    copies = fetch(
        [
            (spatial_hbm, spatial_ref),
            (next_hbm.at[pl.ds(0, 2)], next_ref),
            (late_hbm.at[pl.ds(late_hbm.shape[0] - 2, 2)], late_ref),
            (temporal_hbm, temporal_ref),
        ],
        sems,
    )
    _, ext, columns, _ = mixed_ref.shape
    copies[0].wait()
    put_weight(weight_ref, spatial_ref)
    copies[1].wait()

    def one(f, _):
        out = convolve(flat(next_ref[f]), weight_ref[...], ext, columns, False)
        held_ref[f] = out.astype(jnp.bfloat16).reshape(held_ref.shape[1:])
        return 0

    lax.fori_loop(0, 2, one, 0)
    copies[2].wait()
    copies[3].wait()
    for f in range(2):
        blocks = [flat(late_ref[f + k]) if f + k < 2 else flat(held_ref[f + k - 2]) for k in range(3)]
        mixed_ref[f] = mix(blocks, temporal_ref).reshape(mixed_ref.shape[1:])


def counts(f, frames, time_devices, per_frame):
    at = iota((time_devices, TILE), 0) * frames + (f + 1)
    return at.astype(jnp.float32) * per_frame


def statistics_and_sums(
    time_devices,
    height_devices,
    per_frame,
    got_ref,
    mixed_ref,
    cot_ref,
    gain_ref,
    shift_ref,
    stats_ref,
    out_ref,
):
    frames, rows, _, _ = cot_ref.shape
    me = lax.axis_index("tm")
    got = got_ref[...]
    here = per_device_sums(got, time_devices, height_devices, False)
    earlier = per_device_sums(got, time_devices, height_devices, True)
    group = group_matrix(frames)
    lane = iota(here.shape, 1) % frames
    for f in range(frames):
        sums = exact_dot(earlier + jnp.where(lane <= f, here, 0.0), group)
        count = counts(f, frames, time_devices, per_frame)
        mean = sums[:time_devices] / count
        variance = sums[time_devices:] / count - mean * mean
        at = 2 * f * time_devices
        stats_ref[at : at + time_devices] = mean
        stats_ref[at + time_devices : at + 2 * time_devices] = lax.rsqrt(variance + EPS)
    gain, shift = gain_ref[...], shift_ref[...]
    step = 4
    firsts, seconds = [], []
    for f in range(frames):
        mean = stats_ref[pl.ds(2 * f * time_devices + me, 1)]
        inv_std = stats_ref[pl.ds((2 * f + 1) * time_devices + me, 1)]

        def some(i, sums, f=f, mean=mean, inv_std=inv_std):
            normed = (flat(mixed_ref[f, pl.ds(1 + i * step, step)]) - mean) * inv_std
            pre = normed * gain + shift
            sigma = 1.0 / (1.0 + jnp.exp(-pre))
            cot = flat(cot_ref[f, pl.ds(i * step, step)]).astype(jnp.float32)
            grad = cot * (sigma * (1.0 + pre * (1.0 - sigma)))
            split = (-1, 8, TILE)
            return (
                sums[0] + grad.reshape(split).sum(0),
                sums[1] + (grad * normed).reshape(split).sum(0),
            )

        zero = jnp.zeros((8, TILE), jnp.float32)
        a, b = lax.fori_loop(0, rows // step, some, (zero, zero), unroll=2)
        firsts.append(a.sum(0, keepdims=True))
        seconds.append(b.sum(0, keepdims=True))
    put_payload(out_ref, [a * gain for a in firsts], [b * gain for b in seconds])
    total_a, total_b = sum(firsts[1:], firsts[0]), sum(seconds[1:], seconds[0])
    at = 2 * frames * time_devices
    stats_ref[at : at + 16] = jnp.where(iota((16, TILE), 0) < 8, total_b, total_a)


def outputs_and_grads(
    time_devices,
    stats_ref,
    mixed_ref,
    mixed_next_ref,
    x_ref,
    cot_ref,
    gain_ref,
    shift_ref,
    before_hbm,
    after_hbm,
    next_hbm,
    outputs_ref,
    scaled_hbm,
    scaled_ref,
    before_ref,
    after_ref,
    next_ref,
    in_sems,
    out_sems,
):
    frames, rows, columns, _ = cot_ref.shape
    copies = fetch(
        [
            (before_hbm.at[pl.ds(frames, frames)], before_ref),
            (after_hbm.at[pl.ds(frames, frames)], after_ref),
            (next_hbm.at[pl.ds(2, 2)], next_ref),
        ],
        in_sems,
    )
    me = lax.axis_index("tm")
    following = jnp.minimum(me + 1, time_devices - 1)
    gain, shift = gain_ref[...], shift_ref[...]
    step = 4

    def grads(mixed, cot, mean, inv_std):
        pre = (mixed - mean) * inv_std * gain + shift
        sigma = 1.0 / (1.0 + jnp.exp(-pre))
        grad = cot.astype(jnp.float32) * (sigma * (1.0 + pre * (1.0 - sigma)))
        return pre * sigma, inv_std * (grad * gain)

    leaving = []

    for f in range(frames + 2):
        own = f < frames
        at, g = (me, f) if own else (following, f - frames)
        mean = stats_ref[pl.ds(2 * g * time_devices + at, 1)]
        inv_std = stats_ref[pl.ds((2 * g + 1) * time_devices + at, 1)]
        source = mixed_ref if own else mixed_next_ref

        def edge(row, cot, f=f, g=g, mean=mean, inv_std=inv_std, source=source):
            _, scaled = grads(source[g, row], cot, mean, inv_std)
            scaled_ref[f, row] = scaled


        if f == frames:
            copies[2].wait()

        def some(i, _, f=f, g=g, own=own, mean=mean, inv_std=inv_std, source=source):
            here = pl.ds(1 + i * step, step)
            cot = cot_ref[g, pl.ds(i * step, step)] if own else next_ref[g, pl.ds(2 + i * step, step)]
            silu, scaled = grads(flat(source[g, here]), flat(cot), mean, inv_std)
            scaled_ref[f, here] = scaled.reshape(step, columns, TILE)
            if own:
                kept = flat(x_ref[g, pl.ds(i * step, step)]).astype(jnp.float32) + silu
                outputs_ref[g, pl.ds(i * step, step)] = kept.astype(jnp.bfloat16).reshape(
                    step, columns, TILE
                )
            return 0

        lax.fori_loop(0, rows // step, some, 0, unroll=2)
        if f == 0:
            copies[0].wait()
            copies[1].wait()
        edge(0, before_ref[g, 1] if own else next_ref[g, 1])
        edge(rows + 1, after_ref[g, 0] if own else next_ref[g, rows + 2])
        copy = pltpu.make_async_copy(scaled_ref.at[f], scaled_hbm.at[f], out_sems.at[f])
        copy.start()
        leaving.append(copy)
    for copy in leaving:
        copy.wait()


def parameter_grads(
    time_devices,
    height_devices,
    per_frame,
    got_ref,
    stats_ref,
    mixed_hbm,
    mixed_next_hbm,
    scaled_hbm,
    xt_hbm,
    ft_hbm,
    temporal_hbm,
    out_ref,
    feature_grad_hbm,
    carry_ref,
    mixed_grad_ref,
    feature_grad_ref,
    mixed_ref,
    scaled_ref,
    xt_ref,
    ft_ref,
    temporal_ref,
    shifted_ref,
    sems,
    out_sems,
):
    frames, ext, columns, _ = feature_grad_ref.shape
    rows = ext - 2
    copies = fetch(
        [
            (mixed_hbm, mixed_ref.at[pl.ds(0, frames)]),
            (mixed_next_hbm, mixed_ref.at[pl.ds(frames, 2)]),
            (scaled_hbm, scaled_ref),
            (temporal_hbm, temporal_ref),
            (xt_hbm, xt_ref),
            (ft_hbm, ft_ref),
        ],
        sems,
    )
    me, level = lax.axis_index("tm"), lax.axis_index("height")
    following = jnp.minimum(me + 1, time_devices - 1)
    here = per_device_sums(got_ref[...], time_devices, height_devices, False)
    group = group_matrix(frames)
    lane = iota(here.shape, 1) % frames
    firsts, seconds = [], []
    for f in range(frames):
        sums = exact_dot(jnp.where(lane == f, here, 0.0), group)
        sum_a, sum_b = sums[:time_devices], sums[time_devices:]
        at = 2 * f * time_devices
        mean = stats_ref[at : at + time_devices]
        inv_std = stats_ref[at + time_devices : at + 2 * time_devices]
        count = counts(f, frames, time_devices, per_frame)
        firsts.append((-inv_std * sum_a + inv_std * inv_std * sum_b * mean) / count)
        seconds.append(-inv_std * inv_std * sum_b / (2.0 * count))
    square = (time_devices, time_devices)
    later = (iota(square, 1) > iota(square, 0)).astype(jnp.float32)
    for kind, values in enumerate((firsts, seconds)):
        run = exact_dot(later, sum(values[1:], values[0]))
        for f in range(frames - 1, -1, -1):
            run = run + values[f]
            at = (2 * f + kind) * time_devices
            carry_ref[at : at + time_devices] = run
    for copy in copies[:3]:
        copy.wait()
    exists = (me < time_devices - 1).astype(jnp.float32)
    for f in range(frames + 2):
        own = f < frames
        at, g = (me, f) if own else (following, f - frames)
        first = carry_ref[pl.ds(2 * g * time_devices + at, 1)]
        second = 2.0 * carry_ref[pl.ds((2 * g + 1) * time_devices + at, 1)]

        def some(i, _, f=f, own=own, first=first, second=second):
            at = pl.ds(i * 3, 3)
            grad = flat(scaled_ref[f, at]) + first + flat(mixed_ref[f, at]) * second
            if not own:
                grad = grad * exists
            mixed_grad_ref[f, at] = grad.astype(jnp.bfloat16).reshape(3, columns, TILE)
            return 0

        lax.fori_loop(0, ext // 3, some, 0, unroll=3)
    copies[3].wait()
    back = jnp.concatenate([temporal_ref[k] for k in range(3)], axis=1)
    leaving = []
    place = iota((ext * columns, TILE), 0) // columns
    outside = ((place == 0) & (level == 0)) | ((place == ext - 1) & (level == height_devices - 1))
    size = rows * columns
    for f in range(frames):
        blocks = [flat(mixed_grad_ref[f + 2 - k]) for k in range(3)]
        grad = dot(jnp.concatenate(blocks, axis=1), back, True)
        grad = jnp.where(outside, 0.0, grad).astype(jnp.bfloat16)
        feature_grad_ref[f] = grad.reshape(ext, columns, TILE)
        copy = pltpu.make_async_copy(
            feature_grad_ref.at[f], feature_grad_hbm.at[f], out_sems.at[f]
        )
        copy.start()
        leaving.append(copy)
        inner = grad[columns : (rows + 1) * columns]
        wide = inner.astype(jnp.float32)
        shifted_ref[f * size : (f + 1) * size] = jnp.concatenate(
            [
                moved(wide, -1, columns).astype(jnp.bfloat16),
                inner,
                moved(wide, 1, columns).astype(jnp.bfloat16),
            ],
            axis=1,
        )
    for copy in copies[4:]:
        copy.wait()
    inner = flat(mixed_grad_ref[:frames, 1 : rows + 1])
    temporal = [dot(ft_ref[:, k * size : (k + frames) * size], inner) for k in range(3)]
    spatial = dot(xt_ref[...], shifted_ref[...])
    pieces = out_ref.shape[0]
    piece = 12 * TILE // pieces
    blocks = [spatial[:, j * TILE : (j + 1) * TILE] for j in range(3)] + temporal
    whole = jnp.concatenate(blocks, axis=0).astype(jnp.bfloat16)
    for p in range(pieces):
        out_ref[p, :piece] = whole[p * piece : (p + 1) * piece]
        at = 2 * frames * time_devices + 8 * min(p, 1)
        tail = stats_ref[at : at + 8]
        tail = jnp.where((iota((8, TILE), 0) == 0) & (p < 2), tail, 0.0)
        out_ref[p, piece : piece + 8] = tail.astype(jnp.bfloat16)
    for copy in leaving:
        copy.wait()


def input_grads(grad_ref, cot_ref, spatial_ref, out_ref, weight_ref):
    frames, rows, columns, _ = cot_ref.shape
    for s in range(3):
        for j in range(3):
            weight_ref[j * TILE : (j + 1) * TILE, s * TILE : (s + 1) * TILE] = spatial_ref[2 - s, j]

    def one(f, _):
        out = convolve(flat(grad_ref[f]), weight_ref[...], rows, columns, True)
        out = out + flat(cot_ref[f]).astype(jnp.float32)
        out_ref[f] = out.astype(jnp.bfloat16).reshape(out_ref.shape[1:])
        return 0

    lax.fori_loop(0, frames, one, 0)


def sum_and_copy(got_ref, out_ref):
    total = got_ref[0].astype(jnp.float32)
    for i in range(1, got_ref.shape[0]):
        total = total + got_ref[i].astype(jnp.float32)
    total = total.astype(jnp.bfloat16)
    for i in range(out_ref.shape[0]):
        out_ref[i] = total


def finish(scale, got_ref, spatial_ref, temporal_ref, gain_ref, shift_ref):
    pieces, piece = got_ref.shape[0], got_ref.shape[1] - 8
    for p in range(pieces):
        value = got_ref[p].astype(jnp.float32) * scale
        if p < 2:
            (gain_ref, shift_ref)[p][...] = value[piece : piece + 1]
        at = p * piece
        while at < (p + 1) * piece:
            block, row = at // TILE, at % TILE
            size = min(TILE - row, (p + 1) * piece - at)
            part = value[at - p * piece : at - p * piece + size]
            if block < 9:
                spatial_ref[block % 3, block // 3, row : row + size] = part
            else:
                temporal_ref[block - 9, row : row + size] = part
            at += size


def call(body, outs, args, scratch=(), flops=0, far=(), far_outs=(), limit=WIDE):
    everything = (*args, *far, *outs, *far_outs)
    moved_bytes = sum(a.size * a.dtype.itemsize for a in everything)
    near, away = pl.BlockSpec(memory_space=pltpu.VMEM), pl.BlockSpec(memory_space=pl.ANY)
    return pl.pallas_call(
        body,
        out_shape=[*outs, *far_outs],
        in_specs=[near] * len(args) + [away] * len(far),
        out_specs=[near] * len(outs) + [away] * len(far_outs),
        scratch_shapes=list(scratch),
        compiler_params=pltpu.CompilerParams(vmem_limit_bytes=limit * 1024 * 1024),
        cost_estimate=pl.CostEstimate(
            flops=flops, bytes_accessed=moved_bytes, transcendentals=0
        ),
    )(*args, *far)


def shards(inputs, spatial_kernel, temporal_kernel, norm_gain, norm_shift, cotangent):
    x, cot = inputs[0], cotangent[0]
    frames, rows, columns, channels = x.shape
    ext = rows + 2
    reps, time_devices, height_devices = (lax.axis_size(a) for a in ("rep", "tm", "height"))
    per_frame = float(rows * height_devices * columns * (channels // GROUPS))
    bf16, f32 = jnp.bfloat16, jnp.float32
    out = jax.ShapeDtypeStruct
    frame = (columns, channels)
    gain, shift = norm_gain[None], norm_shift[None]
    weight = pltpu.VMEM((3 * channels, 3 * channels), bf16)
    conv = 2 * 9 * channels * channels * columns

    up = [(i, i + 1) for i in range(height_devices - 1)]
    down = [(j, i) for i, j in up]
    before = lax.ppermute(jnp.concatenate([x[:, rows - 2 :], cot[:, rows - 2 :]], 0), "height", up)
    after = lax.ppermute(jnp.concatenate([x[:, :2], cot[:, :2]], 0), "height", down)
    onward = [(i, i + 1) for i in range(time_devices - 1)]
    back = [(j, i) for i, j in onward]
    last = jnp.concatenate([before[2:4], x[2:4], after[2:4]], 1)
    prev = lax.ppermute(last, "tm", onward)
    first = jnp.concatenate(
        [
            jnp.concatenate([before[:2], before[4:6]], 0),
            jnp.concatenate([x[:2], cot[:2]], 0),
            jnp.concatenate([after[:2], after[4:6]], 0),
        ],
        1,
    )
    following = lax.ppermute(first, "tm", back)

    dma = lambda count: pltpu.SemaphoreType.DMA((count,))
    turned_x = out((3 * channels, frames * rows * columns), bf16)
    turned_features = out((channels, (frames + 2) * rows * columns), bf16)
    held = lambda a: pltpu.VMEM(a.shape, a.dtype)
    two = out((2, ext) + frame, bf16)
    own_two = out((frames, ext) + frame, bf16)
    feature, late = call(
        own_features,
        [own_two],
        (x, before, after, spatial_kernel),
        [weight, dma(1)],
        conv * frames * ext,
        far_outs=[own_two],
        limit=NARROW,
    )
    peers = time_devices * height_devices
    mixed, payload = call(
        mixed_and_sums,
        [out((frames, ext) + frame, f32), out((2 * peers, channels), f32)],
        (feature, prev, spatial_kernel, temporal_kernel),
        [weight, held(two)],
        conv * frames * ext,
        limit=NARROW,
    )
    share = ("tm", "height")
    got = lax.all_to_all(payload, share, 0, 0, tiled=True)
    xt, ft = call(
        turn,
        [turned_x, turned_features],
        (x, before, after, prev, late, spatial_kernel),
        [weight, held(two)],
        conv * frames * ext,
    )
    (mixed_next,) = call(
        next_frames,
        [out((2, ext) + frame, f32)],
        (),
        [
            weight,
            held(two),
            pltpu.VMEM((2, rows + 4) + frame, bf16),
            held(two),
            held(spatial_kernel),
            held(temporal_kernel),
            dma(4),
        ],
        conv * 2 * ext,
        far=(following, late, spatial_kernel, temporal_kernel),
    )
    stats, payload = call(
        functools.partial(statistics_and_sums, time_devices, height_devices, per_frame),
        [
            out((2 * frames * time_devices + 16, channels), f32),
            out((2 * peers, channels), f32),
        ],
        (got, mixed, cot, gain, shift),
        limit=NARROW,
    )
    got = lax.all_to_all(payload, share, 0, 0, tiled=True)
    scaled_shape = out((frames + 2, ext) + frame, f32)
    outputs, scaled = call(
        functools.partial(outputs_and_grads, time_devices),
        [out((frames, rows) + frame, bf16)],
        (stats, mixed, mixed_next, x, cot, gain, shift),
        [
            held(scaled_shape),
            pltpu.VMEM((frames, 2) + frame, bf16),
            pltpu.VMEM((frames, 2) + frame, bf16),
            pltpu.VMEM((2, rows + 4) + frame, bf16),
            dma(3),
            dma(frames + 2),
        ],
        far=(before, after, following),
        far_outs=[scaled_shape],
    )
    ends = ("rep", "height")
    pieces = reps * height_devices
    partial, feature_grad = call(
        functools.partial(parameter_grads, time_devices, height_devices, per_frame),
        [out((pieces, 12 * TILE // pieces + 8, channels), bf16)],
        (got, stats),
        [
            pltpu.VMEM((2 * frames * time_devices, channels), f32),
            pltpu.VMEM((frames + 2, ext) + frame, bf16),
            held(own_two),
            held(scaled_shape),
            held(scaled_shape),
            held(turned_x),
            held(turned_features),
            held(temporal_kernel),
            pltpu.VMEM((frames * rows * columns, 3 * channels), bf16),
            dma(6),
            dma(frames),
        ],
        conv * frames * rows * 2,
        far=(mixed, mixed_next, scaled, xt, ft, temporal_kernel),
        far_outs=[own_two],
    )
    partial = lax.all_to_all(partial, ends, 0, 0, tiled=True)
    (grad_inputs,) = call(
        input_grads,
        [out((frames, rows) + frame, bf16)],
        (feature_grad, cot, spatial_kernel),
        [weight],
        conv * frames * rows,
    )
    piece = partial.shape[1:]
    (partial,) = call(sum_and_copy, [out((time_devices,) + piece, bf16)], (partial,), limit=NARROW)
    partial = lax.all_to_all(partial, "tm", 0, 0, tiled=True)
    (partial,) = call(sum_and_copy, [out((pieces,) + piece, bf16)], (partial,), limit=NARROW)
    sums = lax.all_to_all(partial, ends, 0, 0, tiled=True)
    pixel_total = reps * frames * time_devices * rows * height_devices * columns
    spatial_sum, temporal_sum, gain_sum, shift_sum = call(
        functools.partial(finish, 1.0 / math.sqrt(pixel_total)),
        [
            out(spatial_kernel.shape, f32),
            out(temporal_kernel.shape, f32),
            out((1, channels), f32),
            out((1, channels), f32),
        ],
        (sums,),
        limit=NARROW,
    )
    return (
        outputs[None],
        grad_inputs[None],
        spatial_sum,
        temporal_sum,
        gain_sum[0],
        shift_sum[0],
    )


def solution(mesh):
    in_specs = (
        P("rep", "tm", "height", None, None),
        P(),
        P(),
        P(),
        P(),
        P("rep", "tm", "height", None, None),
    )
    out_specs = (
        P("rep", "tm", "height", None, None),
        P("rep", "tm", "height", None, None),
        P(),
        P(),
        P(),
        P(),
    )
    return jax.shard_map(shards, mesh=mesh, in_specs=in_specs, out_specs=out_specs, check_vma=False)
```

```python
import functools
import math

import jax
import jax.numpy as jnp
from jax import lax
from jax.experimental import pallas as pl
from jax.experimental.pallas import tpu as pltpu
from jax.sharding import PartitionSpec as P

GROUPS = 32


EPS = 1e-05
TILE = 128
WIDE, NARROW = 58, 16


def iota(shape, dim):
    return lax.broadcasted_iota(jnp.int32, shape, dim)


def exact_dot(a, b):
    return lax.dot_general(
        a,
        b,
        (((1,), (0,)), ((), ())),
        precision=lax.Precision.HIGHEST,
        preferred_element_type=jnp.float32,
    )


def dot(a, b, turned=False):
    return lax.dot_general(
        a,
        b,
        (((1,), (1 if turned else 0,)), ((), ())),
        preferred_element_type=jnp.float32,
    )


def group_matrix(size):
    return (iota((TILE, TILE), 0) // size == iota((TILE, TILE), 1) // size).astype(jnp.float32)


def per_device_sums(got, time_devices, height_devices, earlier):
    shape = (2 * time_devices, got.shape[0])
    row, col = iota(shape, 0), iota(shape, 1)
    at, source = row % time_devices, col // (2 * height_devices)
    keep = (source < at) if earlier else (source == at)
    keep = keep & (row // time_devices == col % 2)
    return exact_dot(keep.astype(jnp.float32), got)


def moved(value, step, columns):
    pixels = value.shape[0]
    rolled = pltpu.roll(value, step % pixels, 0)
    place = iota(value.shape, 0) % columns
    edge = 0 if step > 0 else columns - 1
    return jnp.where(place == edge, 0.0, rolled)


def three_rows(block, rows, columns):
    size = rows * columns
    return jnp.concatenate(
        [block[i * columns : i * columns + size] for i in range(3)], axis=1
    )


def convolve(block, weight, rows, columns, turned):
    taps = dot(three_rows(block, rows, columns), weight, turned)
    c = taps.shape[1] // 3
    sign = -1 if turned else 1
    return (
        taps[:, c : 2 * c]
        + moved(taps[:, :c], sign, columns)
        + moved(taps[:, 2 * c :], -sign, columns)
    )


def flat(value):
    return value.reshape(-1, value.shape[-1])


def put_weight(weight_ref, spatial_ref):
    for i in range(3):
        for j in range(3):
            weight_ref[i * TILE : (i + 1) * TILE, j * TILE : (j + 1) * TILE] = spatial_ref[i, j]


def put_payload(out_ref, firsts, seconds):
    frames = len(firsts)
    sums = exact_dot(jnp.concatenate(firsts + seconds, 0), group_matrix(frames))
    lane = iota((1, TILE), 1) % frames
    rows = []
    for start in (0, frames):
        line = jnp.zeros((1, TILE), jnp.float32)
        for f in range(frames):
            line = jnp.where(lane == f, sums[start + f : start + f + 1], line)
        rows.append(line)
    line = jnp.where(iota((8, TILE), 0) % 2 == 0, rows[0], rows[1])
    for i in range(out_ref.shape[0] // 8):
        out_ref[i * 8 : (i + 1) * 8] = line


def fetch(pairs, sems):
    copies = [pltpu.make_async_copy(a, b, sems.at[i]) for i, (a, b) in enumerate(pairs)]
    for copy in copies:
        copy.start()
    return copies


def turned(value):
    return value.astype(jnp.float32).T.astype(jnp.bfloat16)


def joined(before_ref, main_ref, after_ref, f):
    return jnp.concatenate([flat(before_ref[f]), flat(main_ref[f]), flat(after_ref[f])], 0)


def own_features(
    x_ref, before_ref, after_ref, spatial_ref, feature_ref, far_ref, weight_ref, sems
):
    put_weight(weight_ref, spatial_ref)
    frames, rows, columns, _ = x_ref.shape

    def one(f, _):
        block = jnp.concatenate([flat(before_ref[f]), flat(x_ref[f]), flat(after_ref[f])], 0)
        out = convolve(block, weight_ref[...], rows + 2, columns, False)
        feature_ref[f] = out.astype(jnp.bfloat16).reshape(feature_ref.shape[1:])
        return 0

    lax.fori_loop(0, frames, one, 0)
    for copy in fetch([(feature_ref, far_ref)], sems):
        copy.wait()


def turn(
    x_ref,
    before_ref,
    after_ref,
    prev_ref,
    prev_before_ref,
    prev_after_ref,
    feature_ref,
    spatial_ref,
    xt_ref,
    ft_ref,
    weight_ref,
    prior_ref,
):
    put_weight(weight_ref, spatial_ref)
    frames, rows, columns, _ = x_ref.shape
    size = rows * columns

    def one(f, _):
        block = joined(prev_before_ref, prev_ref, prev_after_ref, f)
        out = convolve(block, weight_ref[...], rows + 2, columns, False)
        prior_ref[f] = out.astype(jnp.bfloat16).reshape(prior_ref.shape[1:])
        return 0

    lax.fori_loop(0, 2, one, 0)
    for f in range(frames + 2):
        seen = prior_ref[f, 1 : rows + 1] if f < 2 else feature_ref[f - 2, 1 : rows + 1]
        ft_ref[:, f * size : (f + 1) * size] = turned(flat(seen))
    for f in range(frames):
        block = jnp.concatenate(
            [flat(before_ref[f, 1:]), flat(x_ref[f]), flat(after_ref[f, :1])], 0
        )
        xt_ref[:, f * size : (f + 1) * size] = turned(three_rows(block, rows, columns))


def mix(blocks, temporal_ref):
    return dot(jnp.concatenate(blocks, axis=1), flat(temporal_ref[...]))


def mixed_and_sums(
    feature_ref,
    prev_ref,
    prev_before_ref,
    prev_after_ref,
    spatial_ref,
    temporal_ref,
    mixed_ref,
    out_ref,
    weight_ref,
    prior_ref,
):
    put_weight(weight_ref, spatial_ref)
    frames, rows, columns, _ = mixed_ref.shape

    def one(f, _):
        block = joined(prev_before_ref, prev_ref, prev_after_ref, f)
        out = convolve(block, weight_ref[...], rows, columns, False)
        prior_ref[f] = out.astype(jnp.bfloat16).reshape(prior_ref.shape[1:])
        return 0

    lax.fori_loop(0, 2, one, 0)
    firsts, seconds = [], []
    for f in range(frames):
        blocks = [
            flat(prior_ref[f + k]) if f + k < 2 else flat(feature_ref[f + k - 2]) for k in range(3)
        ]
        out = mix(blocks, temporal_ref)
        mixed_ref[f] = out.reshape(mixed_ref.shape[1:])
        inner = out[columns : (rows - 1) * columns]
        firsts.append(inner.sum(0, keepdims=True))
        seconds.append((inner * inner).sum(0, keepdims=True))
    put_payload(out_ref, firsts, seconds)


def next_frames(
    next_hbm,
    late_hbm,
    spatial_hbm,
    temporal_hbm,
    mixed_ref,
    weight_ref,
    held_ref,
    next_ref,
    late_ref,
    spatial_ref,
    temporal_ref,
    sems,
):
    copies = fetch(
        [
            (spatial_hbm, spatial_ref),
            (next_hbm.at[pl.ds(0, 2)], next_ref),
            (late_hbm.at[pl.ds(late_hbm.shape[0] - 2, 2)], late_ref),
            (temporal_hbm, temporal_ref),
        ],
        sems,
    )
    _, ext, columns, _ = mixed_ref.shape
    copies[0].wait()
    put_weight(weight_ref, spatial_ref)
    copies[1].wait()

    def one(f, _):
        out = convolve(flat(next_ref[f]), weight_ref[...], ext, columns, False)
        held_ref[f] = out.astype(jnp.bfloat16).reshape(held_ref.shape[1:])
        return 0

    lax.fori_loop(0, 2, one, 0)
    copies[2].wait()
    copies[3].wait()
    for f in range(2):
        blocks = [flat(late_ref[f + k]) if f + k < 2 else flat(held_ref[f + k - 2]) for k in range(3)]
        mixed_ref[f] = mix(blocks, temporal_ref).reshape(mixed_ref.shape[1:])


def counts(f, frames, time_devices, per_frame):
    at = iota((time_devices, TILE), 0) * frames + (f + 1)
    return at.astype(jnp.float32) * per_frame


def statistics_and_sums(
    time_devices,
    height_devices,
    per_frame,
    got_ref,
    mixed_ref,
    cot_ref,
    gain_ref,
    shift_ref,
    stats_ref,
    out_ref,
):
    frames, rows, _, _ = cot_ref.shape
    me = lax.axis_index("tm")
    got = got_ref[...]
    here = per_device_sums(got, time_devices, height_devices, False)
    earlier = per_device_sums(got, time_devices, height_devices, True)
    group = group_matrix(frames)
    lane = iota(here.shape, 1) % frames
    for f in range(frames):
        sums = exact_dot(earlier + jnp.where(lane <= f, here, 0.0), group)
        count = counts(f, frames, time_devices, per_frame)
        mean = sums[:time_devices] / count
        variance = sums[time_devices:] / count - mean * mean
        at = 2 * f * time_devices
        stats_ref[at : at + time_devices] = mean
        stats_ref[at + time_devices : at + 2 * time_devices] = lax.rsqrt(variance + EPS)
    gain, shift = gain_ref[...], shift_ref[...]
    step = 4
    firsts, seconds = [], []
    for f in range(frames):
        mean = stats_ref[pl.ds(2 * f * time_devices + me, 1)]
        inv_std = stats_ref[pl.ds((2 * f + 1) * time_devices + me, 1)]

        def some(i, sums, f=f, mean=mean, inv_std=inv_std):
            normed = (flat(mixed_ref[f, pl.ds(1 + i * step, step)]) - mean) * inv_std
            pre = normed * gain + shift
            sigma = 1.0 / (1.0 + jnp.exp(-pre))
            cot = flat(cot_ref[f, pl.ds(i * step, step)]).astype(jnp.float32)
            grad = cot * (sigma * (1.0 + pre * (1.0 - sigma)))
            split = (-1, 8, TILE)
            return (
                sums[0] + grad.reshape(split).sum(0),
                sums[1] + (grad * normed).reshape(split).sum(0),
            )

        zero = jnp.zeros((8, TILE), jnp.float32)
        a, b = lax.fori_loop(0, rows // step, some, (zero, zero), unroll=2)
        firsts.append(a.sum(0, keepdims=True))
        seconds.append(b.sum(0, keepdims=True))
    put_payload(out_ref, [a * gain for a in firsts], [b * gain for b in seconds])
    total_a, total_b = sum(firsts[1:], firsts[0]), sum(seconds[1:], seconds[0])
    at = 2 * frames * time_devices
    stats_ref[at : at + 16] = jnp.where(iota((16, TILE), 0) < 8, total_b, total_a)


def normalised(mixed, mean, inv_std, gain, shift):
    pre = (mixed - mean) * inv_std * gain + shift
    return pre, 1.0 / (1.0 + jnp.exp(-pre))


def write_outputs(time_devices, stats_ref, mixed_ref, x_ref, gain_ref, shift_ref, outputs_ref):
    frames, rows, columns, _ = x_ref.shape
    me = lax.axis_index("tm")
    gain, shift = gain_ref[...], shift_ref[...]
    step = 4
    for f in range(frames):
        mean = stats_ref[pl.ds(2 * f * time_devices + me, 1)]
        inv_std = stats_ref[pl.ds((2 * f + 1) * time_devices + me, 1)]

        def some(i, _, f=f, mean=mean, inv_std=inv_std):
            at = pl.ds(i * step, step)
            mixed = flat(mixed_ref[f, pl.ds(1 + i * step, step)])
            pre, sigma = normalised(mixed, mean, inv_std, gain, shift)
            kept = flat(x_ref[f, at]).astype(jnp.float32) + pre * sigma
            outputs_ref[f, at] = kept.astype(jnp.bfloat16).reshape(step, columns, TILE)
            return 0

        lax.fori_loop(0, rows // step, some, 0, unroll=2)


def mixed_grads(
    time_devices,
    stats_ref,
    gain_ref,
    shift_ref,
    mixed_hbm,
    mixed_next_hbm,
    cot_hbm,
    before_hbm,
    after_hbm,
    next_hbm,
    scaled_hbm,
    scaled_ref,
    mixed_ref,
    cot_ref,
    before_ref,
    after_ref,
    in_sems,
    out_sems,
):
    frames, rows, columns, _ = cot_hbm.shape
    pairs = [
        (before_hbm.at[pl.ds(frames, frames)], before_ref),
        (after_hbm.at[pl.ds(frames, frames)], after_ref),
    ]
    for f in range(frames + 2):
        own = f < frames
        pairs.append((mixed_hbm.at[f] if own else mixed_next_hbm.at[f - frames], mixed_ref.at[f]))
        if own:
            pairs.append((cot_hbm.at[f], cot_ref.at[f, pl.ds(2, rows)]))
        else:
            pairs.append((next_hbm.at[2 + f - frames], cot_ref.at[f]))
    copies = fetch(pairs, in_sems)
    me = lax.axis_index("tm")
    following = jnp.minimum(me + 1, time_devices - 1)
    gain, shift = gain_ref[...], shift_ref[...]
    step = 4

    def grads(mixed, cot, mean, inv_std):
        pre, sigma = normalised(mixed, mean, inv_std, gain, shift)
        grad = cot.astype(jnp.float32) * (sigma * (1.0 + pre * (1.0 - sigma)))
        return inv_std * (grad * gain)

    leaving = []
    copies[0].wait()
    copies[1].wait()
    for f in range(frames + 2):
        own = f < frames
        at, g = (me, f) if own else (following, f - frames)
        mean = stats_ref[pl.ds(2 * g * time_devices + at, 1)]
        inv_std = stats_ref[pl.ds((2 * g + 1) * time_devices + at, 1)]
        copies[2 + 2 * f].wait()
        copies[3 + 2 * f].wait()

        def some(i, _, f=f, mean=mean, inv_std=inv_std):
            here = pl.ds(1 + i * step, step)
            cot = flat(cot_ref[f, pl.ds(2 + i * step, step)])
            scaled = grads(flat(mixed_ref[f, here]), cot, mean, inv_std)
            scaled_ref[f, here] = scaled.reshape(step, columns, TILE)
            return 0

        lax.fori_loop(0, rows // step, some, 0, unroll=2)
        top = before_ref[f, 1] if own else cot_ref[f, 1]
        bottom = after_ref[f, 0] if own else cot_ref[f, rows + 2]
        for row, cot in ((0, top), (rows + 1, bottom)):
            scaled_ref[f, row] = grads(mixed_ref[f, row], cot, mean, inv_std)
        copy = pltpu.make_async_copy(scaled_ref.at[f], scaled_hbm.at[f], out_sems.at[f])
        copy.start()
        leaving.append(copy)
    for copy in leaving:
        copy.wait()


def parameter_grads(
    time_devices,
    height_devices,
    per_frame,
    got_ref,
    stats_ref,
    mixed_hbm,
    mixed_next_hbm,
    scaled_hbm,
    xt_hbm,
    ft_hbm,
    temporal_hbm,
    out_ref,
    feature_grad_hbm,
    carry_ref,
    mixed_grad_ref,
    feature_grad_ref,
    mixed_ref,
    scaled_ref,
    xt_ref,
    ft_ref,
    temporal_ref,
    shifted_ref,
    sems,
    out_sems,
):
    frames, ext, columns, _ = feature_grad_ref.shape
    rows = ext - 2
    copies = fetch(
        [
            (mixed_hbm, mixed_ref.at[pl.ds(0, frames)]),
            (mixed_next_hbm, mixed_ref.at[pl.ds(frames, 2)]),
            (scaled_hbm, scaled_ref),
            (temporal_hbm, temporal_ref),
            (xt_hbm, xt_ref),
            (ft_hbm, ft_ref),
        ],
        sems,
    )
    me, level = lax.axis_index("tm"), lax.axis_index("height")
    following = jnp.minimum(me + 1, time_devices - 1)
    here = per_device_sums(got_ref[...], time_devices, height_devices, False)
    group = group_matrix(frames)
    lane = iota(here.shape, 1) % frames
    firsts, seconds = [], []
    for f in range(frames):
        sums = exact_dot(jnp.where(lane == f, here, 0.0), group)
        sum_a, sum_b = sums[:time_devices], sums[time_devices:]
        at = 2 * f * time_devices
        mean = stats_ref[at : at + time_devices]
        inv_std = stats_ref[at + time_devices : at + 2 * time_devices]
        count = counts(f, frames, time_devices, per_frame)
        firsts.append((-inv_std * sum_a + inv_std * inv_std * sum_b * mean) / count)
        seconds.append(-inv_std * inv_std * sum_b / (2.0 * count))
    square = (time_devices, time_devices)
    later = (iota(square, 1) > iota(square, 0)).astype(jnp.float32)
    for kind, values in enumerate((firsts, seconds)):
        run = exact_dot(later, sum(values[1:], values[0]))
        for f in range(frames - 1, -1, -1):
            run = run + values[f]
            at = (2 * f + kind) * time_devices
            carry_ref[at : at + time_devices] = run
    for copy in copies[:3]:
        copy.wait()
    exists = (me < time_devices - 1).astype(jnp.float32)
    for f in range(frames + 2):
        own = f < frames
        at, g = (me, f) if own else (following, f - frames)
        first = carry_ref[pl.ds(2 * g * time_devices + at, 1)]
        second = 2.0 * carry_ref[pl.ds((2 * g + 1) * time_devices + at, 1)]

        def some(i, _, f=f, own=own, first=first, second=second):
            at = pl.ds(i * 3, 3)
            grad = flat(scaled_ref[f, at]) + first + flat(mixed_ref[f, at]) * second
            if not own:
                grad = grad * exists
            mixed_grad_ref[f, at] = grad.astype(jnp.bfloat16).reshape(3, columns, TILE)
            return 0

        lax.fori_loop(0, ext // 3, some, 0, unroll=3)
    copies[3].wait()
    back = jnp.concatenate([temporal_ref[k] for k in range(3)], axis=1)
    leaving = []
    place = iota((ext * columns, TILE), 0) // columns
    outside = ((place == 0) & (level == 0)) | ((place == ext - 1) & (level == height_devices - 1))
    size = rows * columns
    for f in range(frames):
        blocks = [flat(mixed_grad_ref[f + 2 - k]) for k in range(3)]
        grad = dot(jnp.concatenate(blocks, axis=1), back, True)
        grad = jnp.where(outside, 0.0, grad).astype(jnp.bfloat16)
        feature_grad_ref[f] = grad.reshape(ext, columns, TILE)
        copy = pltpu.make_async_copy(
            feature_grad_ref.at[f], feature_grad_hbm.at[f], out_sems.at[f]
        )
        copy.start()
        leaving.append(copy)
        inner = grad[columns : (rows + 1) * columns]
        wide = inner.astype(jnp.float32)
        shifted_ref[f * size : (f + 1) * size] = jnp.concatenate(
            [
                moved(wide, -1, columns).astype(jnp.bfloat16),
                inner,
                moved(wide, 1, columns).astype(jnp.bfloat16),
            ],
            axis=1,
        )
    for copy in copies[4:]:
        copy.wait()
    inner = flat(mixed_grad_ref[:frames, 1 : rows + 1])
    temporal = [dot(ft_ref[:, k * size : (k + frames) * size], inner) for k in range(3)]
    spatial = dot(xt_ref[...], shifted_ref[...])
    pieces = out_ref.shape[0]
    piece = 12 * TILE // pieces
    blocks = [spatial[:, j * TILE : (j + 1) * TILE] for j in range(3)] + temporal
    whole = jnp.concatenate(blocks, axis=0).astype(jnp.bfloat16)
    for p in range(pieces):
        out_ref[p, :piece] = whole[p * piece : (p + 1) * piece]
        at = 2 * frames * time_devices + 8 * min(p, 1)
        tail = stats_ref[at : at + 8]
        tail = jnp.where((iota((8, TILE), 0) == 0) & (p < 2), tail, 0.0)
        out_ref[p, piece : piece + 8] = tail.astype(jnp.bfloat16)
    for copy in leaving:
        copy.wait()


def input_grads(grad_ref, cot_ref, spatial_ref, out_ref, weight_ref):
    frames, rows, columns, _ = cot_ref.shape
    for s in range(3):
        for j in range(3):
            weight_ref[j * TILE : (j + 1) * TILE, s * TILE : (s + 1) * TILE] = spatial_ref[2 - s, j]

    def one(f, _):
        out = convolve(flat(grad_ref[f]), weight_ref[...], rows, columns, True)
        out = out + flat(cot_ref[f]).astype(jnp.float32)
        out_ref[f] = out.astype(jnp.bfloat16).reshape(out_ref.shape[1:])
        return 0

    lax.fori_loop(0, frames, one, 0)


def sum_and_copy(got_ref, out_ref):
    total = got_ref[0].astype(jnp.float32)
    for i in range(1, got_ref.shape[0]):
        total = total + got_ref[i].astype(jnp.float32)
    total = total.astype(jnp.bfloat16)
    for i in range(out_ref.shape[0]):
        out_ref[i] = total


def finish(scale, got_ref, spatial_ref, temporal_ref, gain_ref, shift_ref):
    pieces, piece = got_ref.shape[0], got_ref.shape[1] - 8
    for p in range(pieces):
        value = got_ref[p].astype(jnp.float32) * scale
        if p < 2:
            (gain_ref, shift_ref)[p][...] = value[piece : piece + 1]
        at = p * piece
        while at < (p + 1) * piece:
            block, row = at // TILE, at % TILE
            size = min(TILE - row, (p + 1) * piece - at)
            part = value[at - p * piece : at - p * piece + size]
            if block < 9:
                spatial_ref[block % 3, block // 3, row : row + size] = part
            else:
                temporal_ref[block - 9, row : row + size] = part
            at += size


def call(body, outs, args, scratch=(), flops=0, far=(), far_outs=(), limit=WIDE):
    everything = (*args, *far, *outs, *far_outs)
    moved_bytes = sum(a.size * a.dtype.itemsize for a in everything)
    near, away = pl.BlockSpec(memory_space=pltpu.VMEM), pl.BlockSpec(memory_space=pl.ANY)
    return pl.pallas_call(
        body,
        out_shape=[*outs, *far_outs],
        in_specs=[near] * len(args) + [away] * len(far),
        out_specs=[near] * len(outs) + [away] * len(far_outs),
        scratch_shapes=list(scratch),
        compiler_params=pltpu.CompilerParams(vmem_limit_bytes=limit * 1024 * 1024),
        cost_estimate=pl.CostEstimate(
            flops=flops, bytes_accessed=moved_bytes, transcendentals=0
        ),
    )(*args, *far)


def shards(inputs, spatial_kernel, temporal_kernel, norm_gain, norm_shift, cotangent):
    x, cot = inputs[0], cotangent[0]
    frames, rows, columns, channels = x.shape
    ext = rows + 2
    reps, time_devices, height_devices = (lax.axis_size(a) for a in ("rep", "tm", "height"))
    per_frame = float(rows * height_devices * columns * (channels // GROUPS))
    bf16, f32 = jnp.bfloat16, jnp.float32
    out = jax.ShapeDtypeStruct
    frame = (columns, channels)
    gain, shift = norm_gain[None], norm_shift[None]
    weight = pltpu.VMEM((3 * channels, 3 * channels), bf16)
    conv = 2 * 9 * channels * channels * columns

    onward = [(i, i + 1) for i in range(time_devices - 1)]
    back = [(j, i) for i, j in onward]
    late_frames = x[frames - 2 :]
    prev = lax.ppermute(late_frames, "tm", onward)
    up = [(i, i + 1) for i in range(height_devices - 1)]
    down = [(j, i) for i, j in up]
    before = lax.ppermute(jnp.concatenate([x[:, rows - 2 :], cot[:, rows - 2 :]], 0), "height", up)
    after = lax.ppermute(jnp.concatenate([x[:, :2], cot[:, :2]], 0), "height", down)
    cross = ("tm", "height")
    slant = [(t * height_devices + i, (t + 1) * height_devices + j) for t, _ in onward for i, j in up]
    prev_before = lax.ppermute(late_frames[:, rows - 2 :], cross, slant)
    slant = [(t * height_devices + i, (t + 1) * height_devices + j) for t, _ in onward for i, j in down]
    prev_after = lax.ppermute(late_frames[:, :2], cross, slant)
    first = jnp.concatenate(
        [
            jnp.concatenate([before[:2], before[4:6]], 0),
            jnp.concatenate([x[:2], cot[:2]], 0),
            jnp.concatenate([after[:2], after[4:6]], 0),
        ],
        1,
    )
    following = lax.ppermute(first, "tm", back)

    dma = lambda count: pltpu.SemaphoreType.DMA((count,))
    turned_x = out((3 * channels, frames * rows * columns), bf16)
    turned_features = out((channels, (frames + 2) * rows * columns), bf16)
    held = lambda a: pltpu.VMEM(a.shape, a.dtype)
    two = out((2, ext) + frame, bf16)
    own_two = out((frames, ext) + frame, bf16)
    feature, late = call(
        own_features,
        [own_two],
        (x, before, after, spatial_kernel),
        [weight, dma(1)],
        conv * frames * ext,
        far_outs=[own_two],
        limit=NARROW,
    )
    peers = time_devices * height_devices
    mixed, payload = call(
        mixed_and_sums,
        [out((frames, ext) + frame, f32), out((2 * peers, channels), f32)],
        (feature, prev, prev_before, prev_after, spatial_kernel, temporal_kernel),
        [weight, held(two)],
        conv * frames * ext,
        limit=NARROW,
    )
    share = ("tm", "height")
    got = lax.all_to_all(payload, share, 0, 0, tiled=True)
    xt, ft = call(
        turn,
        [turned_x, turned_features],
        (x, before, after, prev, prev_before, prev_after, late, spatial_kernel),
        [weight, held(two)],
        conv * frames * ext,
    )
    (mixed_next,) = call(
        next_frames,
        [out((2, ext) + frame, f32)],
        (),
        [
            weight,
            held(two),
            pltpu.VMEM((2, rows + 4) + frame, bf16),
            held(two),
            held(spatial_kernel),
            held(temporal_kernel),
            dma(4),
        ],
        conv * 2 * ext,
        far=(following, late, spatial_kernel, temporal_kernel),
    )
    stats, payload = call(
        functools.partial(statistics_and_sums, time_devices, height_devices, per_frame),
        [
            out((2 * frames * time_devices + 16, channels), f32),
            out((2 * peers, channels), f32),
        ],
        (got, mixed, cot, gain, shift),
        limit=NARROW,
    )
    got = lax.all_to_all(payload, share, 0, 0, tiled=True)
    scaled_shape = out((frames + 2, ext) + frame, f32)
    (scaled,) = call(
        functools.partial(mixed_grads, time_devices),
        [],
        (stats, gain, shift),
        [
            held(scaled_shape),
            held(scaled_shape),
            pltpu.VMEM((frames + 2, rows + 4) + frame, bf16),
            pltpu.VMEM((frames, 2) + frame, bf16),
            pltpu.VMEM((frames, 2) + frame, bf16),
            dma(2 * frames + 6),
            dma(frames + 2),
        ],
        far=(mixed, mixed_next, cot, before, after, following),
        far_outs=[scaled_shape],
    )
    (outputs,) = call(
        functools.partial(write_outputs, time_devices),
        [out((frames, rows) + frame, bf16)],
        (stats, mixed, x, gain, shift),
    )
    ends = ("rep", "height")
    pieces = reps * height_devices
    partial, feature_grad = call(
        functools.partial(parameter_grads, time_devices, height_devices, per_frame),
        [out((pieces, 12 * TILE // pieces + 8, channels), bf16)],
        (got, stats),
        [
            pltpu.VMEM((2 * frames * time_devices, channels), f32),
            pltpu.VMEM((frames + 2, ext) + frame, bf16),
            held(own_two),
            held(scaled_shape),
            held(scaled_shape),
            held(turned_x),
            held(turned_features),
            held(temporal_kernel),
            pltpu.VMEM((frames * rows * columns, 3 * channels), bf16),
            dma(6),
            dma(frames),
        ],
        conv * frames * rows * 2,
        far=(mixed, mixed_next, scaled, xt, ft, temporal_kernel),
        far_outs=[own_two],
    )
    partial = lax.all_to_all(partial, ends, 0, 0, tiled=True)
    (grad_inputs,) = call(
        input_grads,
        [out((frames, rows) + frame, bf16)],
        (feature_grad, cot, spatial_kernel),
        [weight],
        conv * frames * rows,
    )
    piece = partial.shape[1:]
    (partial,) = call(sum_and_copy, [out((time_devices,) + piece, bf16)], (partial,), limit=NARROW)
    partial = lax.all_to_all(partial, "tm", 0, 0, tiled=True)
    (partial,) = call(sum_and_copy, [out((pieces,) + piece, bf16)], (partial,), limit=NARROW)
    sums = lax.all_to_all(partial, ends, 0, 0, tiled=True)
    pixel_total = reps * frames * time_devices * rows * height_devices * columns
    spatial_sum, temporal_sum, gain_sum, shift_sum = call(
        functools.partial(finish, 1.0 / math.sqrt(pixel_total)),
        [
            out(spatial_kernel.shape, f32),
            out(temporal_kernel.shape, f32),
            out((1, channels), f32),
            out((1, channels), f32),
        ],
        (sums,),
        limit=NARROW,
    )
    return (
        outputs[None],
        grad_inputs[None],
        spatial_sum,
        temporal_sum,
        gain_sum[0],
        shift_sum[0],
    )


def solution(mesh):
    in_specs = (
        P("rep", "tm", "height", None, None),
        P(),
        P(),
        P(),
        P(),
        P("rep", "tm", "height", None, None),
    )
    out_specs = (
        P("rep", "tm", "height", None, None),
        P("rep", "tm", "height", None, None),
        P(),
        P(),
        P(),
        P(),
    )
    return jax.shard_map(shards, mesh=mesh, in_specs=in_specs, out_specs=out_specs, check_vma=False)
```

```python
import functools
import math

import jax
import jax.numpy as jnp
from jax import lax
from jax.experimental import pallas as pl
from jax.experimental.pallas import tpu as pltpu
from jax.sharding import PartitionSpec as P

GROUPS = 32


EPS = 1e-05
TILE = 128
FULL, WIDE, NARROW = 58, 53, 16


def iota(shape, dim):
    return lax.broadcasted_iota(jnp.int32, shape, dim)


def exact_dot(a, b):
    return lax.dot_general(
        a,
        b,
        (((1,), (0,)), ((), ())),
        precision=lax.Precision.HIGHEST,
        preferred_element_type=jnp.float32,
    )


def dot(a, b, turned=False):
    return lax.dot_general(
        a,
        b,
        (((1,), (1 if turned else 0,)), ((), ())),
        preferred_element_type=jnp.float32,
    )


def group_matrix(size):
    return (iota((TILE, TILE), 0) // size == iota((TILE, TILE), 1) // size).astype(jnp.float32)


def per_device_sums(got, time_devices, height_devices, earlier):
    shape = (2 * time_devices, got.shape[0])
    row, col = iota(shape, 0), iota(shape, 1)
    at, source = row % time_devices, col // (2 * height_devices)
    keep = (source < at) if earlier else (source == at)
    keep = keep & (row // time_devices == col % 2)
    return exact_dot(keep.astype(jnp.float32), got)


def moved(value, step, columns):
    pixels = value.shape[0]
    rolled = pltpu.roll(value, step % pixels, 0)
    place = iota(value.shape, 0) % columns
    edge = 0 if step > 0 else columns - 1
    return jnp.where(place == edge, 0.0, rolled)


def three_rows(block, rows, columns):
    size = rows * columns
    return jnp.concatenate(
        [block[i * columns : i * columns + size] for i in range(3)], axis=1
    )


def convolve(block, weight, rows, columns, turned):
    taps = dot(three_rows(block, rows, columns), weight, turned)
    c = taps.shape[1] // 3
    sign = -1 if turned else 1
    return (
        taps[:, c : 2 * c]
        + moved(taps[:, :c], sign, columns)
        + moved(taps[:, 2 * c :], -sign, columns)
    )


def flat(value):
    return value.reshape(-1, value.shape[-1])


def put_weight(weight_ref, spatial_ref):
    for i in range(3):
        for j in range(3):
            weight_ref[i * TILE : (i + 1) * TILE, j * TILE : (j + 1) * TILE] = spatial_ref[i, j]


def put_payload(out_ref, firsts, seconds):
    frames = len(firsts)
    sums = exact_dot(jnp.concatenate(firsts + seconds, 0), group_matrix(frames))
    lane = iota((1, TILE), 1) % frames
    rows = []
    for start in (0, frames):
        line = jnp.zeros((1, TILE), jnp.float32)
        for f in range(frames):
            line = jnp.where(lane == f, sums[start + f : start + f + 1], line)
        rows.append(line)
    line = jnp.where(iota((8, TILE), 0) % 2 == 0, rows[0], rows[1])
    for i in range(out_ref.shape[0] // 8):
        out_ref[i * 8 : (i + 1) * 8] = line


def fetch(pairs, sems):
    copies = [pltpu.make_async_copy(a, b, sems.at[i]) for i, (a, b) in enumerate(pairs)]
    for copy in copies:
        copy.start()
    return copies


def turned(value):
    return value.astype(jnp.float32).T.astype(jnp.bfloat16)


def own_features(
    x_ref, before_ref, after_ref, spatial_ref, feature_ref, far_ref, weight_ref, sems
):
    put_weight(weight_ref, spatial_ref)
    frames, rows, columns, _ = x_ref.shape

    def one(f, _):
        block = jnp.concatenate([flat(before_ref[f]), flat(x_ref[f]), flat(after_ref[f])], 0)
        out = convolve(block, weight_ref[...], rows + 2, columns, False)
        feature_ref[f] = out.astype(jnp.bfloat16).reshape(feature_ref.shape[1:])
        return 0

    lax.fori_loop(0, frames, one, 0)
    for copy in fetch([(feature_ref, far_ref)], sems):
        copy.wait()


def turn(
    x_ref,
    before_ref,
    after_ref,
    prev_ref,
    feature_ref,
    spatial_ref,
    xt_ref,
    ft_ref,
    weight_ref,
    prior_ref,
):
    put_weight(weight_ref, spatial_ref)
    frames, rows, columns, _ = x_ref.shape
    size = rows * columns

    def one(f, _):
        out = convolve(flat(prev_ref[f]), weight_ref[...], rows + 2, columns, False)
        prior_ref[f] = out.astype(jnp.bfloat16).reshape(prior_ref.shape[1:])
        return 0

    lax.fori_loop(0, 2, one, 0)
    for f in range(frames + 2):
        seen = prior_ref[f, 1 : rows + 1] if f < 2 else feature_ref[f - 2, 1 : rows + 1]
        ft_ref[:, f * size : (f + 1) * size] = turned(flat(seen))
    for f in range(frames):
        block = jnp.concatenate(
            [flat(before_ref[f, 1:]), flat(x_ref[f]), flat(after_ref[f, :1])], 0
        )
        xt_ref[:, f * size : (f + 1) * size] = turned(three_rows(block, rows, columns))


def mix(blocks, temporal_ref):
    return dot(jnp.concatenate(blocks, axis=1), flat(temporal_ref[...]))


def mixed_and_sums(
    feature_ref,
    prev_ref,
    spatial_ref,
    temporal_ref,
    mixed_ref,
    out_ref,
    weight_ref,
    prior_ref,
):
    put_weight(weight_ref, spatial_ref)
    frames, rows, columns, _ = mixed_ref.shape

    def one(f, _):
        out = convolve(flat(prev_ref[f]), weight_ref[...], rows, columns, False)
        prior_ref[f] = out.astype(jnp.bfloat16).reshape(prior_ref.shape[1:])
        return 0

    lax.fori_loop(0, 2, one, 0)
    firsts, seconds = [], []
    for f in range(frames):
        blocks = [
            flat(prior_ref[f + k]) if f + k < 2 else flat(feature_ref[f + k - 2]) for k in range(3)
        ]
        out = mix(blocks, temporal_ref)
        mixed_ref[f] = out.reshape(mixed_ref.shape[1:])
        inner = out[columns : (rows - 1) * columns]
        firsts.append(inner.sum(0, keepdims=True))
        seconds.append((inner * inner).sum(0, keepdims=True))
    put_payload(out_ref, firsts, seconds)


def next_frames(
    next_hbm,
    late_hbm,
    spatial_hbm,
    temporal_hbm,
    mixed_ref,
    weight_ref,
    held_ref,
    next_ref,
    late_ref,
    spatial_ref,
    temporal_ref,
    sems,
):
    copies = fetch(
        [
            (spatial_hbm, spatial_ref),
            (next_hbm.at[pl.ds(0, 2)], next_ref),
            (late_hbm.at[pl.ds(late_hbm.shape[0] - 2, 2)], late_ref),
            (temporal_hbm, temporal_ref),
        ],
        sems,
    )
    _, ext, columns, _ = mixed_ref.shape
    copies[0].wait()
    put_weight(weight_ref, spatial_ref)
    copies[1].wait()

    def one(f, _):
        out = convolve(flat(next_ref[f]), weight_ref[...], ext, columns, False)
        held_ref[f] = out.astype(jnp.bfloat16).reshape(held_ref.shape[1:])
        return 0

    lax.fori_loop(0, 2, one, 0)
    copies[2].wait()
    copies[3].wait()
    for f in range(2):
        blocks = [flat(late_ref[f + k]) if f + k < 2 else flat(held_ref[f + k - 2]) for k in range(3)]
        mixed_ref[f] = mix(blocks, temporal_ref).reshape(mixed_ref.shape[1:])


def counts(f, frames, time_devices, per_frame):
    at = iota((time_devices, TILE), 0) * frames + (f + 1)
    return at.astype(jnp.float32) * per_frame


def statistics_and_sums(
    time_devices,
    height_devices,
    per_frame,
    got_ref,
    mixed_ref,
    cot_ref,
    gain_ref,
    shift_ref,
    stats_ref,
    out_ref,
):
    frames, rows, _, _ = cot_ref.shape
    me = lax.axis_index("tm")
    got = got_ref[...]
    here = per_device_sums(got, time_devices, height_devices, False)
    earlier = per_device_sums(got, time_devices, height_devices, True)
    group = group_matrix(frames)
    lane = iota(here.shape, 1) % frames
    for f in range(frames):
        sums = exact_dot(earlier + jnp.where(lane <= f, here, 0.0), group)
        count = counts(f, frames, time_devices, per_frame)
        mean = sums[:time_devices] / count
        variance = sums[time_devices:] / count - mean * mean
        at = 2 * f * time_devices
        stats_ref[at : at + time_devices] = mean
        stats_ref[at + time_devices : at + 2 * time_devices] = lax.rsqrt(variance + EPS)
    gain, shift = gain_ref[...], shift_ref[...]
    step = 4
    firsts, seconds = [], []
    for f in range(frames):
        mean = stats_ref[pl.ds(2 * f * time_devices + me, 1)]
        inv_std = stats_ref[pl.ds((2 * f + 1) * time_devices + me, 1)]

        def some(i, sums, f=f, mean=mean, inv_std=inv_std):
            normed = (flat(mixed_ref[f, pl.ds(1 + i * step, step)]) - mean) * inv_std
            pre = normed * gain + shift
            sigma = 1.0 / (1.0 + jnp.exp(-pre))
            cot = flat(cot_ref[f, pl.ds(i * step, step)]).astype(jnp.float32)
            grad = cot * (sigma * (1.0 + pre * (1.0 - sigma)))
            split = (-1, 8, TILE)
            return (
                sums[0] + grad.reshape(split).sum(0),
                sums[1] + (grad * normed).reshape(split).sum(0),
            )

        zero = jnp.zeros((8, TILE), jnp.float32)
        a, b = lax.fori_loop(0, rows // step, some, (zero, zero), unroll=2)
        firsts.append(a.sum(0, keepdims=True))
        seconds.append(b.sum(0, keepdims=True))
    put_payload(out_ref, [a * gain for a in firsts], [b * gain for b in seconds])
    total_a, total_b = sum(firsts[1:], firsts[0]), sum(seconds[1:], seconds[0])
    at = 2 * frames * time_devices
    stats_ref[at : at + 16] = jnp.where(iota((16, TILE), 0) < 8, total_b, total_a)


def normalised(mixed, mean, inv_std, gain, shift):
    pre = (mixed - mean) * inv_std * gain + shift
    return pre, 1.0 / (1.0 + jnp.exp(-pre))


def write_outputs(time_devices, stats_ref, mixed_ref, x_ref, gain_ref, shift_ref, outputs_ref):
    frames, rows, columns, _ = x_ref.shape
    me = lax.axis_index("tm")
    gain, shift = gain_ref[...], shift_ref[...]
    step = 4
    for f in range(frames):
        mean = stats_ref[pl.ds(2 * f * time_devices + me, 1)]
        inv_std = stats_ref[pl.ds((2 * f + 1) * time_devices + me, 1)]

        def some(i, _, f=f, mean=mean, inv_std=inv_std):
            at = pl.ds(i * step, step)
            mixed = flat(mixed_ref[f, pl.ds(1 + i * step, step)])
            pre, sigma = normalised(mixed, mean, inv_std, gain, shift)
            kept = flat(x_ref[f, at]).astype(jnp.float32) + pre * sigma
            outputs_ref[f, at] = kept.astype(jnp.bfloat16).reshape(step, columns, TILE)
            return 0

        lax.fori_loop(0, rows // step, some, 0, unroll=2)


def mixed_grads(
    time_devices,
    stats_ref,
    gain_ref,
    shift_ref,
    mixed_hbm,
    mixed_next_hbm,
    cot_hbm,
    before_hbm,
    after_hbm,
    next_hbm,
    scaled_hbm,
    scaled_ref,
    mixed_ref,
    cot_ref,
    before_ref,
    after_ref,
    in_sems,
    out_sems,
):
    frames, rows, columns, _ = cot_hbm.shape
    pairs = [
        (before_hbm.at[pl.ds(frames, frames)], before_ref),
        (after_hbm.at[pl.ds(frames, frames)], after_ref),
    ]
    for f in range(frames + 2):
        own = f < frames
        pairs.append((mixed_hbm.at[f] if own else mixed_next_hbm.at[f - frames], mixed_ref.at[f]))
        if own:
            pairs.append((cot_hbm.at[f], cot_ref.at[f, pl.ds(2, rows)]))
        else:
            pairs.append((next_hbm.at[2 + f - frames], cot_ref.at[f]))
    copies = fetch(pairs, in_sems)
    me = lax.axis_index("tm")
    following = jnp.minimum(me + 1, time_devices - 1)
    gain, shift = gain_ref[...], shift_ref[...]
    step = 4

    def grads(mixed, cot, mean, inv_std):
        pre, sigma = normalised(mixed, mean, inv_std, gain, shift)
        grad = cot.astype(jnp.float32) * (sigma * (1.0 + pre * (1.0 - sigma)))
        return inv_std * (grad * gain)

    leaving = []
    copies[0].wait()
    copies[1].wait()
    for f in range(frames + 2):
        own = f < frames
        at, g = (me, f) if own else (following, f - frames)
        mean = stats_ref[pl.ds(2 * g * time_devices + at, 1)]
        inv_std = stats_ref[pl.ds((2 * g + 1) * time_devices + at, 1)]
        copies[2 + 2 * f].wait()
        copies[3 + 2 * f].wait()

        def some(i, _, f=f, mean=mean, inv_std=inv_std):
            here = pl.ds(1 + i * step, step)
            cot = flat(cot_ref[f, pl.ds(2 + i * step, step)])
            scaled = grads(flat(mixed_ref[f, here]), cot, mean, inv_std)
            scaled_ref[f, here] = scaled.reshape(step, columns, TILE)
            return 0

        lax.fori_loop(0, rows // step, some, 0, unroll=2)
        top = before_ref[f, 1] if own else cot_ref[f, 1]
        bottom = after_ref[f, 0] if own else cot_ref[f, rows + 2]
        for row, cot in ((0, top), (rows + 1, bottom)):
            scaled_ref[f, row] = grads(mixed_ref[f, row], cot, mean, inv_std)
        copy = pltpu.make_async_copy(scaled_ref.at[f], scaled_hbm.at[f], out_sems.at[f])
        copy.start()
        leaving.append(copy)
    for copy in leaving:
        copy.wait()


def parameter_grads(
    time_devices,
    height_devices,
    per_frame,
    got_ref,
    stats_ref,
    mixed_hbm,
    mixed_next_hbm,
    scaled_hbm,
    xt_hbm,
    ft_hbm,
    temporal_hbm,
    out_ref,
    feature_grad_hbm,
    carry_ref,
    mixed_grad_ref,
    feature_grad_ref,
    mixed_ref,
    scaled_ref,
    xt_ref,
    ft_ref,
    temporal_ref,
    shifted_ref,
    sems,
    out_sems,
):
    frames, ext, columns, _ = feature_grad_ref.shape
    rows = ext - 2
    copies = fetch(
        [
            (mixed_hbm, mixed_ref.at[pl.ds(0, frames)]),
            (mixed_next_hbm, mixed_ref.at[pl.ds(frames, 2)]),
            (scaled_hbm, scaled_ref),
            (temporal_hbm, temporal_ref),
            (xt_hbm, xt_ref),
            (ft_hbm, ft_ref),
        ],
        sems,
    )
    me, level = lax.axis_index("tm"), lax.axis_index("height")
    following = jnp.minimum(me + 1, time_devices - 1)
    here = per_device_sums(got_ref[...], time_devices, height_devices, False)
    group = group_matrix(frames)
    lane = iota(here.shape, 1) % frames
    firsts, seconds = [], []
    for f in range(frames):
        sums = exact_dot(jnp.where(lane == f, here, 0.0), group)
        sum_a, sum_b = sums[:time_devices], sums[time_devices:]
        at = 2 * f * time_devices
        mean = stats_ref[at : at + time_devices]
        inv_std = stats_ref[at + time_devices : at + 2 * time_devices]
        count = counts(f, frames, time_devices, per_frame)
        firsts.append((-inv_std * sum_a + inv_std * inv_std * sum_b * mean) / count)
        seconds.append(-inv_std * inv_std * sum_b / (2.0 * count))
    square = (time_devices, time_devices)
    later = (iota(square, 1) > iota(square, 0)).astype(jnp.float32)
    for kind, values in enumerate((firsts, seconds)):
        run = exact_dot(later, sum(values[1:], values[0]))
        for f in range(frames - 1, -1, -1):
            run = run + values[f]
            at = (2 * f + kind) * time_devices
            carry_ref[at : at + time_devices] = run
    for copy in copies[:3]:
        copy.wait()
    exists = (me < time_devices - 1).astype(jnp.float32)
    for f in range(frames + 2):
        own = f < frames
        at, g = (me, f) if own else (following, f - frames)
        first = carry_ref[pl.ds(2 * g * time_devices + at, 1)]
        second = 2.0 * carry_ref[pl.ds((2 * g + 1) * time_devices + at, 1)]

        def some(i, _, f=f, own=own, first=first, second=second):
            at = pl.ds(i * 3, 3)
            grad = flat(scaled_ref[f, at]) + first + flat(mixed_ref[f, at]) * second
            if not own:
                grad = grad * exists
            mixed_grad_ref[f, at] = grad.astype(jnp.bfloat16).reshape(3, columns, TILE)
            return 0

        lax.fori_loop(0, ext // 3, some, 0, unroll=3)
    copies[3].wait()
    back = jnp.concatenate([temporal_ref[k] for k in range(3)], axis=1)
    leaving = []
    place = iota((ext * columns, TILE), 0) // columns
    outside = ((place == 0) & (level == 0)) | ((place == ext - 1) & (level == height_devices - 1))
    size = rows * columns
    for f in range(frames):
        blocks = [flat(mixed_grad_ref[f + 2 - k]) for k in range(3)]
        grad = dot(jnp.concatenate(blocks, axis=1), back, True)
        grad = jnp.where(outside, 0.0, grad).astype(jnp.bfloat16)
        feature_grad_ref[f] = grad.reshape(ext, columns, TILE)
        copy = pltpu.make_async_copy(
            feature_grad_ref.at[f], feature_grad_hbm.at[f], out_sems.at[f]
        )
        copy.start()
        leaving.append(copy)
        inner = grad[columns : (rows + 1) * columns]
        wide = inner.astype(jnp.float32)
        shifted_ref[f * size : (f + 1) * size] = jnp.concatenate(
            [
                moved(wide, -1, columns).astype(jnp.bfloat16),
                inner,
                moved(wide, 1, columns).astype(jnp.bfloat16),
            ],
            axis=1,
        )
    for copy in copies[4:]:
        copy.wait()
    inner = flat(mixed_grad_ref[:frames, 1 : rows + 1])
    temporal = [dot(ft_ref[:, k * size : (k + frames) * size], inner) for k in range(3)]
    spatial = dot(xt_ref[...], shifted_ref[...])
    pieces = out_ref.shape[0]
    piece = 12 * TILE // pieces
    blocks = [spatial[:, j * TILE : (j + 1) * TILE] for j in range(3)] + temporal
    whole = jnp.concatenate(blocks, axis=0).astype(jnp.bfloat16)
    for p in range(pieces):
        out_ref[p, :piece] = whole[p * piece : (p + 1) * piece]
        at = 2 * frames * time_devices + 8 * min(p, 1)
        tail = stats_ref[at : at + 8]
        tail = jnp.where((iota((8, TILE), 0) == 0) & (p < 2), tail, 0.0)
        out_ref[p, piece : piece + 8] = tail.astype(jnp.bfloat16)
    for copy in leaving:
        copy.wait()


def input_grads(grad_ref, cot_ref, spatial_ref, out_ref, weight_ref):
    frames, rows, columns, _ = cot_ref.shape
    for s in range(3):
        for j in range(3):
            weight_ref[j * TILE : (j + 1) * TILE, s * TILE : (s + 1) * TILE] = spatial_ref[2 - s, j]

    def one(f, _):
        out = convolve(flat(grad_ref[f]), weight_ref[...], rows, columns, True)
        out = out + flat(cot_ref[f]).astype(jnp.float32)
        out_ref[f] = out.astype(jnp.bfloat16).reshape(out_ref.shape[1:])
        return 0

    lax.fori_loop(0, frames, one, 0)


def sum_and_copy(got_ref, out_ref):
    total = got_ref[0].astype(jnp.float32)
    for i in range(1, got_ref.shape[0]):
        total = total + got_ref[i].astype(jnp.float32)
    total = total.astype(jnp.bfloat16)
    for i in range(out_ref.shape[0]):
        out_ref[i] = total


def finish(scale, got_ref, spatial_ref, temporal_ref, gain_ref, shift_ref):
    pieces, piece = got_ref.shape[0], got_ref.shape[1] - 8
    for p in range(pieces):
        value = got_ref[p].astype(jnp.float32) * scale
        if p < 2:
            (gain_ref, shift_ref)[p][...] = value[piece : piece + 1]
        at = p * piece
        while at < (p + 1) * piece:
            block, row = at // TILE, at % TILE
            size = min(TILE - row, (p + 1) * piece - at)
            part = value[at - p * piece : at - p * piece + size]
            if block < 9:
                spatial_ref[block % 3, block // 3, row : row + size] = part
            else:
                temporal_ref[block - 9, row : row + size] = part
            at += size


def call(body, outs, args, scratch=(), flops=0, far=(), far_outs=(), limit=WIDE):
    everything = (*args, *far, *outs, *far_outs)
    moved_bytes = sum(a.size * a.dtype.itemsize for a in everything)
    near, away = pl.BlockSpec(memory_space=pltpu.VMEM), pl.BlockSpec(memory_space=pl.ANY)
    return pl.pallas_call(
        body,
        out_shape=[*outs, *far_outs],
        in_specs=[near] * len(args) + [away] * len(far),
        out_specs=[near] * len(outs) + [away] * len(far_outs),
        scratch_shapes=list(scratch),
        compiler_params=pltpu.CompilerParams(vmem_limit_bytes=limit * 1024 * 1024),
        cost_estimate=pl.CostEstimate(
            flops=flops, bytes_accessed=moved_bytes, transcendentals=0
        ),
    )(*args, *far)


def shards(inputs, spatial_kernel, temporal_kernel, norm_gain, norm_shift, cotangent):
    x, cot = inputs[0], cotangent[0]
    frames, rows, columns, channels = x.shape
    ext = rows + 2
    reps, time_devices, height_devices = (lax.axis_size(a) for a in ("rep", "tm", "height"))
    per_frame = float(rows * height_devices * columns * (channels // GROUPS))
    bf16, f32 = jnp.bfloat16, jnp.float32
    out = jax.ShapeDtypeStruct
    frame = (columns, channels)
    gain, shift = norm_gain[None], norm_shift[None]
    weight = pltpu.VMEM((3 * channels, 3 * channels), bf16)
    conv = 2 * 9 * channels * channels * columns

    up = [(i, i + 1) for i in range(height_devices - 1)]
    down = [(j, i) for i, j in up]
    before = lax.ppermute(jnp.concatenate([x[:, rows - 2 :], cot[:, rows - 2 :]], 0), "height", up)
    after = lax.ppermute(jnp.concatenate([x[:, :2], cot[:, :2]], 0), "height", down)
    onward = [(i, i + 1) for i in range(time_devices - 1)]
    back = [(j, i) for i, j in onward]
    last = jnp.concatenate([before[2:4], x[2:4], after[2:4]], 1)
    prev = lax.ppermute(last, "tm", onward)
    first = jnp.concatenate(
        [
            jnp.concatenate([before[:2], before[4:6]], 0),
            jnp.concatenate([x[:2], cot[:2]], 0),
            jnp.concatenate([after[:2], after[4:6]], 0),
        ],
        1,
    )
    following = lax.ppermute(first, "tm", back)

    dma = lambda count: pltpu.SemaphoreType.DMA((count,))
    turned_x = out((3 * channels, frames * rows * columns), bf16)
    turned_features = out((channels, (frames + 2) * rows * columns), bf16)
    held = lambda a: pltpu.VMEM(a.shape, a.dtype)
    two = out((2, ext) + frame, bf16)
    own_two = out((frames, ext) + frame, bf16)
    feature, late = call(
        own_features,
        [own_two],
        (x, before, after, spatial_kernel),
        [weight, dma(1)],
        conv * frames * ext,
        far_outs=[own_two],
        limit=NARROW,
    )
    peers = time_devices * height_devices
    mixed, payload = call(
        mixed_and_sums,
        [out((frames, ext) + frame, f32), out((2 * peers, channels), f32)],
        (feature, prev, spatial_kernel, temporal_kernel),
        [weight, held(two)],
        conv * frames * ext,
        limit=NARROW,
    )
    share = ("tm", "height")
    got = lax.all_to_all(payload, share, 0, 0, tiled=True)
    xt, ft = call(
        turn,
        [turned_x, turned_features],
        (x, before, after, prev, late, spatial_kernel),
        [weight, held(two)],
        conv * frames * ext,
    )
    (mixed_next,) = call(
        next_frames,
        [out((2, ext) + frame, f32)],
        (),
        [
            weight,
            held(two),
            pltpu.VMEM((2, rows + 4) + frame, bf16),
            held(two),
            held(spatial_kernel),
            held(temporal_kernel),
            dma(4),
        ],
        conv * 2 * ext,
        far=(following, late, spatial_kernel, temporal_kernel),
        limit=FULL,
    )
    stats, payload = call(
        functools.partial(statistics_and_sums, time_devices, height_devices, per_frame),
        [
            out((2 * frames * time_devices + 16, channels), f32),
            out((2 * peers, channels), f32),
        ],
        (got, mixed, cot, gain, shift),
        limit=NARROW,
    )
    got = lax.all_to_all(payload, share, 0, 0, tiled=True)
    scaled_shape = out((frames + 2, ext) + frame, f32)
    (scaled,) = call(
        functools.partial(mixed_grads, time_devices),
        [],
        (stats, gain, shift),
        [
            held(scaled_shape),
            held(scaled_shape),
            pltpu.VMEM((frames + 2, rows + 4) + frame, bf16),
            pltpu.VMEM((frames, 2) + frame, bf16),
            pltpu.VMEM((frames, 2) + frame, bf16),
            dma(2 * frames + 6),
            dma(frames + 2),
        ],
        far=(mixed, mixed_next, cot, before, after, following),
        far_outs=[scaled_shape],
    )
    (outputs,) = call(
        functools.partial(write_outputs, time_devices),
        [out((frames, rows) + frame, bf16)],
        (stats, mixed, x, gain, shift),
    )
    ends = ("rep", "height")
    pieces = reps * height_devices
    partial, feature_grad = call(
        functools.partial(parameter_grads, time_devices, height_devices, per_frame),
        [out((pieces, 12 * TILE // pieces + 8, channels), bf16)],
        (got, stats),
        [
            pltpu.VMEM((2 * frames * time_devices, channels), f32),
            pltpu.VMEM((frames + 2, ext) + frame, bf16),
            held(own_two),
            held(scaled_shape),
            held(scaled_shape),
            held(turned_x),
            held(turned_features),
            held(temporal_kernel),
            pltpu.VMEM((frames * rows * columns, 3 * channels), bf16),
            dma(6),
            dma(frames),
        ],
        conv * frames * rows * 2,
        far=(mixed, mixed_next, scaled, xt, ft, temporal_kernel),
        far_outs=[own_two],
    )
    partial = lax.all_to_all(partial, ends, 0, 0, tiled=True)
    (grad_inputs,) = call(
        input_grads,
        [out((frames, rows) + frame, bf16)],
        (feature_grad, cot, spatial_kernel),
        [weight],
        conv * frames * rows,
    )
    piece = partial.shape[1:]
    (partial,) = call(sum_and_copy, [out((time_devices,) + piece, bf16)], (partial,), limit=NARROW)
    partial = lax.all_to_all(partial, "tm", 0, 0, tiled=True)
    (partial,) = call(sum_and_copy, [out((pieces,) + piece, bf16)], (partial,), limit=NARROW)
    sums = lax.all_to_all(partial, ends, 0, 0, tiled=True)
    pixel_total = reps * frames * time_devices * rows * height_devices * columns
    spatial_sum, temporal_sum, gain_sum, shift_sum = call(
        functools.partial(finish, 1.0 / math.sqrt(pixel_total)),
        [
            out(spatial_kernel.shape, f32),
            out(temporal_kernel.shape, f32),
            out((1, channels), f32),
            out((1, channels), f32),
        ],
        (sums,),
        limit=NARROW,
    )
    return (
        outputs[None],
        grad_inputs[None],
        spatial_sum,
        temporal_sum,
        gain_sum[0],
        shift_sum[0],
    )


def solution(mesh):
    in_specs = (
        P("rep", "tm", "height", None, None),
        P(),
        P(),
        P(),
        P(),
        P("rep", "tm", "height", None, None),
    )
    out_specs = (
        P("rep", "tm", "height", None, None),
        P("rep", "tm", "height", None, None),
        P(),
        P(),
        P(),
        P(),
    )
    return jax.shard_map(shards, mesh=mesh, in_specs=in_specs, out_specs=out_specs, check_vma=False)
```

```python
import functools
import math

import jax
import jax.numpy as jnp
from jax import lax
from jax.experimental import pallas as pl
from jax.experimental.pallas import tpu as pltpu
from jax.sharding import PartitionSpec as P

GROUPS = 32


EPS = 1e-05
TILE = 128
FULL, WIDE, NARROW = 58, 53, 16


def iota(shape, dim):
    return lax.broadcasted_iota(jnp.int32, shape, dim)


def exact_dot(a, b):
    return lax.dot_general(
        a,
        b,
        (((1,), (0,)), ((), ())),
        precision=lax.Precision.HIGHEST,
        preferred_element_type=jnp.float32,
    )


def dot(a, b, turned=False):
    return lax.dot_general(
        a,
        b,
        (((1,), (1 if turned else 0,)), ((), ())),
        preferred_element_type=jnp.float32,
    )


def group_matrix(size):
    return (iota((TILE, TILE), 0) // size == iota((TILE, TILE), 1) // size).astype(jnp.float32)


def per_device_sums(got, time_devices, height_devices, earlier):
    shape = (2 * time_devices, got.shape[0])
    row, col = iota(shape, 0), iota(shape, 1)
    at, source = row % time_devices, col // (2 * height_devices)
    keep = (source < at) if earlier else (source == at)
    keep = keep & (row // time_devices == col % 2)
    return exact_dot(keep.astype(jnp.float32), got)


def moved(value, step, columns):
    pixels = value.shape[0]
    rolled = pltpu.roll(value, step % pixels, 0)
    place = iota(value.shape, 0) % columns
    edge = 0 if step > 0 else columns - 1
    return jnp.where(place == edge, 0.0, rolled)


def three_rows(block, rows, columns):
    size = rows * columns
    return jnp.concatenate(
        [block[i * columns : i * columns + size] for i in range(3)], axis=1
    )


def convolve(block, weight, rows, columns, turned):
    taps = dot(three_rows(block, rows, columns), weight, turned)
    c = taps.shape[1] // 3
    sign = -1 if turned else 1
    return (
        taps[:, c : 2 * c]
        + moved(taps[:, :c], sign, columns)
        + moved(taps[:, 2 * c :], -sign, columns)
    )


def flat(value):
    return value.reshape(-1, value.shape[-1])


def put_weight(weight_ref, spatial_ref):
    for i in range(3):
        for j in range(3):
            weight_ref[i * TILE : (i + 1) * TILE, j * TILE : (j + 1) * TILE] = spatial_ref[i, j]


def put_payload(out_ref, firsts, seconds):
    frames = len(firsts)
    sums = exact_dot(jnp.concatenate(firsts + seconds, 0), group_matrix(frames))
    lane = iota((1, TILE), 1) % frames
    rows = []
    for start in (0, frames):
        line = jnp.zeros((1, TILE), jnp.float32)
        for f in range(frames):
            line = jnp.where(lane == f, sums[start + f : start + f + 1], line)
        rows.append(line)
    line = jnp.where(iota((8, TILE), 0) % 2 == 0, rows[0], rows[1])
    for i in range(out_ref.shape[0] // 8):
        out_ref[i * 8 : (i + 1) * 8] = line


def fetch(pairs, sems):
    copies = [pltpu.make_async_copy(a, b, sems.at[i]) for i, (a, b) in enumerate(pairs)]
    for copy in copies:
        copy.start()
    return copies


def turned(value):
    return value.astype(jnp.float32).T.astype(jnp.bfloat16)


def own_features(
    x_ref, before_ref, after_ref, spatial_ref, feature_ref, far_ref, weight_ref, sems
):
    put_weight(weight_ref, spatial_ref)
    frames, rows, columns, _ = x_ref.shape

    def one(f, _):
        block = jnp.concatenate([flat(before_ref[f]), flat(x_ref[f]), flat(after_ref[f])], 0)
        out = convolve(block, weight_ref[...], rows + 2, columns, False)
        feature_ref[f] = out.astype(jnp.bfloat16).reshape(feature_ref.shape[1:])
        return 0

    lax.fori_loop(0, frames, one, 0)
    for copy in fetch([(feature_ref, far_ref)], sems):
        copy.wait()


def turn(
    x_ref,
    before_ref,
    after_ref,
    prev_ref,
    feature_ref,
    spatial_ref,
    xt_ref,
    ft_ref,
    weight_ref,
    prior_ref,
):
    put_weight(weight_ref, spatial_ref)
    frames, rows, columns, _ = x_ref.shape
    size = rows * columns

    def one(f, _):
        out = convolve(flat(prev_ref[f]), weight_ref[...], rows + 2, columns, False)
        prior_ref[f] = out.astype(jnp.bfloat16).reshape(prior_ref.shape[1:])
        return 0

    lax.fori_loop(0, 2, one, 0)
    for f in range(frames + 2):
        seen = prior_ref[f, 1 : rows + 1] if f < 2 else feature_ref[f - 2, 1 : rows + 1]
        ft_ref[:, f * size : (f + 1) * size] = turned(flat(seen))
    for f in range(frames):
        block = jnp.concatenate(
            [flat(before_ref[f, 1:]), flat(x_ref[f]), flat(after_ref[f, :1])], 0
        )
        xt_ref[:, f * size : (f + 1) * size] = turned(three_rows(block, rows, columns))


def mix(blocks, temporal_ref):
    return dot(jnp.concatenate(blocks, axis=1), flat(temporal_ref[...]))


def mixed_and_sums(
    feature_ref,
    prev_ref,
    spatial_ref,
    temporal_ref,
    mixed_ref,
    out_ref,
    weight_ref,
    prior_ref,
):
    put_weight(weight_ref, spatial_ref)
    frames, rows, columns, _ = mixed_ref.shape

    def one(f, _):
        out = convolve(flat(prev_ref[f]), weight_ref[...], rows, columns, False)
        prior_ref[f] = out.astype(jnp.bfloat16).reshape(prior_ref.shape[1:])
        return 0

    lax.fori_loop(0, 2, one, 0)
    firsts, seconds = [], []
    for f in range(frames):
        blocks = [
            flat(prior_ref[f + k]) if f + k < 2 else flat(feature_ref[f + k - 2]) for k in range(3)
        ]
        out = mix(blocks, temporal_ref)
        mixed_ref[f] = out.reshape(mixed_ref.shape[1:])
        inner = out[columns : (rows - 1) * columns]
        firsts.append(inner.sum(0, keepdims=True))
        seconds.append((inner * inner).sum(0, keepdims=True))
    put_payload(out_ref, firsts, seconds)


def next_frames(
    next_hbm,
    late_hbm,
    spatial_hbm,
    temporal_hbm,
    mixed_ref,
    weight_ref,
    held_ref,
    next_ref,
    late_ref,
    spatial_ref,
    temporal_ref,
    sems,
):
    copies = fetch(
        [
            (spatial_hbm, spatial_ref),
            (next_hbm.at[pl.ds(0, 2)], next_ref),
            (late_hbm.at[pl.ds(late_hbm.shape[0] - 2, 2)], late_ref),
            (temporal_hbm, temporal_ref),
        ],
        sems,
    )
    _, ext, columns, _ = mixed_ref.shape
    copies[0].wait()
    put_weight(weight_ref, spatial_ref)
    copies[1].wait()

    def one(f, _):
        out = convolve(flat(next_ref[f]), weight_ref[...], ext, columns, False)
        held_ref[f] = out.astype(jnp.bfloat16).reshape(held_ref.shape[1:])
        return 0

    lax.fori_loop(0, 2, one, 0)
    copies[2].wait()
    copies[3].wait()
    for f in range(2):
        blocks = [flat(late_ref[f + k]) if f + k < 2 else flat(held_ref[f + k - 2]) for k in range(3)]
        mixed_ref[f] = mix(blocks, temporal_ref).reshape(mixed_ref.shape[1:])


def counts(f, frames, time_devices, per_frame):
    at = iota((time_devices, TILE), 0) * frames + (f + 1)
    return at.astype(jnp.float32) * per_frame


def statistics_and_sums(
    time_devices,
    height_devices,
    per_frame,
    got_ref,
    mixed_ref,
    cot_ref,
    gain_ref,
    shift_ref,
    stats_ref,
    out_ref,
):
    frames, rows, _, _ = cot_ref.shape
    me = lax.axis_index("tm")
    got = got_ref[...]
    here = per_device_sums(got, time_devices, height_devices, False)
    earlier = per_device_sums(got, time_devices, height_devices, True)
    group = group_matrix(frames)
    lane = iota(here.shape, 1) % frames
    for f in range(frames):
        sums = exact_dot(earlier + jnp.where(lane <= f, here, 0.0), group)
        count = counts(f, frames, time_devices, per_frame)
        mean = sums[:time_devices] / count
        variance = sums[time_devices:] / count - mean * mean
        at = 2 * f * time_devices
        stats_ref[at : at + time_devices] = mean
        stats_ref[at + time_devices : at + 2 * time_devices] = lax.rsqrt(variance + EPS)
    gain, shift = gain_ref[...], shift_ref[...]
    step = 4
    firsts, seconds = [], []
    for f in range(frames):
        mean = stats_ref[pl.ds(2 * f * time_devices + me, 1)]
        inv_std = stats_ref[pl.ds((2 * f + 1) * time_devices + me, 1)]

        def some(i, sums, f=f, mean=mean, inv_std=inv_std):
            normed = (flat(mixed_ref[f, pl.ds(1 + i * step, step)]) - mean) * inv_std
            pre = normed * gain + shift
            sigma = sigmoid(pre)
            cot = flat(cot_ref[f, pl.ds(i * step, step)]).astype(jnp.float32)
            grad = cot * (sigma * (1.0 + pre * (1.0 - sigma)))
            split = (-1, 8, TILE)
            return (
                sums[0] + grad.reshape(split).sum(0),
                sums[1] + (grad * normed).reshape(split).sum(0),
            )

        zero = jnp.zeros((8, TILE), jnp.float32)
        a, b = lax.fori_loop(0, rows // step, some, (zero, zero), unroll=2)
        firsts.append(a.sum(0, keepdims=True))
        seconds.append(b.sum(0, keepdims=True))
    put_payload(out_ref, [a * gain for a in firsts], [b * gain for b in seconds])
    total_a, total_b = sum(firsts[1:], firsts[0]), sum(seconds[1:], seconds[0])
    at = 2 * frames * time_devices
    stats_ref[at : at + 16] = jnp.where(iota((16, TILE), 0) < 8, total_b, total_a)


def sigmoid(value):
    return 0.5 + 0.5 * jnp.tanh(0.5 * value)


def normalised(mixed, mean, inv_std, gain, shift):
    pre = (mixed - mean) * inv_std * gain + shift
    return pre, sigmoid(pre)


def write_outputs(time_devices, stats_ref, mixed_ref, x_ref, gain_ref, shift_ref, outputs_ref):
    frames, rows, columns, _ = x_ref.shape
    me = lax.axis_index("tm")
    gain, shift = gain_ref[...], shift_ref[...]
    step = 4
    for f in range(frames):
        mean = stats_ref[pl.ds(2 * f * time_devices + me, 1)]
        inv_std = stats_ref[pl.ds((2 * f + 1) * time_devices + me, 1)]

        def some(i, _, f=f, mean=mean, inv_std=inv_std):
            at = pl.ds(i * step, step)
            mixed = flat(mixed_ref[f, pl.ds(1 + i * step, step)])
            pre, sigma = normalised(mixed, mean, inv_std, gain, shift)
            kept = flat(x_ref[f, at]).astype(jnp.float32) + pre * sigma
            outputs_ref[f, at] = kept.astype(jnp.bfloat16).reshape(step, columns, TILE)
            return 0

        lax.fori_loop(0, rows // step, some, 0, unroll=2)


def mixed_grads(
    time_devices,
    stats_ref,
    gain_ref,
    shift_ref,
    mixed_hbm,
    mixed_next_hbm,
    cot_hbm,
    before_hbm,
    after_hbm,
    next_hbm,
    scaled_hbm,
    scaled_ref,
    mixed_ref,
    cot_ref,
    before_ref,
    after_ref,
    in_sems,
    out_sems,
):
    frames, rows, columns, _ = cot_hbm.shape
    pairs = [
        (before_hbm.at[pl.ds(frames, frames)], before_ref),
        (after_hbm.at[pl.ds(frames, frames)], after_ref),
    ]
    for f in range(frames + 2):
        own = f < frames
        pairs.append((mixed_hbm.at[f] if own else mixed_next_hbm.at[f - frames], mixed_ref.at[f]))
        if own:
            pairs.append((cot_hbm.at[f], cot_ref.at[f, pl.ds(2, rows)]))
        else:
            pairs.append((next_hbm.at[2 + f - frames], cot_ref.at[f]))
    copies = fetch(pairs, in_sems)
    me = lax.axis_index("tm")
    following = jnp.minimum(me + 1, time_devices - 1)
    gain, shift = gain_ref[...], shift_ref[...]
    step = 4

    def grads(mixed, cot, mean, inv_std):
        pre, sigma = normalised(mixed, mean, inv_std, gain, shift)
        grad = cot.astype(jnp.float32) * (sigma * (1.0 + pre * (1.0 - sigma)))
        return inv_std * (grad * gain)

    leaving = []
    copies[0].wait()
    copies[1].wait()
    for f in range(frames + 2):
        own = f < frames
        at, g = (me, f) if own else (following, f - frames)
        mean = stats_ref[pl.ds(2 * g * time_devices + at, 1)]
        inv_std = stats_ref[pl.ds((2 * g + 1) * time_devices + at, 1)]
        copies[2 + 2 * f].wait()
        copies[3 + 2 * f].wait()

        def some(i, _, f=f, mean=mean, inv_std=inv_std):
            here = pl.ds(1 + i * step, step)
            cot = flat(cot_ref[f, pl.ds(2 + i * step, step)])
            scaled = grads(flat(mixed_ref[f, here]), cot, mean, inv_std)
            scaled_ref[f, here] = scaled.reshape(step, columns, TILE)
            return 0

        lax.fori_loop(0, rows // step, some, 0, unroll=2)
        top = before_ref[f, 1] if own else cot_ref[f, 1]
        bottom = after_ref[f, 0] if own else cot_ref[f, rows + 2]
        for row, cot in ((0, top), (rows + 1, bottom)):
            scaled_ref[f, row] = grads(mixed_ref[f, row], cot, mean, inv_std)
        copy = pltpu.make_async_copy(scaled_ref.at[f], scaled_hbm.at[f], out_sems.at[f])
        copy.start()
        leaving.append(copy)
    for copy in leaving:
        copy.wait()


def parameter_grads(
    time_devices,
    height_devices,
    per_frame,
    got_ref,
    stats_ref,
    mixed_hbm,
    mixed_next_hbm,
    scaled_hbm,
    xt_hbm,
    ft_hbm,
    temporal_hbm,
    out_ref,
    feature_grad_hbm,
    carry_ref,
    mixed_grad_ref,
    feature_grad_ref,
    mixed_ref,
    scaled_ref,
    xt_ref,
    ft_ref,
    temporal_ref,
    shifted_ref,
    sems,
    out_sems,
):
    frames, ext, columns, _ = feature_grad_ref.shape
    rows = ext - 2
    copies = fetch(
        [
            (mixed_hbm.at[f] if f < frames else mixed_next_hbm.at[f - frames], mixed_ref.at[f])
            if kind
            else (scaled_hbm.at[f], scaled_ref.at[f])
            for f in range(frames + 2)
            for kind in range(2)
        ]
        + [(temporal_hbm, temporal_ref), (ft_hbm, ft_ref), (xt_hbm, xt_ref)],
        sems,
    )
    last = 2 * (frames + 2)
    me, level = lax.axis_index("tm"), lax.axis_index("height")
    following = jnp.minimum(me + 1, time_devices - 1)
    here = per_device_sums(got_ref[...], time_devices, height_devices, False)
    group = group_matrix(frames)
    lane = iota(here.shape, 1) % frames
    firsts, seconds = [], []
    for f in range(frames):
        sums = exact_dot(jnp.where(lane == f, here, 0.0), group)
        sum_a, sum_b = sums[:time_devices], sums[time_devices:]
        at = 2 * f * time_devices
        mean = stats_ref[at : at + time_devices]
        inv_std = stats_ref[at + time_devices : at + 2 * time_devices]
        count = counts(f, frames, time_devices, per_frame)
        firsts.append((-inv_std * sum_a + inv_std * inv_std * sum_b * mean) / count)
        seconds.append(-inv_std * inv_std * sum_b / (2.0 * count))
    square = (time_devices, time_devices)
    later = (iota(square, 1) > iota(square, 0)).astype(jnp.float32)
    for kind, values in enumerate((firsts, seconds)):
        run = exact_dot(later, sum(values[1:], values[0]))
        for f in range(frames - 1, -1, -1):
            run = run + values[f]
            at = (2 * f + kind) * time_devices
            carry_ref[at : at + time_devices] = run
    exists = (me < time_devices - 1).astype(jnp.float32)
    for f in range(frames + 2):
        own = f < frames
        at, g = (me, f) if own else (following, f - frames)
        first = carry_ref[pl.ds(2 * g * time_devices + at, 1)]
        second = 2.0 * carry_ref[pl.ds((2 * g + 1) * time_devices + at, 1)]
        copies[2 * f].wait()
        copies[2 * f + 1].wait()

        def some(i, _, f=f, own=own, first=first, second=second):
            at = pl.ds(i * 3, 3)
            grad = flat(scaled_ref[f, at]) + first + flat(mixed_ref[f, at]) * second
            if not own:
                grad = grad * exists
            mixed_grad_ref[f, at] = grad.astype(jnp.bfloat16).reshape(3, columns, TILE)
            return 0

        lax.fori_loop(0, ext // 3, some, 0, unroll=3)
    copies[last].wait()
    back = jnp.concatenate([temporal_ref[k] for k in range(3)], axis=1)
    leaving = []
    place = iota((ext * columns, TILE), 0) // columns
    outside = ((place == 0) & (level == 0)) | ((place == ext - 1) & (level == height_devices - 1))
    size = rows * columns
    for f in range(frames):
        blocks = [flat(mixed_grad_ref[f + 2 - k]) for k in range(3)]
        grad = dot(jnp.concatenate(blocks, axis=1), back, True)
        grad = jnp.where(outside, 0.0, grad).astype(jnp.bfloat16)
        feature_grad_ref[f] = grad.reshape(ext, columns, TILE)
        copy = pltpu.make_async_copy(
            feature_grad_ref.at[f], feature_grad_hbm.at[f], out_sems.at[f]
        )
        copy.start()
        leaving.append(copy)
        inner = grad[columns : (rows + 1) * columns]
        wide = inner.astype(jnp.float32)
        shifted_ref[f * size : (f + 1) * size] = jnp.concatenate(
            [
                moved(wide, -1, columns).astype(jnp.bfloat16),
                inner,
                moved(wide, 1, columns).astype(jnp.bfloat16),
            ],
            axis=1,
        )
    for copy in copies[last + 1 :]:
        copy.wait()
    inner = flat(mixed_grad_ref[:frames, 1 : rows + 1])
    temporal = [dot(ft_ref[:, k * size : (k + frames) * size], inner) for k in range(3)]
    spatial = dot(xt_ref[...], shifted_ref[...])
    pieces = out_ref.shape[0]
    piece = 12 * TILE // pieces
    blocks = [spatial[:, j * TILE : (j + 1) * TILE] for j in range(3)] + temporal
    whole = jnp.concatenate(blocks, axis=0).astype(jnp.bfloat16)
    for p in range(pieces):
        out_ref[p, :piece] = whole[p * piece : (p + 1) * piece]
        at = 2 * frames * time_devices + 8 * min(p, 1)
        tail = stats_ref[at : at + 8]
        tail = jnp.where((iota((8, TILE), 0) == 0) & (p < 2), tail, 0.0)
        out_ref[p, piece : piece + 8] = tail.astype(jnp.bfloat16)
    for copy in leaving:
        copy.wait()


def input_grads(grad_ref, cot_ref, spatial_ref, out_ref, weight_ref):
    frames, rows, columns, _ = cot_ref.shape
    for s in range(3):
        for j in range(3):
            weight_ref[j * TILE : (j + 1) * TILE, s * TILE : (s + 1) * TILE] = spatial_ref[2 - s, j]

    def one(f, _):
        out = convolve(flat(grad_ref[f]), weight_ref[...], rows, columns, True)
        out = out + flat(cot_ref[f]).astype(jnp.float32)
        out_ref[f] = out.astype(jnp.bfloat16).reshape(out_ref.shape[1:])
        return 0

    lax.fori_loop(0, frames, one, 0)


def sum_and_copy(got_ref, out_ref):
    total = got_ref[0].astype(jnp.float32)
    for i in range(1, got_ref.shape[0]):
        total = total + got_ref[i].astype(jnp.float32)
    total = total.astype(jnp.bfloat16)
    for i in range(out_ref.shape[0]):
        out_ref[i] = total


def finish(scale, got_ref, spatial_ref, temporal_ref, gain_ref, shift_ref):
    pieces, piece = got_ref.shape[0], got_ref.shape[1] - 8
    for p in range(pieces):
        value = got_ref[p].astype(jnp.float32) * scale
        if p < 2:
            (gain_ref, shift_ref)[p][...] = value[piece : piece + 1]
        at = p * piece
        while at < (p + 1) * piece:
            block, row = at // TILE, at % TILE
            size = min(TILE - row, (p + 1) * piece - at)
            part = value[at - p * piece : at - p * piece + size]
            if block < 9:
                spatial_ref[block % 3, block // 3, row : row + size] = part
            else:
                temporal_ref[block - 9, row : row + size] = part
            at += size


def call(body, outs, args, scratch=(), flops=0, far=(), far_outs=(), limit=WIDE):
    everything = (*args, *far, *outs, *far_outs)
    moved_bytes = sum(a.size * a.dtype.itemsize for a in everything)
    near, away = pl.BlockSpec(memory_space=pltpu.VMEM), pl.BlockSpec(memory_space=pl.ANY)
    return pl.pallas_call(
        body,
        out_shape=[*outs, *far_outs],
        in_specs=[near] * len(args) + [away] * len(far),
        out_specs=[near] * len(outs) + [away] * len(far_outs),
        scratch_shapes=list(scratch),
        compiler_params=pltpu.CompilerParams(vmem_limit_bytes=limit * 1024 * 1024),
        cost_estimate=pl.CostEstimate(
            flops=flops, bytes_accessed=moved_bytes, transcendentals=0
        ),
    )(*args, *far)


def shards(inputs, spatial_kernel, temporal_kernel, norm_gain, norm_shift, cotangent):
    x, cot = inputs[0], cotangent[0]
    frames, rows, columns, channels = x.shape
    ext = rows + 2
    reps, time_devices, height_devices = (lax.axis_size(a) for a in ("rep", "tm", "height"))
    per_frame = float(rows * height_devices * columns * (channels // GROUPS))
    bf16, f32 = jnp.bfloat16, jnp.float32
    out = jax.ShapeDtypeStruct
    frame = (columns, channels)
    gain, shift = norm_gain[None], norm_shift[None]
    weight = pltpu.VMEM((3 * channels, 3 * channels), bf16)
    conv = 2 * 9 * channels * channels * columns

    up = [(i, i + 1) for i in range(height_devices - 1)]
    down = [(j, i) for i, j in up]
    before = lax.ppermute(jnp.concatenate([x[:, rows - 2 :], cot[:, rows - 2 :]], 0), "height", up)
    after = lax.ppermute(jnp.concatenate([x[:, :2], cot[:, :2]], 0), "height", down)
    onward = [(i, i + 1) for i in range(time_devices - 1)]
    back = [(j, i) for i, j in onward]
    last = jnp.concatenate([before[2:4], x[2:4], after[2:4]], 1)
    prev = lax.ppermute(last, "tm", onward)
    first = jnp.concatenate(
        [
            jnp.concatenate([before[:2], before[4:6]], 0),
            jnp.concatenate([x[:2], cot[:2]], 0),
            jnp.concatenate([after[:2], after[4:6]], 0),
        ],
        1,
    )
    following = lax.ppermute(first, "tm", back)

    dma = lambda count: pltpu.SemaphoreType.DMA((count,))
    turned_x = out((3 * channels, frames * rows * columns), bf16)
    turned_features = out((channels, (frames + 2) * rows * columns), bf16)
    held = lambda a: pltpu.VMEM(a.shape, a.dtype)
    two = out((2, ext) + frame, bf16)
    own_two = out((frames, ext) + frame, bf16)
    feature, late = call(
        own_features,
        [own_two],
        (x, before, after, spatial_kernel),
        [weight, dma(1)],
        conv * frames * ext,
        far_outs=[own_two],
        limit=NARROW,
    )
    peers = time_devices * height_devices
    mixed, payload = call(
        mixed_and_sums,
        [out((frames, ext) + frame, f32), out((2 * peers, channels), f32)],
        (feature, prev, spatial_kernel, temporal_kernel),
        [weight, held(two)],
        conv * frames * ext,
        limit=NARROW,
    )
    share = ("tm", "height")
    got = lax.all_to_all(payload, share, 0, 0, tiled=True)
    xt, ft = call(
        turn,
        [turned_x, turned_features],
        (x, before, after, prev, late, spatial_kernel),
        [weight, held(two)],
        conv * frames * ext,
    )
    (mixed_next,) = call(
        next_frames,
        [out((2, ext) + frame, f32)],
        (),
        [
            weight,
            held(two),
            pltpu.VMEM((2, rows + 4) + frame, bf16),
            held(two),
            held(spatial_kernel),
            held(temporal_kernel),
            dma(4),
        ],
        conv * 2 * ext,
        far=(following, late, spatial_kernel, temporal_kernel),
        limit=FULL,
    )
    stats, payload = call(
        functools.partial(statistics_and_sums, time_devices, height_devices, per_frame),
        [
            out((2 * frames * time_devices + 16, channels), f32),
            out((2 * peers, channels), f32),
        ],
        (got, mixed, cot, gain, shift),
        limit=NARROW,
    )
    got = lax.all_to_all(payload, share, 0, 0, tiled=True)
    scaled_shape = out((frames + 2, ext) + frame, f32)
    (scaled,) = call(
        functools.partial(mixed_grads, time_devices),
        [],
        (stats, gain, shift),
        [
            held(scaled_shape),
            held(scaled_shape),
            pltpu.VMEM((frames + 2, rows + 4) + frame, bf16),
            pltpu.VMEM((frames, 2) + frame, bf16),
            pltpu.VMEM((frames, 2) + frame, bf16),
            dma(2 * frames + 6),
            dma(frames + 2),
        ],
        far=(mixed, mixed_next, cot, before, after, following),
        far_outs=[scaled_shape],
    )
    (outputs,) = call(
        functools.partial(write_outputs, time_devices),
        [out((frames, rows) + frame, bf16)],
        (stats, mixed, x, gain, shift),
    )
    ends = ("rep", "height")
    pieces = reps * height_devices
    partial, feature_grad = call(
        functools.partial(parameter_grads, time_devices, height_devices, per_frame),
        [out((pieces, 12 * TILE // pieces + 8, channels), bf16)],
        (got, stats),
        [
            pltpu.VMEM((2 * frames * time_devices, channels), f32),
            pltpu.VMEM((frames + 2, ext) + frame, bf16),
            held(own_two),
            held(scaled_shape),
            held(scaled_shape),
            held(turned_x),
            held(turned_features),
            held(temporal_kernel),
            pltpu.VMEM((frames * rows * columns, 3 * channels), bf16),
            dma(2 * frames + 7),
            dma(frames),
        ],
        conv * frames * rows * 2,
        far=(mixed, mixed_next, scaled, xt, ft, temporal_kernel),
        far_outs=[own_two],
    )
    partial = lax.all_to_all(partial, ends, 0, 0, tiled=True)
    (grad_inputs,) = call(
        input_grads,
        [out((frames, rows) + frame, bf16)],
        (feature_grad, cot, spatial_kernel),
        [weight],
        conv * frames * rows,
    )
    piece = partial.shape[1:]
    (partial,) = call(sum_and_copy, [out((time_devices,) + piece, bf16)], (partial,), limit=NARROW)
    partial = lax.all_to_all(partial, "tm", 0, 0, tiled=True)
    (partial,) = call(sum_and_copy, [out((pieces,) + piece, bf16)], (partial,), limit=NARROW)
    sums = lax.all_to_all(partial, ends, 0, 0, tiled=True)
    pixel_total = reps * frames * time_devices * rows * height_devices * columns
    spatial_sum, temporal_sum, gain_sum, shift_sum = call(
        functools.partial(finish, 1.0 / math.sqrt(pixel_total)),
        [
            out(spatial_kernel.shape, f32),
            out(temporal_kernel.shape, f32),
            out((1, channels), f32),
            out((1, channels), f32),
        ],
        (sums,),
        limit=NARROW,
    )
    return (
        outputs[None],
        grad_inputs[None],
        spatial_sum,
        temporal_sum,
        gain_sum[0],
        shift_sum[0],
    )


def solution(mesh):
    in_specs = (
        P("rep", "tm", "height", None, None),
        P(),
        P(),
        P(),
        P(),
        P("rep", "tm", "height", None, None),
    )
    out_specs = (
        P("rep", "tm", "height", None, None),
        P("rep", "tm", "height", None, None),
        P(),
        P(),
        P(),
        P(),
    )
    return jax.shard_map(shards, mesh=mesh, in_specs=in_specs, out_specs=out_specs, check_vma=False)
```

```python
import functools
import math

import jax
import jax.numpy as jnp
from jax import lax
from jax.experimental import pallas as pl
from jax.experimental.pallas import tpu as pltpu
from jax.sharding import PartitionSpec as P

GROUPS = 32


EPS = 1e-05
TILE = 128
FULL, WIDE, NARROW = 58, 53, 16


def iota(shape, dim):
    return lax.broadcasted_iota(jnp.int32, shape, dim)


def exact_dot(a, b):
    return lax.dot_general(
        a,
        b,
        (((1,), (0,)), ((), ())),
        precision=lax.Precision.HIGHEST,
        preferred_element_type=jnp.float32,
    )


def dot(a, b, turned=False):
    return lax.dot_general(
        a,
        b,
        (((1,), (1 if turned else 0,)), ((), ())),
        preferred_element_type=jnp.float32,
    )


def group_matrix(size):
    return (iota((TILE, TILE), 0) // size == iota((TILE, TILE), 1) // size).astype(jnp.float32)


def per_device_sums(got, time_devices, height_devices, earlier):
    shape = (2 * time_devices, got.shape[0])
    row, col = iota(shape, 0), iota(shape, 1)
    at, source = row % time_devices, col // (2 * height_devices)
    keep = (source < at) if earlier else (source == at)
    keep = keep & (row // time_devices == col % 2)
    return exact_dot(keep.astype(jnp.float32), got)


def moved(value, step, columns):
    pixels = value.shape[0]
    rolled = pltpu.roll(value, step % pixels, 0)
    place = iota(value.shape, 0) % columns
    edge = 0 if step > 0 else columns - 1
    return jnp.where(place == edge, 0.0, rolled)


def three_rows(block, rows, columns):
    size = rows * columns
    return jnp.concatenate(
        [block[i * columns : i * columns + size] for i in range(3)], axis=1
    )


def convolve(block, weight, rows, columns, turned):
    taps = dot(three_rows(block, rows, columns), weight, turned)
    c = taps.shape[1] // 3
    sign = -1 if turned else 1
    return (
        taps[:, c : 2 * c]
        + moved(taps[:, :c], sign, columns)
        + moved(taps[:, 2 * c :], -sign, columns)
    )


def flat(value):
    return value.reshape(-1, value.shape[-1])


def put_weight(weight_ref, spatial_ref):
    for i in range(3):
        for j in range(3):
            weight_ref[i * TILE : (i + 1) * TILE, j * TILE : (j + 1) * TILE] = spatial_ref[i, j]


def put_payload(out_ref, firsts, seconds):
    frames = len(firsts)
    sums = exact_dot(jnp.concatenate(firsts + seconds, 0), group_matrix(frames))
    lane = iota((1, TILE), 1) % frames
    rows = []
    for start in (0, frames):
        line = jnp.zeros((1, TILE), jnp.float32)
        for f in range(frames):
            line = jnp.where(lane == f, sums[start + f : start + f + 1], line)
        rows.append(line)
    line = jnp.where(iota((8, TILE), 0) % 2 == 0, rows[0], rows[1])
    for i in range(out_ref.shape[0] // 8):
        out_ref[i * 8 : (i + 1) * 8] = line


def fetch(pairs, sems):
    copies = [pltpu.make_async_copy(a, b, sems.at[i]) for i, (a, b) in enumerate(pairs)]
    for copy in copies:
        copy.start()
    return copies


def turned(value):
    return value.astype(jnp.float32).T.astype(jnp.bfloat16)


def own_features(
    x_ref, before_ref, after_ref, spatial_ref, feature_ref, far_ref, weight_ref, sems
):
    put_weight(weight_ref, spatial_ref)
    frames, rows, columns, _ = x_ref.shape

    def one(f, _):
        block = jnp.concatenate([flat(before_ref[f]), flat(x_ref[f]), flat(after_ref[f])], 0)
        out = convolve(block, weight_ref[...], rows + 2, columns, False)
        feature_ref[f] = out.astype(jnp.bfloat16).reshape(feature_ref.shape[1:])
        return 0

    lax.fori_loop(0, frames, one, 0)
    for copy in fetch([(feature_ref, far_ref)], sems):
        copy.wait()


def turn(
    x_ref,
    before_ref,
    after_ref,
    prev_ref,
    feature_ref,
    spatial_ref,
    xt_ref,
    ft_ref,
    weight_ref,
    prior_ref,
):
    put_weight(weight_ref, spatial_ref)
    frames, rows, columns, _ = x_ref.shape
    size = rows * columns

    def one(f, _):
        out = convolve(flat(prev_ref[f]), weight_ref[...], rows + 2, columns, False)
        prior_ref[f] = out.astype(jnp.bfloat16).reshape(prior_ref.shape[1:])
        return 0

    lax.fori_loop(0, 2, one, 0)
    for f in range(frames + 2):
        seen = prior_ref[f, 1 : rows + 1] if f < 2 else feature_ref[f - 2, 1 : rows + 1]
        ft_ref[:, f * size : (f + 1) * size] = turned(flat(seen))
    for f in range(frames):
        block = jnp.concatenate(
            [flat(before_ref[f, 1:]), flat(x_ref[f]), flat(after_ref[f, :1])], 0
        )
        xt_ref[:, f * size : (f + 1) * size] = turned(three_rows(block, rows, columns))


def mix(blocks, temporal_ref):
    return dot(jnp.concatenate(blocks, axis=1), flat(temporal_ref[...]))


def mixed_and_sums(
    feature_ref,
    prev_ref,
    spatial_ref,
    temporal_ref,
    mixed_ref,
    out_ref,
    weight_ref,
    prior_ref,
):
    put_weight(weight_ref, spatial_ref)
    frames, rows, columns, _ = mixed_ref.shape

    def one(f, _):
        out = convolve(flat(prev_ref[f]), weight_ref[...], rows, columns, False)
        prior_ref[f] = out.astype(jnp.bfloat16).reshape(prior_ref.shape[1:])
        return 0

    lax.fori_loop(0, 2, one, 0)
    firsts, seconds = [], []
    for f in range(frames):
        blocks = [
            flat(prior_ref[f + k]) if f + k < 2 else flat(feature_ref[f + k - 2]) for k in range(3)
        ]
        out = mix(blocks, temporal_ref)
        mixed_ref[f] = out.reshape(mixed_ref.shape[1:])
        inner = out[columns : (rows - 1) * columns]
        firsts.append(inner.sum(0, keepdims=True))
        seconds.append((inner * inner).sum(0, keepdims=True))
    put_payload(out_ref, firsts, seconds)


def next_frames(
    next_hbm,
    late_hbm,
    spatial_hbm,
    temporal_hbm,
    mixed_ref,
    weight_ref,
    held_ref,
    next_ref,
    late_ref,
    spatial_ref,
    temporal_ref,
    sems,
):
    copies = fetch(
        [
            (spatial_hbm, spatial_ref),
            (next_hbm.at[pl.ds(0, 2)], next_ref),
            (late_hbm.at[pl.ds(late_hbm.shape[0] - 2, 2)], late_ref),
            (temporal_hbm, temporal_ref),
        ],
        sems,
    )
    _, ext, columns, _ = mixed_ref.shape
    copies[0].wait()
    put_weight(weight_ref, spatial_ref)
    copies[1].wait()

    def one(f, _):
        out = convolve(flat(next_ref[f]), weight_ref[...], ext, columns, False)
        held_ref[f] = out.astype(jnp.bfloat16).reshape(held_ref.shape[1:])
        return 0

    lax.fori_loop(0, 2, one, 0)
    copies[2].wait()
    copies[3].wait()
    for f in range(2):
        blocks = [flat(late_ref[f + k]) if f + k < 2 else flat(held_ref[f + k - 2]) for k in range(3)]
        mixed_ref[f] = mix(blocks, temporal_ref).reshape(mixed_ref.shape[1:])


def counts(f, frames, time_devices, per_frame):
    at = iota((time_devices, TILE), 0) * frames + (f + 1)
    return at.astype(jnp.float32) * per_frame


def statistics_and_sums(
    time_devices,
    height_devices,
    per_frame,
    got_ref,
    mixed_ref,
    cot_ref,
    gain_ref,
    shift_ref,
    stats_ref,
    out_ref,
):
    frames, rows, _, _ = cot_ref.shape
    me = lax.axis_index("tm")
    got = got_ref[...]
    here = per_device_sums(got, time_devices, height_devices, False)
    earlier = per_device_sums(got, time_devices, height_devices, True)
    group = group_matrix(frames)
    lane = iota(here.shape, 1) % frames
    for f in range(frames):
        sums = exact_dot(earlier + jnp.where(lane <= f, here, 0.0), group)
        count = counts(f, frames, time_devices, per_frame)
        mean = sums[:time_devices] / count
        variance = sums[time_devices:] / count - mean * mean
        at = 2 * f * time_devices
        stats_ref[at : at + time_devices] = mean
        stats_ref[at + time_devices : at + 2 * time_devices] = lax.rsqrt(variance + EPS)
    gain, shift = gain_ref[...], shift_ref[...]
    step = 4
    firsts, seconds = [], []
    for f in range(frames):
        mean = stats_ref[pl.ds(2 * f * time_devices + me, 1)]
        inv_std = stats_ref[pl.ds((2 * f + 1) * time_devices + me, 1)]

        def some(i, sums, f=f, mean=mean, inv_std=inv_std):
            normed = (flat(mixed_ref[f, pl.ds(1 + i * step, step)]) - mean) * inv_std
            pre = normed * gain + shift
            sigma = sigmoid(pre)
            cot = flat(cot_ref[f, pl.ds(i * step, step)]).astype(jnp.float32)
            grad = cot * (sigma * (1.0 + pre * (1.0 - sigma)))
            split = (-1, 8, TILE)
            return (
                sums[0] + grad.reshape(split).sum(0),
                sums[1] + (grad * normed).reshape(split).sum(0),
            )

        zero = jnp.zeros((8, TILE), jnp.float32)
        a, b = lax.fori_loop(0, rows // step, some, (zero, zero), unroll=4)
        firsts.append(a.sum(0, keepdims=True))
        seconds.append(b.sum(0, keepdims=True))
    put_payload(out_ref, [a * gain for a in firsts], [b * gain for b in seconds])
    total_a, total_b = sum(firsts[1:], firsts[0]), sum(seconds[1:], seconds[0])
    at = 2 * frames * time_devices
    stats_ref[at : at + 16] = jnp.where(iota((16, TILE), 0) < 8, total_b, total_a)


def sigmoid(value):
    return 1.0 / (1.0 + jnp.exp(-value))


def normalised(mixed, mean, inv_std, gain, shift):
    pre = (mixed - mean) * inv_std * gain + shift
    return pre, sigmoid(pre)


def write_outputs(time_devices, stats_ref, mixed_ref, x_ref, gain_ref, shift_ref, outputs_ref):
    frames, rows, columns, _ = x_ref.shape
    me = lax.axis_index("tm")
    gain, shift = gain_ref[...], shift_ref[...]
    step = 4
    for f in range(frames):
        mean = stats_ref[pl.ds(2 * f * time_devices + me, 1)]
        inv_std = stats_ref[pl.ds((2 * f + 1) * time_devices + me, 1)]

        def some(i, _, f=f, mean=mean, inv_std=inv_std):
            at = pl.ds(i * step, step)
            mixed = flat(mixed_ref[f, pl.ds(1 + i * step, step)])
            pre, sigma = normalised(mixed, mean, inv_std, gain, shift)
            kept = flat(x_ref[f, at]).astype(jnp.float32) + pre * sigma
            outputs_ref[f, at] = kept.astype(jnp.bfloat16).reshape(step, columns, TILE)
            return 0

        lax.fori_loop(0, rows // step, some, 0, unroll=2)


def mixed_grads(
    time_devices,
    stats_ref,
    gain_ref,
    shift_ref,
    mixed_hbm,
    mixed_next_hbm,
    cot_hbm,
    before_hbm,
    after_hbm,
    next_hbm,
    scaled_hbm,
    scaled_ref,
    mixed_ref,
    cot_ref,
    before_ref,
    after_ref,
    in_sems,
    out_sems,
):
    frames, rows, columns, _ = cot_hbm.shape
    pairs = [
        (before_hbm.at[pl.ds(frames, frames)], before_ref),
        (after_hbm.at[pl.ds(frames, frames)], after_ref),
    ]
    for f in range(frames + 2):
        own = f < frames
        pairs.append((mixed_hbm.at[f] if own else mixed_next_hbm.at[f - frames], mixed_ref.at[f]))
        if own:
            pairs.append((cot_hbm.at[f], cot_ref.at[f, pl.ds(2, rows)]))
        else:
            pairs.append((next_hbm.at[2 + f - frames], cot_ref.at[f]))
    copies = fetch(pairs, in_sems)
    me = lax.axis_index("tm")
    following = jnp.minimum(me + 1, time_devices - 1)
    gain, shift = gain_ref[...], shift_ref[...]
    step = 4

    def grads(mixed, cot, mean, inv_std):
        pre, sigma = normalised(mixed, mean, inv_std, gain, shift)
        grad = cot.astype(jnp.float32) * (sigma * (1.0 + pre * (1.0 - sigma)))
        return inv_std * (grad * gain)

    leaving = []
    copies[0].wait()
    copies[1].wait()
    for f in range(frames + 2):
        own = f < frames
        at, g = (me, f) if own else (following, f - frames)
        mean = stats_ref[pl.ds(2 * g * time_devices + at, 1)]
        inv_std = stats_ref[pl.ds((2 * g + 1) * time_devices + at, 1)]
        copies[2 + 2 * f].wait()
        copies[3 + 2 * f].wait()

        def some(i, _, f=f, mean=mean, inv_std=inv_std):
            here = pl.ds(1 + i * step, step)
            cot = flat(cot_ref[f, pl.ds(2 + i * step, step)])
            scaled = grads(flat(mixed_ref[f, here]), cot, mean, inv_std)
            scaled_ref[f, here] = scaled.reshape(step, columns, TILE)
            return 0

        lax.fori_loop(0, rows // step, some, 0, unroll=2)
        top = before_ref[f, 1] if own else cot_ref[f, 1]
        bottom = after_ref[f, 0] if own else cot_ref[f, rows + 2]
        for row, cot in ((0, top), (rows + 1, bottom)):
            scaled_ref[f, row] = grads(mixed_ref[f, row], cot, mean, inv_std)
        copy = pltpu.make_async_copy(scaled_ref.at[f], scaled_hbm.at[f], out_sems.at[f])
        copy.start()
        leaving.append(copy)
    for copy in leaving:
        copy.wait()


def parameter_grads(
    time_devices,
    height_devices,
    per_frame,
    got_ref,
    stats_ref,
    mixed_hbm,
    mixed_next_hbm,
    scaled_hbm,
    xt_hbm,
    ft_hbm,
    temporal_hbm,
    out_ref,
    feature_grad_hbm,
    carry_ref,
    mixed_grad_ref,
    feature_grad_ref,
    mixed_ref,
    scaled_ref,
    xt_ref,
    ft_ref,
    temporal_ref,
    shifted_ref,
    sems,
    out_sems,
):
    frames, ext, columns, _ = feature_grad_ref.shape
    rows = ext - 2
    copies = fetch(
        [
            (mixed_hbm.at[f] if f < frames else mixed_next_hbm.at[f - frames], mixed_ref.at[f])
            if kind
            else (scaled_hbm.at[f], scaled_ref.at[f])
            for f in range(frames + 2)
            for kind in range(2)
        ]
        + [(temporal_hbm, temporal_ref), (ft_hbm, ft_ref), (xt_hbm, xt_ref)],
        sems,
    )
    last = 2 * (frames + 2)
    me, level = lax.axis_index("tm"), lax.axis_index("height")
    following = jnp.minimum(me + 1, time_devices - 1)
    here = per_device_sums(got_ref[...], time_devices, height_devices, False)
    group = group_matrix(frames)
    lane = iota(here.shape, 1) % frames
    firsts, seconds = [], []
    for f in range(frames):
        sums = exact_dot(jnp.where(lane == f, here, 0.0), group)
        sum_a, sum_b = sums[:time_devices], sums[time_devices:]
        at = 2 * f * time_devices
        mean = stats_ref[at : at + time_devices]
        inv_std = stats_ref[at + time_devices : at + 2 * time_devices]
        count = counts(f, frames, time_devices, per_frame)
        firsts.append((-inv_std * sum_a + inv_std * inv_std * sum_b * mean) / count)
        seconds.append(-inv_std * inv_std * sum_b / (2.0 * count))
    square = (time_devices, time_devices)
    later = (iota(square, 1) > iota(square, 0)).astype(jnp.float32)
    for kind, values in enumerate((firsts, seconds)):
        run = exact_dot(later, sum(values[1:], values[0]))
        for f in range(frames - 1, -1, -1):
            run = run + values[f]
            at = (2 * f + kind) * time_devices
            carry_ref[at : at + time_devices] = run
    exists = (me < time_devices - 1).astype(jnp.float32)
    for f in range(frames + 2):
        own = f < frames
        at, g = (me, f) if own else (following, f - frames)
        first = carry_ref[pl.ds(2 * g * time_devices + at, 1)]
        second = 2.0 * carry_ref[pl.ds((2 * g + 1) * time_devices + at, 1)]
        copies[2 * f].wait()
        copies[2 * f + 1].wait()

        def some(i, _, f=f, own=own, first=first, second=second):
            at = pl.ds(i * 3, 3)
            grad = flat(scaled_ref[f, at]) + first + flat(mixed_ref[f, at]) * second
            if not own:
                grad = grad * exists
            mixed_grad_ref[f, at] = grad.astype(jnp.bfloat16).reshape(3, columns, TILE)
            return 0

        lax.fori_loop(0, ext // 3, some, 0, unroll=6)
    copies[last].wait()
    back = jnp.concatenate([temporal_ref[k] for k in range(3)], axis=1)
    leaving = []
    place = iota((ext * columns, TILE), 0) // columns
    outside = ((place == 0) & (level == 0)) | ((place == ext - 1) & (level == height_devices - 1))
    size = rows * columns
    for f in range(frames):
        blocks = [flat(mixed_grad_ref[f + 2 - k]) for k in range(3)]
        grad = dot(jnp.concatenate(blocks, axis=1), back, True)
        grad = jnp.where(outside, 0.0, grad).astype(jnp.bfloat16)
        feature_grad_ref[f] = grad.reshape(ext, columns, TILE)
        copy = pltpu.make_async_copy(
            feature_grad_ref.at[f], feature_grad_hbm.at[f], out_sems.at[f]
        )
        copy.start()
        leaving.append(copy)
        inner = grad[columns : (rows + 1) * columns]
        wide = inner.astype(jnp.float32)
        shifted_ref[f * size : (f + 1) * size] = jnp.concatenate(
            [
                moved(wide, -1, columns).astype(jnp.bfloat16),
                inner,
                moved(wide, 1, columns).astype(jnp.bfloat16),
            ],
            axis=1,
        )
    for copy in copies[last + 1 :]:
        copy.wait()
    inner = flat(mixed_grad_ref[:frames, 1 : rows + 1])
    temporal = [dot(ft_ref[:, k * size : (k + frames) * size], inner) for k in range(3)]
    spatial = dot(xt_ref[...], shifted_ref[...])
    pieces = out_ref.shape[0]
    piece = 12 * TILE // pieces
    blocks = [spatial[:, j * TILE : (j + 1) * TILE] for j in range(3)] + temporal
    whole = jnp.concatenate(blocks, axis=0).astype(jnp.bfloat16)
    for p in range(pieces):
        out_ref[p, :piece] = whole[p * piece : (p + 1) * piece]
        at = 2 * frames * time_devices + 8 * min(p, 1)
        tail = stats_ref[at : at + 8]
        tail = jnp.where((iota((8, TILE), 0) == 0) & (p < 2), tail, 0.0)
        out_ref[p, piece : piece + 8] = tail.astype(jnp.bfloat16)
    for copy in leaving:
        copy.wait()


def input_grads(grad_ref, cot_ref, spatial_ref, out_ref, weight_ref):
    frames, rows, columns, _ = cot_ref.shape
    for s in range(3):
        for j in range(3):
            weight_ref[j * TILE : (j + 1) * TILE, s * TILE : (s + 1) * TILE] = spatial_ref[2 - s, j]

    def one(f, _):
        out = convolve(flat(grad_ref[f]), weight_ref[...], rows, columns, True)
        out = out + flat(cot_ref[f]).astype(jnp.float32)
        out_ref[f] = out.astype(jnp.bfloat16).reshape(out_ref.shape[1:])
        return 0

    lax.fori_loop(0, frames, one, 0)


def sum_and_copy(got_ref, out_ref):
    total = got_ref[0].astype(jnp.float32)
    for i in range(1, got_ref.shape[0]):
        total = total + got_ref[i].astype(jnp.float32)
    total = total.astype(jnp.bfloat16)
    for i in range(out_ref.shape[0]):
        out_ref[i] = total


def finish(scale, got_ref, spatial_ref, temporal_ref, gain_ref, shift_ref):
    pieces, piece = got_ref.shape[0], got_ref.shape[1] - 8
    for p in range(pieces):
        value = got_ref[p].astype(jnp.float32) * scale
        if p < 2:
            (gain_ref, shift_ref)[p][...] = value[piece : piece + 1]
        at = p * piece
        while at < (p + 1) * piece:
            block, row = at // TILE, at % TILE
            size = min(TILE - row, (p + 1) * piece - at)
            part = value[at - p * piece : at - p * piece + size]
            if block < 9:
                spatial_ref[block % 3, block // 3, row : row + size] = part
            else:
                temporal_ref[block - 9, row : row + size] = part
            at += size


def call(body, outs, args, scratch=(), flops=0, far=(), far_outs=(), limit=WIDE):
    everything = (*args, *far, *outs, *far_outs)
    moved_bytes = sum(a.size * a.dtype.itemsize for a in everything)
    near, away = pl.BlockSpec(memory_space=pltpu.VMEM), pl.BlockSpec(memory_space=pl.ANY)
    return pl.pallas_call(
        body,
        out_shape=[*outs, *far_outs],
        in_specs=[near] * len(args) + [away] * len(far),
        out_specs=[near] * len(outs) + [away] * len(far_outs),
        scratch_shapes=list(scratch),
        compiler_params=pltpu.CompilerParams(vmem_limit_bytes=limit * 1024 * 1024),
        cost_estimate=pl.CostEstimate(
            flops=flops, bytes_accessed=moved_bytes, transcendentals=0
        ),
    )(*args, *far)


def shards(inputs, spatial_kernel, temporal_kernel, norm_gain, norm_shift, cotangent):
    x, cot = inputs[0], cotangent[0]
    frames, rows, columns, channels = x.shape
    ext = rows + 2
    reps, time_devices, height_devices = (lax.axis_size(a) for a in ("rep", "tm", "height"))
    per_frame = float(rows * height_devices * columns * (channels // GROUPS))
    bf16, f32 = jnp.bfloat16, jnp.float32
    out = jax.ShapeDtypeStruct
    frame = (columns, channels)
    gain, shift = norm_gain[None], norm_shift[None]
    weight = pltpu.VMEM((3 * channels, 3 * channels), bf16)
    conv = 2 * 9 * channels * channels * columns

    up = [(i, i + 1) for i in range(height_devices - 1)]
    down = [(j, i) for i, j in up]
    before = lax.ppermute(jnp.concatenate([x[:, rows - 2 :], cot[:, rows - 2 :]], 0), "height", up)
    after = lax.ppermute(jnp.concatenate([x[:, :2], cot[:, :2]], 0), "height", down)
    onward = [(i, i + 1) for i in range(time_devices - 1)]
    back = [(j, i) for i, j in onward]
    last = jnp.concatenate([before[2:4], x[2:4], after[2:4]], 1)
    prev = lax.ppermute(last, "tm", onward)
    first = jnp.concatenate(
        [
            jnp.concatenate([before[:2], before[4:6]], 0),
            jnp.concatenate([x[:2], cot[:2]], 0),
            jnp.concatenate([after[:2], after[4:6]], 0),
        ],
        1,
    )
    following = lax.ppermute(first, "tm", back)

    dma = lambda count: pltpu.SemaphoreType.DMA((count,))
    turned_x = out((3 * channels, frames * rows * columns), bf16)
    turned_features = out((channels, (frames + 2) * rows * columns), bf16)
    held = lambda a: pltpu.VMEM(a.shape, a.dtype)
    two = out((2, ext) + frame, bf16)
    own_two = out((frames, ext) + frame, bf16)
    feature, late = call(
        own_features,
        [own_two],
        (x, before, after, spatial_kernel),
        [weight, dma(1)],
        conv * frames * ext,
        far_outs=[own_two],
        limit=NARROW,
    )
    peers = time_devices * height_devices
    mixed, payload = call(
        mixed_and_sums,
        [out((frames, ext) + frame, f32), out((2 * peers, channels), f32)],
        (feature, prev, spatial_kernel, temporal_kernel),
        [weight, held(two)],
        conv * frames * ext,
        limit=NARROW,
    )
    share = ("tm", "height")
    got = lax.all_to_all(payload, share, 0, 0, tiled=True)
    xt, ft = call(
        turn,
        [turned_x, turned_features],
        (x, before, after, prev, late, spatial_kernel),
        [weight, held(two)],
        conv * frames * ext,
    )
    (mixed_next,) = call(
        next_frames,
        [out((2, ext) + frame, f32)],
        (),
        [
            weight,
            held(two),
            pltpu.VMEM((2, rows + 4) + frame, bf16),
            held(two),
            held(spatial_kernel),
            held(temporal_kernel),
            dma(4),
        ],
        conv * 2 * ext,
        far=(following, late, spatial_kernel, temporal_kernel),
        limit=FULL,
    )
    stats, payload = call(
        functools.partial(statistics_and_sums, time_devices, height_devices, per_frame),
        [
            out((2 * frames * time_devices + 16, channels), f32),
            out((2 * peers, channels), f32),
        ],
        (got, mixed, cot, gain, shift),
        limit=NARROW,
    )
    got = lax.all_to_all(payload, share, 0, 0, tiled=True)
    scaled_shape = out((frames + 2, ext) + frame, f32)
    (scaled,) = call(
        functools.partial(mixed_grads, time_devices),
        [],
        (stats, gain, shift),
        [
            held(scaled_shape),
            held(scaled_shape),
            pltpu.VMEM((frames + 2, rows + 4) + frame, bf16),
            pltpu.VMEM((frames, 2) + frame, bf16),
            pltpu.VMEM((frames, 2) + frame, bf16),
            dma(2 * frames + 6),
            dma(frames + 2),
        ],
        far=(mixed, mixed_next, cot, before, after, following),
        far_outs=[scaled_shape],
    )
    (outputs,) = call(
        functools.partial(write_outputs, time_devices),
        [out((frames, rows) + frame, bf16)],
        (stats, mixed, x, gain, shift),
    )
    ends = ("rep", "height")
    pieces = reps * height_devices
    partial, feature_grad = call(
        functools.partial(parameter_grads, time_devices, height_devices, per_frame),
        [out((pieces, 12 * TILE // pieces + 8, channels), bf16)],
        (got, stats),
        [
            pltpu.VMEM((2 * frames * time_devices, channels), f32),
            pltpu.VMEM((frames + 2, ext) + frame, bf16),
            held(own_two),
            held(scaled_shape),
            held(scaled_shape),
            held(turned_x),
            held(turned_features),
            held(temporal_kernel),
            pltpu.VMEM((frames * rows * columns, 3 * channels), bf16),
            dma(2 * frames + 7),
            dma(frames),
        ],
        conv * frames * rows * 2,
        far=(mixed, mixed_next, scaled, xt, ft, temporal_kernel),
        far_outs=[own_two],
    )
    partial = lax.all_to_all(partial, ends, 0, 0, tiled=True)
    (grad_inputs,) = call(
        input_grads,
        [out((frames, rows) + frame, bf16)],
        (feature_grad, cot, spatial_kernel),
        [weight],
        conv * frames * rows,
    )
    piece = partial.shape[1:]
    (partial,) = call(sum_and_copy, [out((time_devices,) + piece, bf16)], (partial,), limit=NARROW)
    partial = lax.all_to_all(partial, "tm", 0, 0, tiled=True)
    (partial,) = call(sum_and_copy, [out((pieces,) + piece, bf16)], (partial,), limit=NARROW)
    sums = lax.all_to_all(partial, ends, 0, 0, tiled=True)
    pixel_total = reps * frames * time_devices * rows * height_devices * columns
    spatial_sum, temporal_sum, gain_sum, shift_sum = call(
        functools.partial(finish, 1.0 / math.sqrt(pixel_total)),
        [
            out(spatial_kernel.shape, f32),
            out(temporal_kernel.shape, f32),
            out((1, channels), f32),
            out((1, channels), f32),
        ],
        (sums,),
        limit=NARROW,
    )
    return (
        outputs[None],
        grad_inputs[None],
        spatial_sum,
        temporal_sum,
        gain_sum[0],
        shift_sum[0],
    )


def solution(mesh):
    in_specs = (
        P("rep", "tm", "height", None, None),
        P(),
        P(),
        P(),
        P(),
        P("rep", "tm", "height", None, None),
    )
    out_specs = (
        P("rep", "tm", "height", None, None),
        P("rep", "tm", "height", None, None),
        P(),
        P(),
        P(),
        P(),
    )
    return jax.shard_map(shards, mesh=mesh, in_specs=in_specs, out_specs=out_specs, check_vma=False)
```
